32 devices in a mesh: ctx: 8 (over z, x), lat: 4 (over y, core).
Axes of the slice: x: 2, y: 2, z: 4, core: 2. Of those that a mesh axis runs over, the one named last changes fastest.
Arguments:
- token_ids: int32 [4096], P('ctx'), may hold values from 0 to 255
- latent_offset: int32 [1], replicated, may hold values from 2944 to 3072
- embed_table: bfloat16 [256, 2048], replicated, may hold values from -6 to 6
- cross_q: bfloat16 [2048, 2048], P('ctx', 'lat')
- cross_kv: bfloat16 [2, 2048, 2048], P(None, 'ctx', 'lat')
- cross_out: bfloat16 [2048, 2048], P('lat'), may hold values from -0.375 to 0.375
- self_qkv: bfloat16 [3, 2048, 2048], P(None, None, 'lat')
- self_out: bfloat16 [2048, 2048], P('lat'), may hold values from -0.25 to 0.25
- mlp_in: bfloat16 [2048, 8192], P(None, 'ctx'), may hold values from -0.125 to 0.125
- mlp_out: bfloat16 [8192, 2048], P('ctx'), may hold values from -0.0625 to 0.0625
Outputs:
- latent_out: bfloat16 [4, 256, 2048], P('lat', 'ctx')
The draws below stay inside these ranges and needn't reach their ends.
Inputs may be any that keep to these rules, and one draw needn't show every extreme that they name: `latent_offset`: the latent rows lie inside the context.
All inputs are finite; a program needn't handle non-finite values.
Results may differ from the reference program's by a relative error of at most 0.014.
Values may be sent and summed in bfloat16 or wider, within the bound.
No kernel may reach another device: no remote copies, remote signals or barrier semaphores. Data moves between devices by JAX's collectives and lax.ppermute only.
A program may use at most 128 MiB of HBM per device.

```python
import math
import jax
import jax.numpy as jnp
import numpy as np
from jax import lax

D = 2048
H = 16
HD = 128
FF = 8192
VOCAB = 256
LATENTS = 1024
CTX_DEV = 512
CONTEXT = 4096
N_CTX = 8
N_LAT = 4


def query_key_pair(key, salt):
    own_query = jax.random.normal(jax.random.fold_in(key, salt + 2), (D, D), jnp.float32) / math.sqrt(D)
    own_key = jax.random.normal(jax.random.fold_in(key, salt + 3), (D, D), jnp.float32) / math.sqrt(D)
    return (own_query, own_key)


def draw_cross_q(key, part):
    return query_key_pair(key, 100)[0].astype(jnp.bfloat16)


def draw_cross_kv(key, part):
    key_part = query_key_pair(key, 100)[1]
    value_part = jax.random.normal(jax.random.fold_in(key, 150), (D, D), jnp.float32) / math.sqrt(D)
    return jnp.stack([key_part, value_part]).astype(jnp.bfloat16)


def draw_self_qkv(key, part):
    query_part, key_part = query_key_pair(key, 200)
    value_part = jax.random.normal(jax.random.fold_in(key, 250), (D, D), jnp.float32) / math.sqrt(D)
    return jnp.stack([query_part, key_part, value_part]).astype(jnp.bfloat16)


def set_ends(entries, rng, least, top_value):
    shape = entries.shape
    index_at = [jax.random.randint(jax.random.fold_in(rng, axis), (), 0, shape[axis]) for axis in range(len(shape))]
    entries = entries.at[tuple(index_at)].set(least)
    longest = shape.index(max(shape))
    index_at[longest] = (index_at[longest] + 1) % shape[longest]
    return entries.at[tuple(index_at)].set(top_value)


def block_levels(stream_key, shape, split, low, top_value):
    factor_of, own = 1.0, jax.random.fold_in(stream_key, 6)
    for position, blocks in split:
        steps = jnp.exp(jax.random.uniform(jax.random.fold_in(own, position), (blocks,), jnp.float32, low / len(split), top_value / len(split)))
        factor_of = factor_of * jnp.repeat(steps, shape[position] // blocks).reshape([-1 if axis == position else 1 for axis in range(len(shape))])
    return factor_of


def cumulative_ranks(number_of, lean):
    weights = [(1 << 20) // math.isqrt(rank ** lean) + 1 for rank in range(1, number_of + 1)]
    scale = 1 + sum(weights) // (1 << 30)
    return np.cumsum(np.array([max(1, weight // scale) for weight in weights]))


def ranked_ids(stream_key, extent, count, slope):
    table = cumulative_ranks(count, slope)
    ticket = jax.random.randint(jax.random.fold_in(stream_key, 1), extent, 0, int(table[count - 1]))
    standing = jnp.searchsorted(jnp.asarray(table, jnp.int32), ticket, side="right")
    return jax.random.permutation(jax.random.fold_in(stream_key, 2), count)[standing].astype(jnp.int32)


def normal_values(key, dims, deviation, limit, shards=(), held_as=jnp.bfloat16):
    factor_of = block_levels(key, dims, shards, -0.22, 0.18) if shards else 1.0
    values = jax.random.normal(key, dims, jnp.float32) * deviation * factor_of
    return jnp.minimum(jnp.maximum(values, -limit), limit).astype(held_as)


def setup_inputs(seed: int = 0) -> dict:
    splits = jax.random.split(jax.random.key(seed), 11)
    return {
        "token_ids": set_ends(ranked_ids(splits[0], (CONTEXT,), VOCAB, 2), jax.random.fold_in(splits[0], 3), 0, VOCAB - 1).astype(jnp.int32),
        "latent_offset": jax.random.randint(splits[1], (1,), CONTEXT - LATENTS - CTX_DEV // 4, CONTEXT - LATENTS + 1).astype(jnp.int32),
        "embed_table": normal_values(splits[2], (VOCAB, D), 1.0, 6.0),
        "cross_q": draw_cross_q(jax.random.fold_in(splits[10], 71), 0),
        "cross_kv": draw_cross_kv(jax.random.fold_in(splits[10], 71), 0),
        "cross_out": normal_values(splits[5], (D, D), (3.0 * D ** -0.5), 0.375, ((0, 4),)),
        "self_qkv": draw_self_qkv(jax.random.fold_in(splits[10], 71), 0),
        "self_out": normal_values(splits[7], (D, D), (2.0 * D ** -0.5), 0.25, ((0, 4),)),
        "mlp_in": normal_values(splits[8], (D, FF), D ** -0.5, 0.125, ((1, 8),)),
        "mlp_out": normal_values(splits[9], (FF, D), FF ** -0.5, 0.0625, ((0, 8),)),
    }


EPSILON = 1e-06
MASKED = -1e+30

def rms_normalize(values):
    return values * lax.rsqrt(lax.optimization_barrier(jnp.mean(values * values, axis=-1, keepdims=True)) + EPSILON)

def sinusoid(places, width):
    index = jnp.arange(width // 2).astype(jnp.float32)
    rates = jnp.exp(index * (-2.0 * math.log(10000.0) / width))
    angles = places.astype(jnp.float32)[:, None] * rates[None, :]
    return jnp.stack([jnp.sin(angles), jnp.cos(angles)], axis=-1).reshape(places.shape[0], width)

def reference(token_ids, latent_offset, embed_table, cross_q, cross_kv, cross_out, self_qkv, self_out, mlp_in, mlp_out):
    offset = latent_offset[0]
    scale = 1.0 / math.sqrt(HD)
    places = jnp.arange(CONTEXT, dtype=jnp.int32)
    looked = embed_table[token_ids].astype(jnp.float32)
    context = rms_normalize(looked + sinusoid(places, D)).astype(jnp.bfloat16)
    keys = jnp.dot(context, cross_kv[0], preferred_element_type=jnp.float32).astype(jnp.bfloat16)
    values = jnp.dot(context, cross_kv[1], preferred_element_type=jnp.float32).astype(jnp.bfloat16)
    latent = lax.dynamic_slice_in_dim(context, offset, LATENTS, 0)
    queries = jnp.dot(latent, cross_q, preferred_element_type=jnp.float32).astype(jnp.bfloat16)
    query_places = offset + jnp.arange(LATENTS, dtype=jnp.int32)
    blocked = places.reshape(N_CTX, CTX_DEV)[None, :, :] > query_places[:, None, None]

    def cross_head(head_index):
        query = lax.dynamic_slice_in_dim(queries, head_index * HD, HD, 1).astype(jnp.float32)
        key = lax.dynamic_slice_in_dim(keys, head_index * HD, HD, 1).astype(jnp.float32).reshape(N_CTX, CTX_DEV, HD)
        value = lax.dynamic_slice_in_dim(values, head_index * HD, HD, 1).astype(jnp.float32).reshape(N_CTX, CTX_DEV, HD)
        scores = jnp.einsum('ld,ncd->lnc', query, key) * scale
        scores = jnp.where(blocked, MASKED, scores)
        block_max = lax.optimization_barrier(jnp.max(scores, axis=2))
        weights = jnp.exp(scores - block_max[:, :, None]).astype(jnp.bfloat16)
        block_total = lax.optimization_barrier(jnp.sum(weights.astype(jnp.float32), axis=2))
        block_output = jnp.einsum('lnc,ncd->lnd', weights.astype(jnp.float32), value)
        row_max = lax.optimization_barrier(jnp.max(block_max, axis=1))
        factor = jnp.exp(block_max - row_max[:, None])
        total = lax.optimization_barrier(jnp.sum(block_total * factor, axis=1))
        merged = lax.optimization_barrier(jnp.sum(block_output * factor[:, :, None], axis=1))
        return merged / total[:, None]
    heads_out = lax.map(cross_head, jnp.arange(H, dtype=jnp.int32))
    cross_attended = jnp.transpose(heads_out, (1, 0, 2)).reshape(LATENTS, D).astype(jnp.bfloat16)
    first_stream = latent.astype(jnp.float32) + jnp.dot(cross_attended, cross_out, preferred_element_type=jnp.float32)
    self_normed = rms_normalize(first_stream).astype(jnp.bfloat16)
    self_queries = jnp.dot(self_normed, self_qkv[0], preferred_element_type=jnp.float32).astype(jnp.bfloat16)
    self_keys = jnp.dot(self_normed, self_qkv[1], preferred_element_type=jnp.float32).astype(jnp.bfloat16)
    self_values = jnp.dot(self_normed, self_qkv[2], preferred_element_type=jnp.float32).astype(jnp.bfloat16)
    rows = jnp.arange(LATENTS, dtype=jnp.int32)
    later = rows[None, :] > rows[:, None]

    def self_head(head_index):
        query = lax.dynamic_slice_in_dim(self_queries, head_index * HD, HD, 1).astype(jnp.float32)
        key = lax.dynamic_slice_in_dim(self_keys, head_index * HD, HD, 1).astype(jnp.float32)
        value = lax.dynamic_slice_in_dim(self_values, head_index * HD, HD, 1).astype(jnp.float32)
        scores = jnp.einsum('id,jd->ij', query, key) * scale
        scores = jnp.where(later, MASKED, scores)
        peak = lax.optimization_barrier(jnp.max(scores, axis=1))
        weights = jnp.exp(scores - peak[:, None]).astype(jnp.bfloat16)
        total = lax.optimization_barrier(jnp.sum(weights.astype(jnp.float32), axis=1))
        return jnp.einsum('ij,jd->id', weights.astype(jnp.float32), value) / total[:, None]
    self_out_heads = lax.map(self_head, jnp.arange(H, dtype=jnp.int32))
    self_attended = jnp.transpose(self_out_heads, (1, 0, 2)).reshape(LATENTS, D).astype(jnp.bfloat16)
    second_stream = first_stream + jnp.dot(self_attended, self_out, preferred_element_type=jnp.float32)
    mlp_normed = rms_normalize(second_stream).astype(jnp.bfloat16)
    pre_hidden = jnp.dot(mlp_normed, mlp_in, preferred_element_type=jnp.float32)
    mlp_hidden = jax.nn.gelu(pre_hidden, approximate=True).astype(jnp.bfloat16)
    final = second_stream + jnp.dot(mlp_hidden, mlp_out, preferred_element_type=jnp.float32)
    return final.astype(jnp.bfloat16).reshape(N_LAT, LATENTS // N_LAT, D)
```

```python
import math

import jax
import jax.numpy as jnp
from jax import lax
from jax.experimental import pallas as pl
from jax.experimental.pallas import tpu as pltpu
from jax.sharding import PartitionSpec as P

HD = 128
LATENTS = 1024


EPSILON = 1e-06
MASKED = -1e30


def rms_normalize(values):
    return values * lax.rsqrt(jnp.mean(values * values, axis=-1, keepdims=True) + EPSILON)


def sinusoid(places, width):
    index = jnp.arange(width // 2).astype(jnp.float32)
    rates = jnp.exp(index * (-2.0 * math.log(10000.0) / width))
    angles = places.astype(jnp.float32)[:, None] * rates[None, :]
    return jnp.stack([jnp.sin(angles), jnp.cos(angles)], axis=-1).reshape(places.shape[0], width)


def embed_rows(token_rows, table, places):
    vocab_range = jnp.arange(table.shape[0], dtype=jnp.int32)
    one_hot = (token_rows[:, None] == vocab_range[None, :]).astype(jnp.bfloat16)
    looked = jnp.dot(one_hot, table, preferred_element_type=jnp.float32)
    return rms_normalize(looked + sinusoid(places, table.shape[1])).astype(jnp.bfloat16)


def block_attention(queries, keys, values, blocked, head_size):
    scale = 1.0 / math.sqrt(head_size)
    head_count = queries.shape[1] // head_size
    query_rows = queries.shape[0]
    key_rows = keys.shape[0]
    query_heads = jnp.transpose(queries.reshape(query_rows, head_count, head_size), (1, 0, 2))
    key_heads = jnp.transpose(keys.reshape(key_rows, head_count, head_size), (1, 0, 2))
    value_heads = jnp.transpose(values.reshape(key_rows, head_count, head_size), (1, 0, 2))

    def one_head(operands):
        query, key, value = operands
        scores = (
            lax.dot_general(
                query, key, (((1,), (1,)), ((), ())), preferred_element_type=jnp.float32
            )
            * scale
        )
        scores = jnp.where(blocked, MASKED, scores)
        peak = jnp.max(scores, axis=1)
        weights = jnp.exp(scores - peak[:, None]).astype(jnp.bfloat16)
        total = jnp.sum(weights.astype(jnp.float32), axis=1)
        output = jnp.dot(weights, value, preferred_element_type=jnp.float32)
        return (peak, total, output)

    maxima, totals, outputs = lax.map(one_head, (query_heads, key_heads, value_heads))
    merged = jnp.transpose(outputs, (1, 0, 2)).reshape(query_rows, head_count * head_size)
    return (jnp.transpose(maxima), jnp.transpose(totals), merged)


def general_device(
    token_ids,
    latent_offset,
    embed_table,
    cross_q,
    cross_kv,
    cross_out,
    self_qkv,
    self_out,
    mlp_in,
    mlp_out,
):
    context_count = lax.axis_size("ctx")
    group_count = lax.axis_size("lat")
    context_index = lax.axis_index("ctx")
    group_index = lax.axis_index("lat")
    block_length = token_ids.shape[0]
    head_size = HD
    local_width = cross_q.shape[1]
    local_heads = local_width // head_size
    width = embed_table.shape[1]
    offset = latent_offset[0]
    latent_count = LATENTS
    row_count = latent_count // context_count
    group_rows = latent_count // group_count
    places = context_index * block_length + jnp.arange(block_length, dtype=jnp.int32)
    context = embed_rows(token_ids, embed_table, places)
    piece = lax.all_gather(cross_kv, "ctx", axis=1, tiled=True)
    columns = context
    key_sum = jnp.dot(columns, piece[0], preferred_element_type=jnp.float32)
    value_sum = jnp.dot(columns, piece[1], preferred_element_type=jnp.float32)
    keys = key_sum.astype(jnp.bfloat16)
    values = value_sum.astype(jnp.bfloat16)
    every_token = lax.all_gather(token_ids, "ctx", axis=0, tiled=True)
    latent_tokens = lax.dynamic_slice_in_dim(every_token, offset, latent_count, 0)
    latent_places = offset + jnp.arange(latent_count, dtype=jnp.int32)
    latent = embed_rows(latent_tokens, embed_table, latent_places)
    columns = latent
    query_sum = jnp.dot(
        columns,
        lax.all_gather(cross_q, "ctx", axis=0, tiled=True),
        preferred_element_type=jnp.float32,
    )
    queries = query_sum.astype(jnp.bfloat16)
    blocked = places[None, :] > latent_places[:, None]
    maxima, totals, outputs = block_attention(queries, keys, values, blocked, head_size)
    row_start = context_index * row_count
    came_max, came_total, came_out = (
        lax.all_to_all(maxima[:, None, :], "ctx", split_axis=0, concat_axis=1, tiled=True),
        lax.all_to_all(totals[:, None, :], "ctx", split_axis=0, concat_axis=1, tiled=True),
        lax.all_to_all(outputs[:, None, :], "ctx", split_axis=0, concat_axis=1, tiled=True),
    )
    peak = jnp.max(came_max, axis=1, keepdims=True)
    factor = jnp.exp(came_max - peak)
    own_totals = jnp.sum(came_total * factor, axis=1)
    spread = (
        came_out.reshape(row_count, context_count, local_heads, head_size) * factor[:, :, :, None]
    )
    own_outputs = jnp.sum(spread, axis=1).reshape(row_count, local_width)
    attended = (own_outputs / jnp.repeat(own_totals, head_size, axis=1)).astype(jnp.bfloat16)
    own_latent = lax.dynamic_slice_in_dim(latent, row_start, row_count, 0).astype(jnp.float32)
    first_stream = own_latent + lax.psum(
        jnp.dot(attended, cross_out, preferred_element_type=jnp.float32), "lat"
    )
    self_normed = rms_normalize(first_stream).astype(jnp.bfloat16)
    self_queries = jnp.dot(self_normed, self_qkv[0], preferred_element_type=jnp.float32).astype(
        jnp.bfloat16
    )
    self_keys = jnp.dot(self_normed, self_qkv[1], preferred_element_type=jnp.float32).astype(
        jnp.bfloat16
    )
    self_values = jnp.dot(self_normed, self_qkv[2], preferred_element_type=jnp.float32).astype(
        jnp.bfloat16
    )
    all_keys, all_values = (
        lax.all_gather(self_keys, "ctx", axis=0, tiled=True),
        lax.all_gather(self_values, "ctx", axis=0, tiled=True),
    )
    own_places = row_start + jnp.arange(row_count, dtype=jnp.int32)
    later = jnp.arange(latent_count, dtype=jnp.int32)[None, :] > own_places[:, None]
    self_peak, self_totals, self_outputs = block_attention(
        self_queries, all_keys, all_values, later, head_size
    )
    self_attended = (self_outputs / jnp.repeat(self_totals, head_size, axis=1)).astype(jnp.bfloat16)
    second_stream = first_stream + lax.psum(
        jnp.dot(self_attended, self_out, preferred_element_type=jnp.float32).astype(jnp.bfloat16),
        "lat",
    ).astype(jnp.float32)
    mlp_normed = rms_normalize(second_stream).astype(jnp.bfloat16)
    gathered = lax.all_gather(mlp_normed, "ctx", axis=0, tiled=True)
    group_input = lax.dynamic_slice_in_dim(gathered, group_index * group_rows, group_rows, 0)
    pre_hidden = jnp.dot(group_input, mlp_in, preferred_element_type=jnp.float32)
    hidden = jax.nn.gelu(pre_hidden, approximate=True).astype(jnp.bfloat16)
    place = context_index * row_count - group_index * group_rows
    inside = jnp.logical_and(place >= 0, place < group_rows)
    residual = jnp.zeros((group_rows, width), jnp.float32)
    residual = lax.dynamic_update_slice_in_dim(
        residual, second_stream, jnp.clip(place, 0, group_rows - row_count), 0
    )
    residual = jnp.where(inside, residual, 0.0)
    result = lax.psum_scatter(
        jnp.dot(hidden, mlp_out, preferred_element_type=jnp.float32) + residual,
        "ctx",
        scatter_dimension=0,
        tiled=True,
    )
    return result.astype(jnp.bfloat16)[None]


FINE = 16


def rate_row(width):
    index = (jnp.arange(width, dtype=jnp.int32) // 2).astype(jnp.float32)
    return jnp.exp(index * (-2.0 * math.log(10000.0) / width))


def context_kernel(halves, ids_ref, coarse_ref, fine_ref, table_ref, out_ref, cos_ref, sin_ref):
    @pl.when(pl.program_id(0) == 0)
    def _():
        low_cos, low_sin = fine_ref[2], fine_ref[3]
        for step in range(FINE):
            high_cos, high_sin = fine_ref[0, step : step + 1, :], fine_ref[1, step : step + 1, :]
            rows = pl.ds(step * FINE, FINE)
            cos_ref[rows, :] = high_cos * low_cos - high_sin * low_sin
            sin_ref[rows, :] = high_sin * low_cos + high_cos * low_sin

    vocab, width = table_ref.shape
    rows = out_ref.shape[0]
    one_hot = (
        lax.broadcasted_iota(jnp.int32, (vocab, rows), 0) == ids_ref[0]
    ).astype(jnp.float32).astype(jnp.bfloat16)
    looked = lax.dot_general(
        one_hot, table_ref[...], (((0,), (0,)), ((), ())), preferred_element_type=jnp.float32
    )
    total = looked + coarse_ref[0, 0:1, :] * cos_ref[...] + coarse_ref[0, 1:2, :] * sin_ref[...]
    power = jnp.mean(total * total, axis=1, keepdims=True)
    normed = (total * lax.rsqrt(power + EPSILON)).astype(jnp.bfloat16)
    part = width // (2 * halves)
    for half in range(2):
        for owner in range(halves):
            source = (owner * 2 + half) * part
            target = (half * halves + owner) * part
            out_ref[:, target : target + part] = normed[:, source : source + part]


def context_rows(ids, starts, table, owners):
    count, rows = ids.shape[0], FINE * FINE
    width = table.shape[1]
    rates = rate_row(width)
    odd = (jnp.arange(width, dtype=jnp.int32) % 2)[None, :] == 1
    angles = starts.astype(jnp.float32)[:, None] * rates[None, :]
    sines, cosines = jnp.sin(angles), jnp.cos(angles)
    coarse = jnp.stack(
        [jnp.where(odd, cosines, sines), jnp.where(odd, -sines, cosines)], axis=1
    )
    steps = jnp.arange(FINE, dtype=jnp.float32)
    high = (steps * FINE)[:, None] * rates[None, :]
    low = steps[:, None] * rates[None, :]
    fine = jnp.stack([jnp.cos(high), jnp.sin(high), jnp.cos(low), jnp.sin(low)])
    return pl.pallas_call(
        lambda *refs: context_kernel(owners, *refs),
        grid=(count,),
        in_specs=[
            pl.BlockSpec((1, 1, rows), lambda i: (i, 0, 0)),
            pl.BlockSpec((1, 2, width), lambda i: (i, 0, 0)),
            pl.BlockSpec((4, FINE, width), lambda i: (0, 0, 0)),
            pl.BlockSpec(table.shape, lambda i: (0, 0)),
        ],
        out_specs=pl.BlockSpec((rows, width), lambda i: (i, 0)),
        out_shape=jax.ShapeDtypeStruct((count * rows, width), jnp.bfloat16),
        scratch_shapes=[pltpu.VMEM((rows, width), jnp.float32)] * 2,
        cost_estimate=pl.CostEstimate(
            flops=count * rows * width * table.shape[0] * 2,
            bytes_accessed=count * rows * width * 2,
            transcendentals=0,
        ),
        name="context_rows",
    )(ids[:, None, :], coarse, fine, table)


def attention_kernel(key_block, scale, starts_ref, query_ref, own_ref, other_ref, out_ref):
    tile = pl.program_id(0)
    query = query_ref[...]
    rows, size = query.shape
    query_place = starts_ref[0, tile] + lax.broadcasted_iota(jnp.int32, (rows, 1), 0)
    peak = jnp.full((rows, 1), MASKED, jnp.float32)
    total = jnp.zeros((rows, 1), jnp.float32)
    output = jnp.zeros((rows, size), jnp.float32)
    blocks = own_ref.shape[0] // key_block
    for side, ref in enumerate((own_ref, other_ref)):
        for block in range(blocks):
            span = pl.ds(block * key_block, key_block)
            key, value = ref[span, 0:size], ref[span, size : 2 * size]
            scores = (
                lax.dot_general(
                    query, key, (((1,), (1,)), ((), ())), preferred_element_type=jnp.float32
                )
                * scale
            )
            key_place = starts_ref[1 + side, block] + lax.broadcasted_iota(
                jnp.int32, (1, key_block), 1
            )
            scores = jnp.where(key_place > query_place, MASKED, scores)
            new_peak = jnp.maximum(peak, jnp.max(scores, axis=1, keepdims=True))
            factor = jnp.exp(peak - new_peak)
            weights = jnp.exp(scores - new_peak).astype(jnp.bfloat16)
            total = total * factor + jnp.sum(
                weights.astype(jnp.float32), axis=1, keepdims=True
            )
            output = output * factor + jnp.dot(
                weights, value, preferred_element_type=jnp.float32
            )
            peak = new_peak
    out_ref[...] = (output / total).astype(jnp.bfloat16)


def head_attention(query, own, other, query_starts, own_starts, other_starts, tile, key_block):
    rows, size = query.shape
    slots = max(query_starts.shape[0], own_starts.shape[0])
    pad = lambda starts: jnp.pad(starts, (0, slots - starts.shape[0]))
    starts = jnp.stack([pad(query_starts), pad(own_starts), pad(other_starts)]).astype(jnp.int32)
    keys = own.shape[0] + other.shape[0]
    return pl.pallas_call(
        lambda *refs: attention_kernel(key_block, 1.0 / math.sqrt(size), *refs),
        grid_spec=pltpu.PrefetchScalarGridSpec(
            num_scalar_prefetch=1,
            grid=(rows // tile,),
            in_specs=[
                pl.BlockSpec((tile, size), lambda i, s: (i, 0)),
                pl.BlockSpec(own.shape, lambda i, s: (0, 0)),
                pl.BlockSpec(other.shape, lambda i, s: (0, 0)),
            ],
            out_specs=pl.BlockSpec((tile, size), lambda i, s: (i, 0)),
        ),
        out_shape=jax.ShapeDtypeStruct((rows, size), jnp.bfloat16),
        cost_estimate=pl.CostEstimate(
            flops=4 * rows * keys * size, bytes_accessed=keys * size * 4, transcendentals=rows * keys
        ),
        name="head_attention",
    )(starts, query, own, other)


def dot32(left, right):
    return jnp.dot(left, right, preferred_element_type=jnp.float32)


def paired_device(
    token_ids,
    latent_offset,
    embed_table,
    cross_q,
    cross_kv,
    cross_out,
    self_qkv,
    self_out,
    mlp_in,
    mlp_out,
):
    owners = lax.axis_size("ctx")
    groups = lax.axis_size("lat")
    place = lax.axis_index("ctx")
    group = lax.axis_index("lat")
    core = group % 2
    duo = group // 2
    duos = groups // 2
    first = core == 0
    offset = latent_offset[0]
    block = token_ids.shape[0]
    width = embed_table.shape[1]
    share, columns = cross_q.shape
    heads = columns // HD
    group_rows = LATENTS // groups
    rows = group_rows // owners
    duo_rows = duos * rows
    half = share // 2

    def swap(value):
        return lax.ppermute(value, "lat", [(i, i ^ 1) for i in range(groups)])

    def cross(value):
        return lax.ppermute(value, "lat", [(i, i ^ 2) for i in range(groups)])

    def exchange(value):
        return lax.all_to_all(value, "ctx", 0, 0, tiled=True)

    def ordered(mine, theirs):
        return jnp.where(
            first, jnp.concatenate([mine, theirs]), jnp.concatenate([theirs, mine])
        )

    every_token = exchange(jnp.broadcast_to(token_ids[None], (owners, block)))

    stacked = jnp.concatenate([cross_q[None], cross_kv]).reshape(3, 2, half, heads, HD)
    stacked = jnp.transpose(stacked, (1, 3, 2, 0, 4)).reshape(2, heads, half, 3 * HD)
    mine = lax.dynamic_index_in_dim(stacked, core, 0, keepdims=False)
    theirs = swap(lax.dynamic_index_in_dim(stacked, 1 - core, 0, keepdims=False))
    arrived = exchange(ordered(mine, theirs)).reshape(owners * half, 3 * HD)
    weights = ordered(arrived, swap(arrived))

    cross_out_other = swap(cross_out)
    self_qkv_other = swap(self_qkv)
    self_out_other = swap(self_out)

    step = FINE * FINE
    latent_starts = (2 * jnp.arange(duos, dtype=jnp.int32) + core) * group_rows
    pieces = block // step
    half_blocks = owners // 2
    token_blocks = every_token.reshape(half_blocks, 2, block)
    own_ids = lax.dynamic_index_in_dim(token_blocks, core, 1, keepdims=False)
    flat_tokens = every_token.reshape(owners * block)
    latent_ids = jnp.stack(
        [
            lax.dynamic_slice_in_dim(
                flat_tokens, offset + (2 * i + core) * group_rows, group_rows, 0
            )
            for i in range(duos)
        ]
    )
    block_starts = (2 * jnp.arange(half_blocks, dtype=jnp.int32) + core) * block
    other_starts = (2 * jnp.arange(half_blocks, dtype=jnp.int32) + 1 - core) * block
    inner = jnp.arange(pieces, dtype=jnp.int32) * step
    latent_inner = jnp.arange(group_rows // step, dtype=jnp.int32) * step
    starts = jnp.concatenate(
        [
            (block_starts[:, None] + inner[None, :]).reshape(-1),
            (offset + latent_starts[:, None] + latent_inner[None, :]).reshape(-1),
        ]
    )
    ids = jnp.concatenate([own_ids.reshape(-1, step), latent_ids.reshape(-1, step)])
    context = context_rows(ids, starts, embed_table, owners)
    own_context = half_blocks * block
    latent = context[own_context:]

    pairs = dot32(context[:own_context], weights[:, HD:]).astype(jnp.bfloat16)
    queries = dot32(latent, weights[:, :HD]).astype(jnp.bfloat16)
    other_pairs = swap(pairs)
    tile = group_rows
    attended = head_attention(
        queries,
        pairs,
        other_pairs,
        offset + latent_starts,
        block_starts,
        other_starts,
        tile,
        block,
    )

    def to_rows(value):
        value = jnp.transpose(value.reshape(duos, owners, rows, HD), (1, 0, 2, 3))
        value = exchange(value.reshape(owners, duo_rows, HD))
        return jnp.transpose(value, (1, 0, 2)).reshape(duo_rows, 2, heads * HD)

    def project(value, mine, theirs):
        value = jnp.where(first, value, value[:, ::-1])
        product = dot32(value[:, 0], mine) + dot32(value[:, 1], theirs)
        product = product.reshape(duos, rows, width)
        kept = lax.dynamic_index_in_dim(product, duo, 0, keepdims=False)
        given = lax.dynamic_index_in_dim(product, 1 - duo, 0, keepdims=False)
        return kept + cross(given.astype(jnp.bfloat16)).astype(jnp.float32)

    own_latent = lax.dynamic_slice_in_dim(latent, duo * group_rows + place * rows, rows, 0)
    own_latent = jnp.transpose(own_latent.reshape(rows, 2, owners, half), (0, 2, 1, 3))
    own_latent = own_latent.reshape(rows, width).astype(jnp.float32)
    first_stream = own_latent + project(to_rows(attended), cross_out, cross_out_other)

    normed = rms_normalize(first_stream).astype(jnp.bfloat16)
    normed_other = cross(normed)
    normed = jnp.where(
        duo == 0,
        jnp.concatenate([normed, normed_other]),
        jnp.concatenate([normed_other, normed]),
    )

    def project_heads(matrices):
        parts = [dot32(normed, matrices[i]).astype(jnp.bfloat16) for i in range(3)]
        value = jnp.stack([part.reshape(duo_rows, heads, HD) for part in parts], axis=2)
        return jnp.transpose(value, (1, 0, 2, 3)).reshape(heads, duo_rows, 3 * HD)

    triples = exchange(ordered(project_heads(self_qkv), project_heads(self_qkv_other)))
    triples = jnp.transpose(triples.reshape(owners, duos, rows, 3 * HD), (1, 0, 2, 3))
    triples = triples.reshape(duos * group_rows, 3 * HD)
    self_pairs = triples[:, HD:]
    self_attended = head_attention(
        triples[:, :HD],
        self_pairs,
        swap(self_pairs),
        latent_starts,
        latent_starts,
        (2 * jnp.arange(duos, dtype=jnp.int32) + 1 - core) * group_rows,
        tile,
        group_rows,
    )
    second_stream = first_stream + project(to_rows(self_attended), self_out, self_out_other)

    mlp_normed = rms_normalize(second_stream).astype(jnp.bfloat16)
    gathered = exchange(jnp.broadcast_to(mlp_normed[None], (owners, rows, width)))
    pre_hidden = dot32(gathered.reshape(group_rows, width), mlp_in)
    hidden = jax.nn.gelu(pre_hidden, approximate=True).astype(jnp.bfloat16)
    shares = dot32(hidden, mlp_out).astype(jnp.bfloat16).reshape(owners, rows, width)
    shares = exchange(shares)
    result = second_stream + jnp.sum(shares.astype(jnp.float32), axis=0)
    return result.astype(jnp.bfloat16)[None]


def solution(mesh):
    placed = (
        P("ctx"),
        P(),
        P(),
        P("ctx", "lat"),
        P(None, "ctx", "lat"),
        P("lat", None),
        P(None, None, "lat"),
        P("lat", None),
        P(None, "ctx"),
        P("ctx", None),
    )

    def per_device(*arguments):
        owners, groups = lax.axis_size("ctx"), lax.axis_size("lat")
        local_heads = arguments[3].shape[1] // HD
        paired = groups == 4 and owners == 2 * local_heads
        return (paired_device if paired else general_device)(*arguments)

    return jax.shard_map(
        per_device, mesh=mesh, in_specs=placed, out_specs=P("lat", "ctx", None), check_vma=False
    )
```

```python
import math

import jax
import jax.numpy as jnp
from jax import lax
from jax.experimental import pallas as pl
from jax.experimental.pallas import tpu as pltpu
from jax.sharding import PartitionSpec as P

HD = 128
LATENTS = 1024


EPSILON = 1e-06
MASKED = -1e30


def rms_normalize(values):
    return values * lax.rsqrt(jnp.mean(values * values, axis=-1, keepdims=True) + EPSILON)


def sinusoid(places, width):
    index = jnp.arange(width // 2).astype(jnp.float32)
    rates = jnp.exp(index * (-2.0 * math.log(10000.0) / width))
    angles = places.astype(jnp.float32)[:, None] * rates[None, :]
    return jnp.stack([jnp.sin(angles), jnp.cos(angles)], axis=-1).reshape(places.shape[0], width)


def embed_rows(token_rows, table, places):
    vocab_range = jnp.arange(table.shape[0], dtype=jnp.int32)
    one_hot = (token_rows[:, None] == vocab_range[None, :]).astype(jnp.bfloat16)
    looked = jnp.dot(one_hot, table, preferred_element_type=jnp.float32)
    return rms_normalize(looked + sinusoid(places, table.shape[1])).astype(jnp.bfloat16)


def block_attention(queries, keys, values, blocked, head_size):
    scale = 1.0 / math.sqrt(head_size)
    head_count = queries.shape[1] // head_size
    query_rows = queries.shape[0]
    key_rows = keys.shape[0]
    query_heads = jnp.transpose(queries.reshape(query_rows, head_count, head_size), (1, 0, 2))
    key_heads = jnp.transpose(keys.reshape(key_rows, head_count, head_size), (1, 0, 2))
    value_heads = jnp.transpose(values.reshape(key_rows, head_count, head_size), (1, 0, 2))

    def one_head(operands):
        query, key, value = operands
        scores = (
            lax.dot_general(
                query, key, (((1,), (1,)), ((), ())), preferred_element_type=jnp.float32
            )
            * scale
        )
        scores = jnp.where(blocked, MASKED, scores)
        peak = jnp.max(scores, axis=1)
        weights = jnp.exp(scores - peak[:, None]).astype(jnp.bfloat16)
        total = jnp.sum(weights.astype(jnp.float32), axis=1)
        output = jnp.dot(weights, value, preferred_element_type=jnp.float32)
        return (peak, total, output)

    maxima, totals, outputs = lax.map(one_head, (query_heads, key_heads, value_heads))
    merged = jnp.transpose(outputs, (1, 0, 2)).reshape(query_rows, head_count * head_size)
    return (jnp.transpose(maxima), jnp.transpose(totals), merged)


def general_device(
    token_ids,
    latent_offset,
    embed_table,
    cross_q,
    cross_kv,
    cross_out,
    self_qkv,
    self_out,
    mlp_in,
    mlp_out,
):
    context_count = lax.axis_size("ctx")
    group_count = lax.axis_size("lat")
    context_index = lax.axis_index("ctx")
    group_index = lax.axis_index("lat")
    block_length = token_ids.shape[0]
    head_size = HD
    local_width = cross_q.shape[1]
    local_heads = local_width // head_size
    width = embed_table.shape[1]
    offset = latent_offset[0]
    latent_count = LATENTS
    row_count = latent_count // context_count
    group_rows = latent_count // group_count
    places = context_index * block_length + jnp.arange(block_length, dtype=jnp.int32)
    context = embed_rows(token_ids, embed_table, places)
    piece = lax.all_gather(cross_kv, "ctx", axis=1, tiled=True)
    columns = context
    key_sum = jnp.dot(columns, piece[0], preferred_element_type=jnp.float32)
    value_sum = jnp.dot(columns, piece[1], preferred_element_type=jnp.float32)
    keys = key_sum.astype(jnp.bfloat16)
    values = value_sum.astype(jnp.bfloat16)
    every_token = lax.all_gather(token_ids, "ctx", axis=0, tiled=True)
    latent_tokens = lax.dynamic_slice_in_dim(every_token, offset, latent_count, 0)
    latent_places = offset + jnp.arange(latent_count, dtype=jnp.int32)
    latent = embed_rows(latent_tokens, embed_table, latent_places)
    columns = latent
    query_sum = jnp.dot(
        columns,
        lax.all_gather(cross_q, "ctx", axis=0, tiled=True),
        preferred_element_type=jnp.float32,
    )
    queries = query_sum.astype(jnp.bfloat16)
    blocked = places[None, :] > latent_places[:, None]
    maxima, totals, outputs = block_attention(queries, keys, values, blocked, head_size)
    row_start = context_index * row_count
    came_max, came_total, came_out = (
        lax.all_to_all(maxima[:, None, :], "ctx", split_axis=0, concat_axis=1, tiled=True),
        lax.all_to_all(totals[:, None, :], "ctx", split_axis=0, concat_axis=1, tiled=True),
        lax.all_to_all(outputs[:, None, :], "ctx", split_axis=0, concat_axis=1, tiled=True),
    )
    peak = jnp.max(came_max, axis=1, keepdims=True)
    factor = jnp.exp(came_max - peak)
    own_totals = jnp.sum(came_total * factor, axis=1)
    spread = (
        came_out.reshape(row_count, context_count, local_heads, head_size) * factor[:, :, :, None]
    )
    own_outputs = jnp.sum(spread, axis=1).reshape(row_count, local_width)
    attended = (own_outputs / jnp.repeat(own_totals, head_size, axis=1)).astype(jnp.bfloat16)
    own_latent = lax.dynamic_slice_in_dim(latent, row_start, row_count, 0).astype(jnp.float32)
    first_stream = own_latent + lax.psum(
        jnp.dot(attended, cross_out, preferred_element_type=jnp.float32), "lat"
    )
    self_normed = rms_normalize(first_stream).astype(jnp.bfloat16)
    self_queries = jnp.dot(self_normed, self_qkv[0], preferred_element_type=jnp.float32).astype(
        jnp.bfloat16
    )
    self_keys = jnp.dot(self_normed, self_qkv[1], preferred_element_type=jnp.float32).astype(
        jnp.bfloat16
    )
    self_values = jnp.dot(self_normed, self_qkv[2], preferred_element_type=jnp.float32).astype(
        jnp.bfloat16
    )
    all_keys, all_values = (
        lax.all_gather(self_keys, "ctx", axis=0, tiled=True),
        lax.all_gather(self_values, "ctx", axis=0, tiled=True),
    )
    own_places = row_start + jnp.arange(row_count, dtype=jnp.int32)
    later = jnp.arange(latent_count, dtype=jnp.int32)[None, :] > own_places[:, None]
    _, self_totals, self_outputs = block_attention(
        self_queries, all_keys, all_values, later, head_size
    )
    self_attended = (self_outputs / jnp.repeat(self_totals, head_size, axis=1)).astype(jnp.bfloat16)
    second_stream = first_stream + lax.psum(
        jnp.dot(self_attended, self_out, preferred_element_type=jnp.float32).astype(jnp.bfloat16),
        "lat",
    ).astype(jnp.float32)
    mlp_normed = rms_normalize(second_stream).astype(jnp.bfloat16)
    gathered = lax.all_gather(mlp_normed, "ctx", axis=0, tiled=True)
    group_input = lax.dynamic_slice_in_dim(gathered, group_index * group_rows, group_rows, 0)
    pre_hidden = jnp.dot(group_input, mlp_in, preferred_element_type=jnp.float32)
    hidden = jax.nn.gelu(pre_hidden, approximate=True).astype(jnp.bfloat16)
    place = context_index * row_count - group_index * group_rows
    inside = jnp.logical_and(place >= 0, place < group_rows)
    residual = jnp.zeros((group_rows, width), jnp.float32)
    residual = lax.dynamic_update_slice_in_dim(
        residual, second_stream, jnp.clip(place, 0, group_rows - row_count), 0
    )
    residual = jnp.where(inside, residual, 0.0)
    result = lax.psum_scatter(
        jnp.dot(hidden, mlp_out, preferred_element_type=jnp.float32) + residual,
        "ctx",
        scatter_dimension=0,
        tiled=True,
    )
    return result.astype(jnp.bfloat16)[None]


FINE = 16
MIB = 1 << 20
BIG = 58 * MIB


def rate_row(width):
    index = (jnp.arange(width, dtype=jnp.int32) // 2).astype(jnp.float32)
    return jnp.exp(index * (-2.0 * math.log(10000.0) / width))


def context_kernel(halves, ids_ref, coarse_ref, fine_ref, table_ref, out_ref, cos_ref, sin_ref):
    @pl.when(pl.program_id(0) == 0)
    def _():
        low_cos, low_sin = fine_ref[2], fine_ref[3]
        for step in range(FINE):
            high_cos, high_sin = fine_ref[0, step : step + 1, :], fine_ref[1, step : step + 1, :]
            rows = pl.ds(step * FINE, FINE)
            cos_ref[rows, :] = high_cos * low_cos - high_sin * low_sin
            sin_ref[rows, :] = high_sin * low_cos + high_cos * low_sin

    vocab, width = table_ref.shape
    rows = out_ref.shape[0]
    one_hot = (
        lax.broadcasted_iota(jnp.int32, (vocab, rows), 0) == ids_ref[0]
    ).astype(jnp.float32).astype(jnp.bfloat16)
    looked = lax.dot_general(
        one_hot, table_ref[...], (((0,), (0,)), ((), ())), preferred_element_type=jnp.float32
    )
    total = looked + coarse_ref[0, 0:1, :] * cos_ref[...] + coarse_ref[0, 1:2, :] * sin_ref[...]
    power = jnp.mean(total * total, axis=1, keepdims=True)
    normed = (total * lax.rsqrt(power + EPSILON)).astype(jnp.bfloat16)
    part = width // (2 * halves)
    for half in range(2):
        for owner in range(halves):
            source = (owner * 2 + half) * part
            target = (half * halves + owner) * part
            out_ref[:, target : target + part] = normed[:, source : source + part]


def sinusoid_tables(starts, width):
    rates = rate_row(width)
    odd = (jnp.arange(width, dtype=jnp.int32) % 2)[None, :] == 1
    angles = starts.astype(jnp.float32)[:, None] * rates[None, :]
    sines, cosines = jnp.sin(angles), jnp.cos(angles)
    coarse = jnp.stack(
        [jnp.where(odd, cosines, sines), jnp.where(odd, -sines, cosines)], axis=1
    )
    steps = jnp.arange(FINE, dtype=jnp.float32)
    high = (steps * FINE)[:, None] * rates[None, :]
    low = steps[:, None] * rates[None, :]
    fine = jnp.stack([jnp.cos(high), jnp.sin(high), jnp.cos(low), jnp.sin(low)])
    return coarse, fine


def context_rows(ids, starts, table, owners):
    count, rows = ids.shape[0], FINE * FINE
    width = table.shape[1]
    coarse, fine = sinusoid_tables(starts, width)
    return pl.pallas_call(
        lambda *refs: context_kernel(owners, *refs),
        grid=(count,),
        in_specs=[
            pl.BlockSpec((1, 1, rows), lambda i: (i, 0, 0)),
            pl.BlockSpec((1, 2, width), lambda i: (i, 0, 0)),
            pl.BlockSpec((4, FINE, width), lambda i: (0, 0, 0)),
            pl.BlockSpec(table.shape, lambda i: (0, 0)),
        ],
        out_specs=pl.BlockSpec((rows, width), lambda i: (i, 0)),
        out_shape=jax.ShapeDtypeStruct((count * rows, width), jnp.bfloat16),
        scratch_shapes=[pltpu.VMEM((rows, width), jnp.float32)] * 2,
        cost_estimate=pl.CostEstimate(
            flops=count * rows * width * table.shape[0] * 2,
            bytes_accessed=count * rows * width * 2,
            transcendentals=0,
        ),
        compiler_params=pltpu.CompilerParams(vmem_limit_bytes=20 * MIB),
        name="context_rows",
    )(ids[:, None, :], coarse, fine, table)


def attention_kernel(key_tile, places_ref, query_ref, own_ref, other_ref, out_ref):
    tile = pl.program_id(0)
    parts, rows, size = query_ref.shape
    query = query_ref[...].reshape(parts * rows, size)
    rows = parts * rows
    query_place = (
        places_ref[0] + tile * places_ref[1] + lax.broadcasted_iota(jnp.int32, (rows, 1), 0)
    )
    peak = jnp.full((rows, 1), MASKED, jnp.float32)
    output = jnp.zeros((rows, 2 * size), jnp.float32)
    outer, blocks, inner, columns = own_ref.shape
    keys = outer * inner
    for side, ref in enumerate((own_ref, other_ref)):
        for block in range(blocks):
            pair = ref[:, block, :, columns - 2 * size :].reshape(keys, 2 * size)
            for part in range(keys // key_tile):
                span = slice(part * key_tile, (part + 1) * key_tile)
                key, value = pair[span, :size], pair[span, size:]
                scores = lax.dot_general(
                    query, key, (((1,), (1,)), ((), ())), preferred_element_type=jnp.float32
                )
                key_place = (
                    places_ref[2 + 2 * side]
                    + block * places_ref[3 + 2 * side]
                    + part * key_tile
                    + lax.broadcasted_iota(jnp.int32, (1, key_tile), 1)
                )
                scores = jnp.where(key_place > query_place, MASKED, scores)
                new_peak = jnp.maximum(peak, jnp.max(scores, axis=1, keepdims=True))
                weights = jnp.exp(scores - new_peak).astype(jnp.bfloat16)
                output = output * jnp.exp(peak - new_peak) + jnp.dot(
                    weights,
                    jnp.concatenate([value, jnp.ones_like(value)], axis=1),
                    preferred_element_type=jnp.float32,
                )
                peak = new_peak
    final = (output[:, :size] / output[:, size:]).astype(jnp.bfloat16)
    out_ref[...] = final.reshape(out_ref.shape)


def head_attention(triples, own, other, places, key_tile):
    owners, tiles, rows = triples.shape[:3]
    keys = 2 * own.shape[0] * own.shape[1] * own.shape[2]
    return pl.pallas_call(
        lambda *refs: attention_kernel(key_tile, *refs),
        grid_spec=pltpu.PrefetchScalarGridSpec(
            num_scalar_prefetch=1,
            grid=(tiles,),
            in_specs=[
                pl.BlockSpec((owners, None, rows, HD), lambda i, s: (0, i, 0, 0)),
                pl.BlockSpec(own.shape, lambda i, s: (0, 0, 0, 0)),
                pl.BlockSpec(other.shape, lambda i, s: (0, 0, 0, 0)),
            ],
            out_specs=pl.BlockSpec((owners, None, rows, HD), lambda i, s: (0, i, 0, 0)),
        ),
        out_shape=jax.ShapeDtypeStruct((owners, tiles, rows, HD), jnp.bfloat16),
        cost_estimate=pl.CostEstimate(
            flops=8 * owners * tiles * rows * keys * HD,
            bytes_accessed=keys * HD * 4,
            transcendentals=owners * tiles * rows * keys,
        ),
        compiler_params=pltpu.CompilerParams(vmem_limit_bytes=14 * MIB),
        name="head_attention",
    )(places, triples, own, other)


def prepare_kernel(core_ref, query_ref, pair_ref, mine_ref, theirs_ref):
    heads, half, columns = mine_ref.shape
    size = columns // 3
    for target, core in ((mine_ref, core_ref[0]), (theirs_ref, 1 - core_ref[0])):
        rows = pl.ds(pl.multiple_of(core * half, half), half)
        for head in range(heads):
            span = slice(head * size, (head + 1) * size)
            target[head, :, 0:size] = query_ref[rows, span]
            target[head, :, size : 2 * size] = pair_ref[0, rows, span]
            target[head, :, 2 * size :] = pair_ref[1, rows, span]


def prepare_weights(core, cross_q, cross_kv):
    share, columns = cross_q.shape
    shape = jax.ShapeDtypeStruct((columns // HD, share // 2, 3 * HD), jnp.bfloat16)
    return pl.pallas_call(
        prepare_kernel,
        in_specs=[pl.BlockSpec(memory_space=pltpu.SMEM)]
        + [pl.BlockSpec(memory_space=pltpu.VMEM)] * 2,
        out_specs=[pl.BlockSpec(memory_space=pltpu.VMEM)] * 2,
        out_shape=[shape, shape],
        compiler_params=pltpu.CompilerParams(vmem_limit_bytes=4 * MIB),
        name="prepare_weights",
    )(core, cross_q, cross_kv)


def project_kernel(scalars_ref, heads_ref, mine_ref, theirs_ref, kept_ref, given_ref):
    core, duo = scalars_ref[0], scalars_ref[1]
    half = heads_ref.shape[0] // 2
    product = 0.0
    for side, matrix in ((core, mine_ref), (1 - core, theirs_ref)):
        left = jnp.concatenate([heads_ref[side * half + head] for head in range(half)], axis=1)
        product += jnp.dot(left, matrix[...], preferred_element_type=jnp.float32)
    kept_rows = kept_ref.shape[0]
    low, high = product[:kept_rows], product[kept_rows:]
    kept_ref[...] = jnp.where(duo == 0, low, high)
    given_ref[...] = jnp.where(duo == 0, high, low).astype(jnp.bfloat16)


IN_VMEM = pl.BlockSpec(memory_space=pltpu.VMEM)
IN_SMEM = pl.BlockSpec(memory_space=pltpu.SMEM)
ANYWHERE = pl.BlockSpec(memory_space=pl.ANY)


def project_rows(scalars, heads, mine, theirs):
    _, rows, _ = heads.shape
    inner, width = mine.shape
    return pl.pallas_call(
        project_kernel,
        in_specs=[IN_SMEM, IN_VMEM, IN_VMEM, IN_VMEM],
        out_specs=[IN_VMEM, IN_VMEM],
        out_shape=[
            jax.ShapeDtypeStruct((rows // 2, width), jnp.float32),
            jax.ShapeDtypeStruct((rows // 2, width), jnp.bfloat16),
        ],
        cost_estimate=pl.CostEstimate(
            flops=4 * rows * inner * width, bytes_accessed=4 * inner * width, transcendentals=0
        ),
        compiler_params=pltpu.CompilerParams(vmem_limit_bytes=8 * MIB),
        name="project_rows",
    )(scalars, heads, mine, theirs)


def triple_kernel(scale, scalars_ref, rows_ref, mine_ref, theirs_ref, out_ref):
    core = scalars_ref[0]
    heads = out_ref.shape[0] // 2
    for side, matrix in ((core, mine_ref), (1 - core, theirs_ref)):
        for kind in range(mine_ref.shape[0]):
            product = jnp.dot(rows_ref[...], matrix[kind], preferred_element_type=jnp.float32)
            product = (product * (scale if kind == 0 else 1.0)).astype(jnp.bfloat16)
            for head in range(heads):
                out_ref[side * heads + head, :, kind * HD : (kind + 1) * HD] = product[
                    :, head * HD : (head + 1) * HD
                ]


def triple_heads(scalars, rows, mine, theirs):
    count, _ = rows.shape
    kinds, inner, columns = mine.shape
    heads = columns // HD
    return pl.pallas_call(
        lambda *refs: triple_kernel(HD**-0.5, *refs),
        in_specs=[IN_SMEM, IN_VMEM, IN_VMEM, IN_VMEM],
        out_specs=IN_VMEM,
        out_shape=jax.ShapeDtypeStruct((2 * heads, count, kinds * HD), jnp.bfloat16),
        cost_estimate=pl.CostEstimate(
            flops=4 * kinds * count * inner * columns,
            bytes_accessed=4 * kinds * inner * columns,
            transcendentals=0,
        ),
        compiler_params=pltpu.CompilerParams(vmem_limit_bytes=16 * MIB),
        name="triple_heads",
    )(scalars, rows, mine, theirs)


def context_heads_kernel(
    scale, scalars_ref, context_hbm, mine_hbm, theirs_hbm, pair_ref, query_ref, latent_ref,
    context_ref, mine_ref, theirs_ref, loaded,
):
    core, duo, place = scalars_ref[0], scalars_ref[1], scalars_ref[2]
    inner = mine_ref.shape[0]
    size = mine_ref.shape[1] // 3
    keys = pair_ref.shape[0]
    owners, _, rows, _ = query_ref.shape
    tile = owners * rows
    count = context_ref.shape[0] // tile
    own = pl.ds(pl.multiple_of(core * inner, inner), inner)
    other = pl.ds(pl.multiple_of((1 - core) * inner, inner), inner)
    loads = [
        pltpu.make_async_copy(mine_hbm, mine_ref, loaded.at[count]),
        pltpu.make_async_copy(theirs_hbm, theirs_ref, loaded.at[count + 1]),
    ] + [
        pltpu.make_async_copy(
            context_hbm.at[pl.ds(i * tile, tile)], context_ref.at[pl.ds(i * tile, tile)], loaded.at[i]
        )
        for i in range(count)
    ]
    for load in loads:
        load.start()
    loads[0].wait()
    loads[1].wait()

    def product(span, columns):
        return jnp.dot(
            context_ref[span, own], mine_ref[:, columns], preferred_element_type=jnp.float32
        ) + jnp.dot(
            context_ref[span, other], theirs_ref[:, columns], preferred_element_type=jnp.float32
        )

    for index in range(count):
        loads[2 + index].wait()
        span = slice(index * tile, (index + 1) * tile)
        if index * tile < keys:
            pair_ref[span, :] = product(span, slice(size, 3 * size)).astype(jnp.bfloat16)
        else:
            query = (product(span, slice(0, size)) * scale).astype(jnp.bfloat16)
            query_ref[:, index - keys // tile] = query.reshape(owners, rows, size)
    start = pl.multiple_of(keys + duo * tile + place * rows, rows)
    latent = context_ref[pl.ds(start, rows), :]
    part = inner // owners
    for half in range(2):
        for owner in range(owners):
            source = half * inner + owner * part
            target = (owner * 2 + half) * part
            latent_ref[:, target : target + part] = latent[:, source : source + part]


def context_heads(scalars, context, mine, theirs, shape):
    owners, tiles, rows = shape
    count, width = context.shape
    tile = owners * rows
    keys = count - tiles * tile
    inner, columns = mine.shape
    size = columns // 3
    return pl.pallas_call(
        lambda *refs: context_heads_kernel(size**-0.5, *refs),
        in_specs=[IN_SMEM] + [ANYWHERE] * 3,
        out_specs=[IN_VMEM] * 3,
        out_shape=[
            jax.ShapeDtypeStruct((keys, 2 * size), jnp.bfloat16),
            jax.ShapeDtypeStruct((owners, tiles, rows, size), jnp.bfloat16),
            jax.ShapeDtypeStruct((rows, width), jnp.bfloat16),
        ],
        scratch_shapes=[
            pltpu.VMEM(context.shape, jnp.bfloat16),
            pltpu.VMEM(mine.shape, jnp.bfloat16),
            pltpu.VMEM(mine.shape, jnp.bfloat16),
            pltpu.SemaphoreType.DMA((count // tile + 2,)),
        ],
        cost_estimate=pl.CostEstimate(
            flops=4 * count * inner * columns, bytes_accessed=context.size * 2, transcendentals=0
        ),
        compiler_params=pltpu.CompilerParams(vmem_limit_bytes=BIG),
        name="context_heads",
    )(scalars, context, mine, theirs)


def mlp_kernel(scalars_ref, *refs):
    group = scalars_ref[3]
    *refs, hidden_ref = refs
    count = (len(refs) - 10) // 2
    blocks, (in_ref, out_ref), rest = refs[:count], refs[count : count + 2], refs[count + 2 :]
    in_parts, out_parts, shares = rest[:4], rest[4:8], rest[8:]
    rows = jnp.concatenate([block[...] for block in blocks])
    depth, units = in_parts[0].shape[0], out_parts[0].shape[0]

    def hidden_of(total):
        return jax.nn.gelu(total, approximate=True).astype(jnp.bfloat16)

    total = jnp.dot(rows, in_ref[...], preferred_element_type=jnp.float32)
    share = jnp.dot(hidden_of(total), out_ref[...], preferred_element_type=jnp.float32)
    quarters = [group, group ^ 2, group ^ 1, group ^ 3]
    total = 0.0
    for quarter, part in zip(quarters, in_parts):
        span = pl.ds(pl.multiple_of(quarter * depth, depth), depth)
        piece = jnp.concatenate([block[:, span] for block in blocks])
        total += jnp.dot(piece, part[...], preferred_element_type=jnp.float32)
    hidden_ref[...] = hidden_of(total)
    for quarter, part in zip(quarters, out_parts):
        span = pl.ds(pl.multiple_of(quarter * units, units), units)
        share += jnp.dot(hidden_ref[:, span], part[...], preferred_element_type=jnp.float32)
    each = blocks[0].shape[0]
    for index, target in enumerate(shares):
        target[...] = share[index * each : (index + 1) * each].astype(target.dtype)


def mlp_shares(scalars, blocks, mlp_in, mlp_out, in_parts, out_parts):
    first = jax.ShapeDtypeStruct(blocks[0].shape, jnp.float32)
    other = jax.ShapeDtypeStruct(blocks[0].shape, jnp.bfloat16)
    operands = [*blocks, mlp_in, mlp_out, *in_parts, *out_parts]
    return pl.pallas_call(
        mlp_kernel,
        in_specs=[IN_SMEM] + [IN_VMEM] * len(operands),
        out_specs=[IN_VMEM] * len(blocks),
        out_shape=[first] + [other] * (len(blocks) - 1),
        scratch_shapes=[
            pltpu.VMEM((len(blocks) * blocks[0].shape[0], mlp_in.shape[1]), jnp.bfloat16)
        ],
        cost_estimate=pl.CostEstimate(
            flops=8 * len(blocks) * blocks[0].size * mlp_in.shape[1],
            bytes_accessed=8 * mlp_in.size,
            transcendentals=0,
        ),
        compiler_params=pltpu.CompilerParams(vmem_limit_bytes=12 * MIB),
        name="mlp_shares",
    )(scalars, *operands)


def paired_device(
    token_ids,
    latent_offset,
    embed_table,
    cross_q,
    cross_kv,
    cross_out,
    self_qkv,
    self_out,
    mlp_in,
    mlp_out,
):
    owners = lax.axis_size("ctx")
    groups = lax.axis_size("lat")
    place = lax.axis_index("ctx")
    group = lax.axis_index("lat")
    core = group % 2
    duo = group // 2
    duos = groups // 2
    first = core == 0
    offset = latent_offset[0]
    block = token_ids.shape[0]
    share = cross_q.shape[0]
    group_rows = LATENTS // groups
    rows = group_rows // owners
    duo_rows = duos * rows
    half = share // 2
    scalars = jnp.stack([core, duo, place, group]).astype(jnp.int32)

    def swap(value):
        return lax.ppermute(value, "lat", [(i, i ^ 1) for i in range(groups)])

    def cross(value):
        return lax.ppermute(value, "lat", [(i, i ^ 2) for i in range(groups)])

    def exchange(value):
        return lax.all_to_all(value, "ctx", 0, 0, tiled=True)

    def across(value, distance):
        return lax.ppermute(value, "ctx", [(i, i ^ distance) for i in range(owners)])

    def quarter(matrix):
        size = matrix.shape[0] // groups
        return lax.dynamic_slice_in_dim(matrix, group * size, size, 0)

    def ordered(mine, theirs):
        return jnp.where(
            first, jnp.concatenate([mine, theirs]), jnp.concatenate([theirs, mine])
        )

    mine, theirs = prepare_weights(scalars, cross_q, cross_kv)
    sent = ordered(mine, swap(theirs))

    every_token = exchange(jnp.broadcast_to(token_ids[None], (owners, block)))
    arrived = exchange(sent).reshape(owners * half, 3 * HD)

    step = FINE * FINE
    latent_starts = (2 * jnp.arange(duos, dtype=jnp.int32) + core) * group_rows
    pieces = block // step
    half_blocks = owners // 2
    token_blocks = every_token.reshape(half_blocks, 2, block)
    own_ids = lax.dynamic_index_in_dim(token_blocks, core, 1, keepdims=False)
    flat_tokens = every_token.reshape(owners * block)
    latent_ids = jnp.stack(
        [
            lax.dynamic_slice_in_dim(
                flat_tokens, offset + (2 * i + core) * group_rows, group_rows, 0
            )
            for i in range(duos)
        ]
    )
    fetched = []
    for matrix in (mlp_in, mlp_out):
        one = across(quarter(matrix), 1)
        two = cross(one)
        three = swap(one)
        four = swap(two)
        fetched.append((one, two, three, four))

    block_starts = (2 * jnp.arange(half_blocks, dtype=jnp.int32) + core) * block
    inner = jnp.arange(pieces, dtype=jnp.int32) * step
    latent_inner = jnp.arange(group_rows // step, dtype=jnp.int32) * step
    starts = jnp.concatenate(
        [
            (block_starts[:, None] + inner[None, :]).reshape(-1),
            (offset + latent_starts[:, None] + latent_inner[None, :]).reshape(-1),
        ]
    )
    ids = jnp.concatenate([own_ids.reshape(-1, step), latent_ids.reshape(-1, step)])
    context = context_rows(ids, starts, embed_table, owners)
    pairs, queries, own_latent = context_heads(
        scalars, context, arrived, swap(arrived), (owners, duos, rows)
    )
    other_pairs = swap(pairs)
    by_block = (1, half_blocks, block, 2 * HD)
    places = jnp.stack(
        [
            offset + core * group_rows,
            2 * group_rows,
            core * block,
            2 * block,
            (1 - core) * block,
            2 * block,
        ]
    ).astype(jnp.int32)
    attended = head_attention(
        queries, pairs.reshape(by_block), other_pairs.reshape(by_block), places, block
    )

    def project(attended, mine, theirs):
        heads = exchange(attended.reshape(owners, duo_rows, HD))
        kept, given = project_rows(scalars, heads, mine, theirs)
        return kept + cross(given).astype(jnp.float32)

    projected = project(attended, cross_out, swap(cross_out))
    first_stream = own_latent.astype(jnp.float32) + projected

    normed = rms_normalize(first_stream).astype(jnp.bfloat16)
    normed_other = cross(normed)
    normed = jnp.where(
        duo == 0,
        jnp.concatenate([normed, normed_other]),
        jnp.concatenate([normed_other, normed]),
    )
    self_qkv_other = swap(self_qkv)
    triples = exchange(triple_heads(scalars, normed, self_qkv, self_qkv_other))
    triples = triples.reshape(owners, duos, rows, 3 * HD)
    self_places = jnp.stack(
        [
            core * group_rows,
            2 * group_rows,
            core * group_rows,
            2 * group_rows,
            (1 - core) * group_rows,
            2 * group_rows,
        ]
    ).astype(jnp.int32)
    self_attended = head_attention(triples, triples, swap(triples), self_places, group_rows)
    projected = project(self_attended, self_out, swap(self_out))
    second_stream = first_stream + projected

    mlp_normed = rms_normalize(second_stream).astype(jnp.bfloat16)
    distances = [2 * i for i in range(1, owners // 2)]
    blocks = [mlp_normed] + [across(mlp_normed, distance) for distance in distances]
    kept, *given = mlp_shares(scalars, blocks, mlp_in, mlp_out, *fetched)
    result = second_stream + kept
    for share, distance in zip(given, distances):
        result = result + across(share, distance).astype(jnp.float32)
    return result.astype(jnp.bfloat16)[None]


def solution(mesh):
    placed = (
        P("ctx"),
        P(),
        P(),
        P("ctx", "lat"),
        P(None, "ctx", "lat"),
        P("lat", None),
        P(None, None, "lat"),
        P("lat", None),
        P(None, "ctx"),
        P("ctx", None),
    )

    def per_device(*arguments):
        owners, groups = lax.axis_size("ctx"), lax.axis_size("lat")
        local_heads = arguments[3].shape[1] // HD
        paired = groups == 4 and owners == 2 * local_heads and owners & (owners - 1) == 0
        return (paired_device if paired else general_device)(*arguments)

    return jax.shard_map(
        per_device, mesh=mesh, in_specs=placed, out_specs=P("lat", "ctx", None), check_vma=False
    )
```

```python
import math

import jax
import jax.numpy as jnp
from jax import lax
from jax.experimental import pallas as pl
from jax.experimental.pallas import tpu as pltpu
from jax.sharding import PartitionSpec as P

HD = 128
LATENTS = 1024


EPSILON = 1e-06
MASKED = -1e30


def rms_normalize(values):
    return values * lax.rsqrt(jnp.mean(values * values, axis=-1, keepdims=True) + EPSILON)


def sinusoid(places, width):
    index = jnp.arange(width // 2).astype(jnp.float32)
    rates = jnp.exp(index * (-2.0 * math.log(10000.0) / width))
    angles = places.astype(jnp.float32)[:, None] * rates[None, :]
    return jnp.stack([jnp.sin(angles), jnp.cos(angles)], axis=-1).reshape(places.shape[0], width)


def embed_rows(token_rows, table, places):
    vocab_range = jnp.arange(table.shape[0], dtype=jnp.int32)
    one_hot = (token_rows[:, None] == vocab_range[None, :]).astype(jnp.bfloat16)
    looked = jnp.dot(one_hot, table, preferred_element_type=jnp.float32)
    return rms_normalize(looked + sinusoid(places, table.shape[1])).astype(jnp.bfloat16)


def block_attention(queries, keys, values, blocked, head_size):
    scale = 1.0 / math.sqrt(head_size)
    head_count = queries.shape[1] // head_size
    query_rows = queries.shape[0]
    key_rows = keys.shape[0]
    query_heads = jnp.transpose(queries.reshape(query_rows, head_count, head_size), (1, 0, 2))
    key_heads = jnp.transpose(keys.reshape(key_rows, head_count, head_size), (1, 0, 2))
    value_heads = jnp.transpose(values.reshape(key_rows, head_count, head_size), (1, 0, 2))

    def one_head(operands):
        query, key, value = operands
        scores = (
            lax.dot_general(
                query, key, (((1,), (1,)), ((), ())), preferred_element_type=jnp.float32
            )
            * scale
        )
        scores = jnp.where(blocked, MASKED, scores)
        peak = jnp.max(scores, axis=1)
        weights = jnp.exp(scores - peak[:, None]).astype(jnp.bfloat16)
        total = jnp.sum(weights.astype(jnp.float32), axis=1)
        output = jnp.dot(weights, value, preferred_element_type=jnp.float32)
        return (peak, total, output)

    maxima, totals, outputs = lax.map(one_head, (query_heads, key_heads, value_heads))
    merged = jnp.transpose(outputs, (1, 0, 2)).reshape(query_rows, head_count * head_size)
    return (jnp.transpose(maxima), jnp.transpose(totals), merged)


def general_device(
    token_ids,
    latent_offset,
    embed_table,
    cross_q,
    cross_kv,
    cross_out,
    self_qkv,
    self_out,
    mlp_in,
    mlp_out,
):
    context_count = lax.axis_size("ctx")
    group_count = lax.axis_size("lat")
    context_index = lax.axis_index("ctx")
    group_index = lax.axis_index("lat")
    block_length = token_ids.shape[0]
    head_size = HD
    local_width = cross_q.shape[1]
    local_heads = local_width // head_size
    width = embed_table.shape[1]
    offset = latent_offset[0]
    latent_count = LATENTS
    row_count = latent_count // context_count
    group_rows = latent_count // group_count
    places = context_index * block_length + jnp.arange(block_length, dtype=jnp.int32)
    context = embed_rows(token_ids, embed_table, places)
    piece = lax.all_gather(cross_kv, "ctx", axis=1, tiled=True)
    columns = context
    key_sum = jnp.dot(columns, piece[0], preferred_element_type=jnp.float32)
    value_sum = jnp.dot(columns, piece[1], preferred_element_type=jnp.float32)
    keys = key_sum.astype(jnp.bfloat16)
    values = value_sum.astype(jnp.bfloat16)
    every_token = lax.all_gather(token_ids, "ctx", axis=0, tiled=True)
    latent_tokens = lax.dynamic_slice_in_dim(every_token, offset, latent_count, 0)
    latent_places = offset + jnp.arange(latent_count, dtype=jnp.int32)
    latent = embed_rows(latent_tokens, embed_table, latent_places)
    columns = latent
    query_sum = jnp.dot(
        columns,
        lax.all_gather(cross_q, "ctx", axis=0, tiled=True),
        preferred_element_type=jnp.float32,
    )
    queries = query_sum.astype(jnp.bfloat16)
    blocked = places[None, :] > latent_places[:, None]
    maxima, totals, outputs = block_attention(queries, keys, values, blocked, head_size)
    row_start = context_index * row_count
    came_max, came_total, came_out = (
        lax.all_to_all(maxima[:, None, :], "ctx", split_axis=0, concat_axis=1, tiled=True),
        lax.all_to_all(totals[:, None, :], "ctx", split_axis=0, concat_axis=1, tiled=True),
        lax.all_to_all(outputs[:, None, :], "ctx", split_axis=0, concat_axis=1, tiled=True),
    )
    peak = jnp.max(came_max, axis=1, keepdims=True)
    factor = jnp.exp(came_max - peak)
    own_totals = jnp.sum(came_total * factor, axis=1)
    spread = (
        came_out.reshape(row_count, context_count, local_heads, head_size) * factor[:, :, :, None]
    )
    own_outputs = jnp.sum(spread, axis=1).reshape(row_count, local_width)
    attended = (own_outputs / jnp.repeat(own_totals, head_size, axis=1)).astype(jnp.bfloat16)
    own_latent = lax.dynamic_slice_in_dim(latent, row_start, row_count, 0).astype(jnp.float32)
    first_stream = own_latent + lax.psum(
        jnp.dot(attended, cross_out, preferred_element_type=jnp.float32), "lat"
    )
    self_normed = rms_normalize(first_stream).astype(jnp.bfloat16)
    self_queries = jnp.dot(self_normed, self_qkv[0], preferred_element_type=jnp.float32).astype(
        jnp.bfloat16
    )
    self_keys = jnp.dot(self_normed, self_qkv[1], preferred_element_type=jnp.float32).astype(
        jnp.bfloat16
    )
    self_values = jnp.dot(self_normed, self_qkv[2], preferred_element_type=jnp.float32).astype(
        jnp.bfloat16
    )
    all_keys, all_values = (
        lax.all_gather(self_keys, "ctx", axis=0, tiled=True),
        lax.all_gather(self_values, "ctx", axis=0, tiled=True),
    )
    own_places = row_start + jnp.arange(row_count, dtype=jnp.int32)
    later = jnp.arange(latent_count, dtype=jnp.int32)[None, :] > own_places[:, None]
    _, self_totals, self_outputs = block_attention(
        self_queries, all_keys, all_values, later, head_size
    )
    self_attended = (self_outputs / jnp.repeat(self_totals, head_size, axis=1)).astype(jnp.bfloat16)
    second_stream = first_stream + lax.psum(
        jnp.dot(self_attended, self_out, preferred_element_type=jnp.float32).astype(jnp.bfloat16),
        "lat",
    ).astype(jnp.float32)
    mlp_normed = rms_normalize(second_stream).astype(jnp.bfloat16)
    gathered = lax.all_gather(mlp_normed, "ctx", axis=0, tiled=True)
    group_input = lax.dynamic_slice_in_dim(gathered, group_index * group_rows, group_rows, 0)
    pre_hidden = jnp.dot(group_input, mlp_in, preferred_element_type=jnp.float32)
    hidden = jax.nn.gelu(pre_hidden, approximate=True).astype(jnp.bfloat16)
    place = context_index * row_count - group_index * group_rows
    inside = jnp.logical_and(place >= 0, place < group_rows)
    residual = jnp.zeros((group_rows, width), jnp.float32)
    residual = lax.dynamic_update_slice_in_dim(
        residual, second_stream, jnp.clip(place, 0, group_rows - row_count), 0
    )
    residual = jnp.where(inside, residual, 0.0)
    result = lax.psum_scatter(
        jnp.dot(hidden, mlp_out, preferred_element_type=jnp.float32) + residual,
        "ctx",
        scatter_dimension=0,
        tiled=True,
    )
    return result.astype(jnp.bfloat16)[None]


FINE = 16
MIB = 1 << 20
BIG = 58 * MIB


def rate_row(width):
    index = (jnp.arange(width, dtype=jnp.int32) // 2).astype(jnp.float32)
    return jnp.exp(index * (-2.0 * math.log(10000.0) / width))


def context_kernel(halves, ids_ref, coarse_ref, fine_ref, table_ref, out_ref, cos_ref, sin_ref):
    @pl.when(pl.program_id(0) == 0)
    def _():
        low_cos, low_sin = fine_ref[2], fine_ref[3]
        for step in range(FINE):
            high_cos, high_sin = fine_ref[0, step : step + 1, :], fine_ref[1, step : step + 1, :]
            rows = pl.ds(step * FINE, FINE)
            cos_ref[rows, :] = high_cos * low_cos - high_sin * low_sin
            sin_ref[rows, :] = high_sin * low_cos + high_cos * low_sin

    vocab, width = table_ref.shape
    rows = out_ref.shape[0]
    one_hot = (
        lax.broadcasted_iota(jnp.int32, (vocab, rows), 0) == ids_ref[0]
    ).astype(jnp.float32).astype(jnp.bfloat16)
    looked = lax.dot_general(
        one_hot, table_ref[...], (((0,), (0,)), ((), ())), preferred_element_type=jnp.float32
    )
    total = looked + coarse_ref[0, 0:1, :] * cos_ref[...] + coarse_ref[0, 1:2, :] * sin_ref[...]
    power = jnp.mean(total * total, axis=1, keepdims=True)
    normed = (total * lax.rsqrt(power + EPSILON)).astype(jnp.bfloat16)
    part = width // (2 * halves)
    for half in range(2):
        for owner in range(halves):
            source = (owner * 2 + half) * part
            target = (half * halves + owner) * part
            out_ref[:, target : target + part] = normed[:, source : source + part]


def sinusoid_tables(starts, width):
    rates = rate_row(width)
    odd = (jnp.arange(width, dtype=jnp.int32) % 2)[None, :] == 1
    angles = starts.astype(jnp.float32)[:, None] * rates[None, :]
    sines, cosines = jnp.sin(angles), jnp.cos(angles)
    coarse = jnp.stack(
        [jnp.where(odd, cosines, sines), jnp.where(odd, -sines, cosines)], axis=1
    )
    steps = jnp.arange(FINE, dtype=jnp.float32)
    high = (steps * FINE)[:, None] * rates[None, :]
    low = steps[:, None] * rates[None, :]
    fine = jnp.stack([jnp.cos(high), jnp.sin(high), jnp.cos(low), jnp.sin(low)])
    return coarse, fine


def context_rows(ids, coarse, fine, table, owners):
    count, rows = ids.shape[0], FINE * FINE
    width = table.shape[1]
    return pl.pallas_call(
        lambda *refs: context_kernel(owners, *refs),
        grid=(count,),
        in_specs=[
            pl.BlockSpec((1, 1, rows), lambda i: (i, 0, 0)),
            pl.BlockSpec((1, 2, width), lambda i: (i, 0, 0)),
            pl.BlockSpec((4, FINE, width), lambda i: (0, 0, 0)),
            pl.BlockSpec(table.shape, lambda i: (0, 0)),
        ],
        out_specs=pl.BlockSpec((rows, width), lambda i: (i, 0)),
        out_shape=jax.ShapeDtypeStruct((count * rows, width), jnp.bfloat16),
        scratch_shapes=[pltpu.VMEM((rows, width), jnp.float32)] * 2,
        cost_estimate=pl.CostEstimate(
            flops=count * rows * width * table.shape[0] * 2,
            bytes_accessed=count * rows * width * 2,
            transcendentals=0,
        ),
        compiler_params=pltpu.CompilerParams(vmem_limit_bytes=20 * MIB),
        name="context_rows",
    )(ids[:, None, :], coarse, fine, table)


def attention_kernel(key_tile, shifted, scalars_ref, query_ref, own_ref, other_ref, out_ref):
    tile, core = pl.program_id(0), scalars_ref[0]
    offset = scalars_ref[4] if shifted else 0
    parts, rows, size = query_ref.shape
    query = query_ref[...].reshape(parts * rows, size)
    rows = parts * rows
    query_place = (
        offset + (2 * tile + core) * rows + lax.broadcasted_iota(jnp.int32, (rows, 1), 0)
    )
    peak = jnp.full((rows, 1), MASKED, jnp.float32)
    output = jnp.zeros((rows, 2 * size), jnp.float32)
    outer, blocks, inner, columns = own_ref.shape
    keys = outer * inner
    for side, ref in enumerate((own_ref, other_ref)):
        for block in range(blocks):
            pair = ref[:, block, :, columns - 2 * size :].reshape(keys, 2 * size)
            for part in range(keys // key_tile):
                span = slice(part * key_tile, (part + 1) * key_tile)
                key, value = pair[span, :size], pair[span, size:]
                scores = lax.dot_general(
                    query, key, (((1,), (1,)), ((), ())), preferred_element_type=jnp.float32
                )
                key_place = (
                    (2 * block + (1 - core if side else core)) * keys
                    + part * key_tile
                    + lax.broadcasted_iota(jnp.int32, (1, key_tile), 1)
                )
                scores = jnp.where(key_place > query_place, MASKED, scores)
                new_peak = jnp.maximum(peak, jnp.max(scores, axis=1, keepdims=True))
                weights = jnp.exp(scores - new_peak).astype(jnp.bfloat16)
                output = output * jnp.exp(peak - new_peak) + jnp.dot(
                    weights,
                    jnp.concatenate([value, jnp.ones_like(value)], axis=1),
                    preferred_element_type=jnp.float32,
                )
                peak = new_peak
    final = (output[:, :size] / output[:, size:]).astype(jnp.bfloat16)
    out_ref[...] = final.reshape(out_ref.shape)


def head_attention(scalars, triples, own, other, shifted, key_tile):
    owners, tiles, rows = triples.shape[:3]
    keys = 2 * own.shape[0] * own.shape[1] * own.shape[2]
    return pl.pallas_call(
        lambda *refs: attention_kernel(key_tile, shifted, *refs),
        grid_spec=pltpu.PrefetchScalarGridSpec(
            num_scalar_prefetch=1,
            grid=(tiles,),
            in_specs=[
                pl.BlockSpec((owners, None, rows, HD), lambda i, s: (0, i, 0, 0)),
                pl.BlockSpec(own.shape, lambda i, s: (0, 0, 0, 0)),
                pl.BlockSpec(other.shape, lambda i, s: (0, 0, 0, 0)),
            ],
            out_specs=pl.BlockSpec((owners, None, rows, HD), lambda i, s: (0, i, 0, 0)),
        ),
        out_shape=jax.ShapeDtypeStruct((owners, tiles, rows, HD), jnp.bfloat16),
        cost_estimate=pl.CostEstimate(
            flops=8 * owners * tiles * rows * keys * HD,
            bytes_accessed=keys * HD * 4,
            transcendentals=owners * tiles * rows * keys,
        ),
        compiler_params=pltpu.CompilerParams(vmem_limit_bytes=14 * MIB),
        name="head_attention",
    )(scalars, triples, own, other)


def prepare_kernel(core_ref, query_ref, pair_ref, mine_ref, theirs_ref):
    heads, half, columns = mine_ref.shape
    size = columns // 3
    for target, core in ((mine_ref, core_ref[0]), (theirs_ref, 1 - core_ref[0])):
        rows = pl.ds(pl.multiple_of(core * half, half), half)
        for head in range(heads):
            span = slice(head * size, (head + 1) * size)
            target[head, :, 0:size] = query_ref[rows, span]
            target[head, :, size : 2 * size] = pair_ref[0, rows, span]
            target[head, :, 2 * size :] = pair_ref[1, rows, span]


def prepare_weights(core, cross_q, cross_kv):
    share, columns = cross_q.shape
    shape = jax.ShapeDtypeStruct((columns // HD, share // 2, 3 * HD), jnp.bfloat16)
    return pl.pallas_call(
        prepare_kernel,
        in_specs=[pl.BlockSpec(memory_space=pltpu.SMEM)]
        + [pl.BlockSpec(memory_space=pltpu.VMEM)] * 2,
        out_specs=[pl.BlockSpec(memory_space=pltpu.VMEM)] * 2,
        out_shape=[shape, shape],
        compiler_params=pltpu.CompilerParams(vmem_limit_bytes=4 * MIB),
        name="prepare_weights",
    )(core, cross_q, cross_kv)


def project_kernel(scalars_ref, heads_ref, mine_ref, theirs_ref, kept_ref, given_ref):
    core, duo = scalars_ref[0], scalars_ref[1]
    half = heads_ref.shape[0] // 2
    product = 0.0
    for side, matrix in ((core, mine_ref), (1 - core, theirs_ref)):
        left = jnp.concatenate([heads_ref[side * half + head] for head in range(half)], axis=1)
        product += jnp.dot(left, matrix[...], preferred_element_type=jnp.float32)
    kept_rows = kept_ref.shape[0]
    low, high = product[:kept_rows], product[kept_rows:]
    kept_ref[...] = jnp.where(duo == 0, low, high)
    given_ref[...] = jnp.where(duo == 0, high, low).astype(jnp.bfloat16)


IN_VMEM = pl.BlockSpec(memory_space=pltpu.VMEM)
IN_SMEM = pl.BlockSpec(memory_space=pltpu.SMEM)
ANYWHERE = pl.BlockSpec(memory_space=pl.ANY)


def project_rows(scalars, heads, mine, theirs):
    _, rows, _ = heads.shape
    inner, width = mine.shape
    return pl.pallas_call(
        project_kernel,
        in_specs=[IN_SMEM, IN_VMEM, IN_VMEM, IN_VMEM],
        out_specs=[IN_VMEM, IN_VMEM],
        out_shape=[
            jax.ShapeDtypeStruct((rows // 2, width), jnp.float32),
            jax.ShapeDtypeStruct((rows // 2, width), jnp.bfloat16),
        ],
        cost_estimate=pl.CostEstimate(
            flops=4 * rows * inner * width, bytes_accessed=4 * inner * width, transcendentals=0
        ),
        compiler_params=pltpu.CompilerParams(vmem_limit_bytes=8 * MIB),
        name="project_rows",
    )(scalars, heads, mine, theirs)


def triple_kernel(scale, scalars_ref, own_ref, other_ref, mine_hbm, theirs_hbm, out_ref, matrices, loaded):
    core, duo = scalars_ref[0], scalars_ref[1]
    heads = out_ref.shape[0] // 2
    kinds = mine_hbm.shape[0]
    loads = [
        pltpu.make_async_copy(source.at[kind], matrices.at[base + kind], loaded.at[base + kind])
        for base, source in ((0, mine_hbm), (kinds, theirs_hbm))
        for kind in range(kinds)
    ]
    ahead = 3
    for load in loads[:ahead]:
        load.start()
    own, other = own_ref[...], other_ref[...]
    rows = jnp.concatenate([jnp.where(duo == 0, own, other), jnp.where(duo == 0, other, own)])
    for index, load in enumerate(loads):
        load.wait()
        for later in loads[index + ahead : index + ahead + 1]:
            later.start()
        kind = index % kinds
        side = core if index < kinds else 1 - core
        product = jnp.dot(rows, matrices[index], preferred_element_type=jnp.float32)
        product = (product * (scale if kind == 0 else 1.0)).astype(jnp.bfloat16)
        for head in range(heads):
            out_ref[side * heads + head, :, kind * HD : (kind + 1) * HD] = product[
                :, head * HD : (head + 1) * HD
            ]


def triple_heads(scalars, own, other, mine, theirs):
    count, _ = own.shape
    kinds, inner, columns = mine.shape
    heads = columns // HD
    return pl.pallas_call(
        lambda *refs: triple_kernel(HD**-0.5, *refs),
        in_specs=[IN_SMEM, IN_VMEM, IN_VMEM, ANYWHERE, ANYWHERE],
        out_specs=IN_VMEM,
        out_shape=jax.ShapeDtypeStruct((2 * heads, 2 * count, kinds * HD), jnp.bfloat16),
        scratch_shapes=[
            pltpu.VMEM((2 * kinds, inner, columns), jnp.bfloat16),
            pltpu.SemaphoreType.DMA((2 * kinds,)),
        ],
        cost_estimate=pl.CostEstimate(
            flops=8 * kinds * count * inner * columns,
            bytes_accessed=4 * kinds * inner * columns,
            transcendentals=0,
        ),
        compiler_params=pltpu.CompilerParams(vmem_limit_bytes=BIG),
        name="triple_heads",
    )(scalars, own, other, mine, theirs)


def add_norm_kernel(base_ref, kept_ref, came_ref, stream_ref, normed_ref):
    total = base_ref[...].astype(jnp.float32) + (
        kept_ref[...] + came_ref[...].astype(jnp.float32)
    )
    stream_ref[...] = total
    normed_ref[...] = rms_normalize(total).astype(jnp.bfloat16)


def add_norm(base, kept, came):
    return pl.pallas_call(
        add_norm_kernel,
        in_specs=[IN_VMEM] * 3,
        out_specs=[IN_VMEM] * 2,
        out_shape=[
            jax.ShapeDtypeStruct(kept.shape, jnp.float32),
            jax.ShapeDtypeStruct(kept.shape, jnp.bfloat16),
        ],
        compiler_params=pltpu.CompilerParams(vmem_limit_bytes=4 * MIB),
        name="add_norm",
    )(base, kept, came)


def context_heads_kernel(
    scale, scalars_ref, context_ref, rows_ref, mine_ref, theirs_ref, pair_ref, query_ref,
    latent_ref, weights_ref,
):
    core, duo, place = scalars_ref[0], scalars_ref[1], scalars_ref[2]
    _, part, columns = mine_ref.shape
    owners, tiles, rows, size = query_ref.shape
    inner = owners * part
    keys = pair_ref.shape[0]
    tile = owners * rows
    for side, ref in ((core, mine_ref), (1 - core, theirs_ref)):
        span = pl.ds(pl.multiple_of(side * inner, inner), inner)
        weights_ref[span, :] = ref[...].reshape(inner, columns)

    def product(left, columns):
        return jnp.dot(left, weights_ref[:, columns], preferred_element_type=jnp.float32)

    for start in range(0, keys, tile):
        span = slice(start, start + tile)
        pair_ref[span, :] = product(context_ref[span, :], slice(size, 3 * size)).astype(
            jnp.bfloat16
        )
    for index in range(tiles):
        left = rows_ref[index * tile : (index + 1) * tile, :]
        query = (product(left, slice(0, size)) * scale).astype(jnp.bfloat16)
        query_ref[:, index] = query.reshape(owners, rows, size)
    start = pl.multiple_of(duo * tile + place * rows, rows)
    latent = rows_ref[pl.ds(start, rows), :]
    for half in range(2):
        for owner in range(owners):
            source = half * inner + owner * part
            target = (owner * 2 + half) * part
            latent_ref[:, target : target + part] = latent[:, source : source + part]


def context_heads(scalars, context, latent, mine, theirs, shape):
    owners, tiles, rows = shape
    keys, width = context.shape
    size = mine.shape[2] // 3
    return pl.pallas_call(
        lambda *refs: context_heads_kernel(size**-0.5, *refs),
        in_specs=[IN_SMEM] + [IN_VMEM] * 4,
        out_specs=[IN_VMEM] * 3,
        out_shape=[
            jax.ShapeDtypeStruct((keys, 2 * size), jnp.bfloat16),
            jax.ShapeDtypeStruct((owners, tiles, rows, size), jnp.bfloat16),
            jax.ShapeDtypeStruct((rows, width), jnp.bfloat16),
        ],
        scratch_shapes=[pltpu.VMEM((width, 3 * size), jnp.bfloat16)],
        cost_estimate=pl.CostEstimate(
            flops=4 * (keys + owners * tiles * rows) * width * size,
            bytes_accessed=keys * width * 2,
            transcendentals=0,
        ),
        compiler_params=pltpu.CompilerParams(vmem_limit_bytes=12 * MIB),
        name="context_heads",
    )(scalars, context, latent, mine, theirs)


def order_kernel(scalars_ref, mine_ref, theirs_ref, *block_refs):
    core, place = scalars_ref[0], scalars_ref[2]
    heads = mine_ref.shape[0]
    for distance, block_ref in enumerate(block_refs):
        head = place ^ distance
        local = lax.rem(head, heads)
        own = lax.div(head, heads) == core

        @pl.when(own)
        def _():
            block_ref[...] = mine_ref[local]

        @pl.when(jnp.logical_not(own))
        def _():
            block_ref[...] = theirs_ref[local]


def order_blocks(scalars, mine, theirs):
    heads, rows, columns = mine.shape
    return pl.pallas_call(
        order_kernel,
        in_specs=[IN_SMEM, IN_VMEM, IN_VMEM],
        out_specs=[IN_VMEM] * (2 * heads),
        out_shape=[jax.ShapeDtypeStruct((rows, columns), jnp.bfloat16)] * (2 * heads),
        compiler_params=pltpu.CompilerParams(vmem_limit_bytes=4 * MIB),
        name="order_blocks",
    )(scalars, mine, theirs)


def gather_kernel(scalars_ref, *refs):
    *block_refs, out_ref = refs
    for distance, block_ref in enumerate(block_refs):
        out_ref[scalars_ref[2] ^ distance] = block_ref[...]


def gather_blocks(scalars, blocks):
    return pl.pallas_call(
        gather_kernel,
        in_specs=[IN_SMEM] + [IN_VMEM] * len(blocks),
        out_specs=IN_VMEM,
        out_shape=jax.ShapeDtypeStruct((len(blocks), *blocks[0].shape), blocks[0].dtype),
        compiler_params=pltpu.CompilerParams(vmem_limit_bytes=4 * MIB),
        name="gather_blocks",
    )(scalars, *blocks)


def mlp_kernel(scalars_ref, *refs):
    group = scalars_ref[3]
    *refs, hidden_ref = refs
    count = (len(refs) - 10) // 2
    blocks, (in_ref, out_ref), rest = refs[:count], refs[count : count + 2], refs[count + 2 :]
    in_parts, out_parts, shares = rest[:4], rest[4:8], rest[8:]
    rows = jnp.concatenate([block[...] for block in blocks])
    depth, units = in_parts[0].shape[0], out_parts[0].shape[0]

    def hidden_of(total):
        return jax.nn.gelu(total, approximate=True).astype(jnp.bfloat16)

    total = jnp.dot(rows, in_ref[...], preferred_element_type=jnp.float32)
    share = jnp.dot(hidden_of(total), out_ref[...], preferred_element_type=jnp.float32)
    quarters = [group, group ^ 2, group ^ 1, group ^ 3]
    total = 0.0
    for quarter, part in zip(quarters, in_parts):
        span = pl.ds(pl.multiple_of(quarter * depth, depth), depth)
        piece = jnp.concatenate([block[:, span] for block in blocks])
        total += jnp.dot(piece, part[...], preferred_element_type=jnp.float32)
    hidden_ref[...] = hidden_of(total)
    for quarter, part in zip(quarters, out_parts):
        span = pl.ds(pl.multiple_of(quarter * units, units), units)
        share += jnp.dot(hidden_ref[:, span], part[...], preferred_element_type=jnp.float32)
    each = blocks[0].shape[0]
    for index, target in enumerate(shares):
        target[...] = share[index * each : (index + 1) * each].astype(target.dtype)


def mlp_shares(scalars, blocks, mlp_in, mlp_out, in_parts, out_parts):
    first = jax.ShapeDtypeStruct(blocks[0].shape, jnp.float32)
    other = jax.ShapeDtypeStruct(blocks[0].shape, jnp.bfloat16)
    operands = [*blocks, mlp_in, mlp_out, *in_parts, *out_parts]
    return pl.pallas_call(
        mlp_kernel,
        in_specs=[IN_SMEM] + [IN_VMEM] * len(operands),
        out_specs=[IN_VMEM] * len(blocks),
        out_shape=[first] + [other] * (len(blocks) - 1),
        scratch_shapes=[
            pltpu.VMEM((len(blocks) * blocks[0].shape[0], mlp_in.shape[1]), jnp.bfloat16)
        ],
        cost_estimate=pl.CostEstimate(
            flops=8 * len(blocks) * blocks[0].size * mlp_in.shape[1],
            bytes_accessed=8 * mlp_in.size,
            transcendentals=0,
        ),
        compiler_params=pltpu.CompilerParams(vmem_limit_bytes=12 * MIB),
        name="mlp_shares",
    )(scalars, *operands)


def paired_device(
    token_ids,
    latent_offset,
    embed_table,
    cross_q,
    cross_kv,
    cross_out,
    self_qkv,
    self_out,
    mlp_in,
    mlp_out,
):
    owners = lax.axis_size("ctx")
    groups = lax.axis_size("lat")
    place = lax.axis_index("ctx")
    group = lax.axis_index("lat")
    core = group % 2
    duo = group // 2
    duos = groups // 2
    offset = latent_offset[0]
    block = token_ids.shape[0]
    width = embed_table.shape[1]
    share = cross_q.shape[0]
    group_rows = LATENTS // groups
    rows = group_rows // owners
    duo_rows = duos * rows
    scalars = jnp.stack([core, duo, place, group, offset]).astype(jnp.int32)

    def swap(value):
        return lax.ppermute(value, "lat", [(i, i ^ 1) for i in range(groups)])

    def cross(value):
        return lax.ppermute(value, "lat", [(i, i ^ 2) for i in range(groups)])

    def exchange(value):
        return lax.all_to_all(value, "ctx", 0, 0, tiled=True)

    def across(value, distance):
        return lax.ppermute(value, "ctx", [(i, i ^ distance) for i in range(owners)])

    def quarter(matrix):
        size = matrix.shape[0] // groups
        return lax.dynamic_slice_in_dim(matrix, group * size, size, 0)

    mine, theirs = prepare_weights(scalars, cross_q, cross_kv)
    blocks = order_blocks(scalars, mine, swap(theirs))

    lanes = token_ids.reshape(1, block // HD, HD)
    every_token = exchange(jnp.broadcast_to(lanes, (owners, block // HD, HD)))
    arrived = [blocks[0]]
    for distance in range(1, owners):
        arrived.append(across(blocks[distance], distance))

    step = FINE * FINE
    latent_starts = (2 * jnp.arange(duos, dtype=jnp.int32) + core) * group_rows
    pieces = block // step
    half_blocks = owners // 2
    token_blocks = every_token.reshape(half_blocks, 2, block)
    own_ids = lax.dynamic_index_in_dim(token_blocks, core, 1, keepdims=False)
    flat_tokens = every_token.reshape(owners * block)
    latent_ids = jnp.stack(
        [
            lax.dynamic_slice_in_dim(
                flat_tokens, offset + (2 * i + core) * group_rows, group_rows, 0
            )
            for i in range(duos)
        ]
    )
    fetched = []
    for matrix in (mlp_in, mlp_out):
        one = across(quarter(matrix), 1)
        two = cross(one)
        three = swap(one)
        four = swap(two)
        fetched.append((one, two, three, four))

    block_starts = (2 * jnp.arange(half_blocks, dtype=jnp.int32) + core) * block
    inner = jnp.arange(pieces, dtype=jnp.int32) * step
    latent_inner = jnp.arange(group_rows // step, dtype=jnp.int32) * step
    starts = jnp.concatenate(
        [
            (block_starts[:, None] + inner[None, :]).reshape(-1),
            (offset + latent_starts[:, None] + latent_inner[None, :]).reshape(-1),
        ]
    )
    coarse, fine = sinusoid_tables(starts, width)
    tiles = half_blocks * pieces
    context = context_rows(own_ids.reshape(-1, step), coarse[:tiles], fine, embed_table, owners)
    latent = context_rows(latent_ids.reshape(-1, step), coarse[tiles:], fine, embed_table, owners)
    arrived = gather_blocks(scalars, arrived)
    arrived_other = swap(arrived)
    pairs, queries, own_latent = context_heads(
        scalars, context, latent, arrived, arrived_other, (owners, duos, rows)
    )
    other_pairs = swap(pairs)
    by_block = (1, half_blocks, block, 2 * HD)
    attended = head_attention(
        scalars, queries, pairs.reshape(by_block), other_pairs.reshape(by_block), True, block
    )

    def project(base, attended, mine, theirs):
        heads = exchange(attended.reshape(owners, duo_rows, HD))
        kept, given = project_rows(scalars, heads, mine, theirs)
        return add_norm(base, kept, cross(given))

    first_stream, normed = project(own_latent, attended, cross_out, swap(cross_out))
    normed_other = cross(normed)
    self_qkv_other = swap(self_qkv)
    triples = exchange(triple_heads(scalars, normed, normed_other, self_qkv, self_qkv_other))
    triples = triples.reshape(owners, duos, rows, 3 * HD)
    self_attended = head_attention(
        scalars, triples, triples, swap(triples), False, group_rows
    )
    second_stream, mlp_normed = project(
        first_stream, self_attended, self_out, swap(self_out)
    )

    distances = [2 * i for i in range(1, owners // 2)]
    blocks = [mlp_normed] + [across(mlp_normed, distance) for distance in distances]
    kept, *given = mlp_shares(scalars, blocks, mlp_in, mlp_out, *fetched)
    result = second_stream + kept
    for share, distance in zip(given, distances):
        result = result + across(share, distance).astype(jnp.float32)
    return result.astype(jnp.bfloat16)[None]


def solution(mesh):
    placed = (
        P("ctx"),
        P(),
        P(),
        P("ctx", "lat"),
        P(None, "ctx", "lat"),
        P("lat", None),
        P(None, None, "lat"),
        P("lat", None),
        P(None, "ctx"),
        P("ctx", None),
    )

    def per_device(*arguments):
        owners, groups = lax.axis_size("ctx"), lax.axis_size("lat")
        local_heads = arguments[3].shape[1] // HD
        paired = groups == 4 and owners == 2 * local_heads and owners & (owners - 1) == 0
        return (paired_device if paired else general_device)(*arguments)

    return jax.shard_map(
        per_device, mesh=mesh, in_specs=placed, out_specs=P("lat", "ctx", None), check_vma=False
    )
```

```python
import math

import jax
import jax.numpy as jnp
from jax import lax
from jax.experimental import pallas as pl
from jax.experimental.pallas import tpu as pltpu
from jax.sharding import PartitionSpec as P

HD = 128
LATENTS = 1024


EPSILON = 1e-06
MASKED = -1e30


def rms_normalize(values):
    return values * lax.rsqrt(jnp.mean(values * values, axis=-1, keepdims=True) + EPSILON)


def sinusoid(places, width):
    index = jnp.arange(width // 2).astype(jnp.float32)
    rates = jnp.exp(index * (-2.0 * math.log(10000.0) / width))
    angles = places.astype(jnp.float32)[:, None] * rates[None, :]
    return jnp.stack([jnp.sin(angles), jnp.cos(angles)], axis=-1).reshape(places.shape[0], width)


def embed_rows(token_rows, table, places):
    vocab_range = jnp.arange(table.shape[0], dtype=jnp.int32)
    one_hot = (token_rows[:, None] == vocab_range[None, :]).astype(jnp.bfloat16)
    looked = jnp.dot(one_hot, table, preferred_element_type=jnp.float32)
    return rms_normalize(looked + sinusoid(places, table.shape[1])).astype(jnp.bfloat16)


def block_attention(queries, keys, values, blocked, head_size):
    scale = 1.0 / math.sqrt(head_size)
    head_count = queries.shape[1] // head_size
    query_rows = queries.shape[0]
    key_rows = keys.shape[0]
    query_heads = jnp.transpose(queries.reshape(query_rows, head_count, head_size), (1, 0, 2))
    key_heads = jnp.transpose(keys.reshape(key_rows, head_count, head_size), (1, 0, 2))
    value_heads = jnp.transpose(values.reshape(key_rows, head_count, head_size), (1, 0, 2))

    def one_head(operands):
        query, key, value = operands
        scores = (
            lax.dot_general(
                query, key, (((1,), (1,)), ((), ())), preferred_element_type=jnp.float32
            )
            * scale
        )
        scores = jnp.where(blocked, MASKED, scores)
        peak = jnp.max(scores, axis=1)
        weights = jnp.exp(scores - peak[:, None]).astype(jnp.bfloat16)
        total = jnp.sum(weights.astype(jnp.float32), axis=1)
        output = jnp.dot(weights, value, preferred_element_type=jnp.float32)
        return (peak, total, output)

    maxima, totals, outputs = lax.map(one_head, (query_heads, key_heads, value_heads))
    merged = jnp.transpose(outputs, (1, 0, 2)).reshape(query_rows, head_count * head_size)
    return (jnp.transpose(maxima), jnp.transpose(totals), merged)


def general_device(
    token_ids,
    latent_offset,
    embed_table,
    cross_q,
    cross_kv,
    cross_out,
    self_qkv,
    self_out,
    mlp_in,
    mlp_out,
):
    context_count = lax.axis_size("ctx")
    group_count = lax.axis_size("lat")
    context_index = lax.axis_index("ctx")
    group_index = lax.axis_index("lat")
    block_length = token_ids.shape[0]
    head_size = HD
    local_width = cross_q.shape[1]
    local_heads = local_width // head_size
    width = embed_table.shape[1]
    offset = latent_offset[0]
    latent_count = LATENTS
    row_count = latent_count // context_count
    group_rows = latent_count // group_count
    places = context_index * block_length + jnp.arange(block_length, dtype=jnp.int32)
    context = embed_rows(token_ids, embed_table, places)
    piece = lax.all_gather(cross_kv, "ctx", axis=1, tiled=True)
    columns = context
    key_sum = jnp.dot(columns, piece[0], preferred_element_type=jnp.float32)
    value_sum = jnp.dot(columns, piece[1], preferred_element_type=jnp.float32)
    keys = key_sum.astype(jnp.bfloat16)
    values = value_sum.astype(jnp.bfloat16)
    every_token = lax.all_gather(token_ids, "ctx", axis=0, tiled=True)
    latent_tokens = lax.dynamic_slice_in_dim(every_token, offset, latent_count, 0)
    latent_places = offset + jnp.arange(latent_count, dtype=jnp.int32)
    latent = embed_rows(latent_tokens, embed_table, latent_places)
    columns = latent
    query_sum = jnp.dot(
        columns,
        lax.all_gather(cross_q, "ctx", axis=0, tiled=True),
        preferred_element_type=jnp.float32,
    )
    queries = query_sum.astype(jnp.bfloat16)
    blocked = places[None, :] > latent_places[:, None]
    maxima, totals, outputs = block_attention(queries, keys, values, blocked, head_size)
    row_start = context_index * row_count
    came_max, came_total, came_out = (
        lax.all_to_all(maxima[:, None, :], "ctx", split_axis=0, concat_axis=1, tiled=True),
        lax.all_to_all(totals[:, None, :], "ctx", split_axis=0, concat_axis=1, tiled=True),
        lax.all_to_all(outputs[:, None, :], "ctx", split_axis=0, concat_axis=1, tiled=True),
    )
    peak = jnp.max(came_max, axis=1, keepdims=True)
    factor = jnp.exp(came_max - peak)
    own_totals = jnp.sum(came_total * factor, axis=1)
    spread = (
        came_out.reshape(row_count, context_count, local_heads, head_size) * factor[:, :, :, None]
    )
    own_outputs = jnp.sum(spread, axis=1).reshape(row_count, local_width)
    attended = (own_outputs / jnp.repeat(own_totals, head_size, axis=1)).astype(jnp.bfloat16)
    own_latent = lax.dynamic_slice_in_dim(latent, row_start, row_count, 0).astype(jnp.float32)
    first_stream = own_latent + lax.psum(
        jnp.dot(attended, cross_out, preferred_element_type=jnp.float32), "lat"
    )
    self_normed = rms_normalize(first_stream).astype(jnp.bfloat16)
    self_queries = jnp.dot(self_normed, self_qkv[0], preferred_element_type=jnp.float32).astype(
        jnp.bfloat16
    )
    self_keys = jnp.dot(self_normed, self_qkv[1], preferred_element_type=jnp.float32).astype(
        jnp.bfloat16
    )
    self_values = jnp.dot(self_normed, self_qkv[2], preferred_element_type=jnp.float32).astype(
        jnp.bfloat16
    )
    all_keys, all_values = (
        lax.all_gather(self_keys, "ctx", axis=0, tiled=True),
        lax.all_gather(self_values, "ctx", axis=0, tiled=True),
    )
    own_places = row_start + jnp.arange(row_count, dtype=jnp.int32)
    later = jnp.arange(latent_count, dtype=jnp.int32)[None, :] > own_places[:, None]
    _, self_totals, self_outputs = block_attention(
        self_queries, all_keys, all_values, later, head_size
    )
    self_attended = (self_outputs / jnp.repeat(self_totals, head_size, axis=1)).astype(jnp.bfloat16)
    second_stream = first_stream + lax.psum(
        jnp.dot(self_attended, self_out, preferred_element_type=jnp.float32).astype(jnp.bfloat16),
        "lat",
    ).astype(jnp.float32)
    mlp_normed = rms_normalize(second_stream).astype(jnp.bfloat16)
    gathered = lax.all_gather(mlp_normed, "ctx", axis=0, tiled=True)
    group_input = lax.dynamic_slice_in_dim(gathered, group_index * group_rows, group_rows, 0)
    pre_hidden = jnp.dot(group_input, mlp_in, preferred_element_type=jnp.float32)
    hidden = jax.nn.gelu(pre_hidden, approximate=True).astype(jnp.bfloat16)
    place = context_index * row_count - group_index * group_rows
    inside = jnp.logical_and(place >= 0, place < group_rows)
    residual = jnp.zeros((group_rows, width), jnp.float32)
    residual = lax.dynamic_update_slice_in_dim(
        residual, second_stream, jnp.clip(place, 0, group_rows - row_count), 0
    )
    residual = jnp.where(inside, residual, 0.0)
    result = lax.psum_scatter(
        jnp.dot(hidden, mlp_out, preferred_element_type=jnp.float32) + residual,
        "ctx",
        scatter_dimension=0,
        tiled=True,
    )
    return result.astype(jnp.bfloat16)[None]


FINE = 16
MIB = 1 << 20


def rate_row(width):
    index = (jnp.arange(width, dtype=jnp.int32) // 2).astype(jnp.float32)
    return jnp.exp(index * (-2.0 * math.log(10000.0) / width))


def context_kernel(
    halves, first, ids_ref, sine_ref, cosine_ref, high_cos_ref, high_sin_ref, low_cos_ref,
    low_sin_ref, table_ref, out_ref, cos_ref, sin_ref,
):
    tile = pl.program_id(0)

    @pl.when(tile == 0)
    def _():
        low_cos, low_sin = low_cos_ref[...], low_sin_ref[...]
        for step in range(FINE):
            high_cos, high_sin = high_cos_ref[step : step + 1], high_sin_ref[step : step + 1]
            rows = pl.ds(step * FINE, FINE)
            cos_ref[rows, :] = high_cos * low_cos - high_sin * low_sin
            sin_ref[rows, :] = high_sin * low_cos + high_cos * low_sin

    vocab, width = table_ref.shape
    rows = out_ref.shape[0]
    one_hot = (
        lax.broadcasted_iota(jnp.int32, (vocab, rows), 0) == ids_ref[0]
    ).astype(jnp.float32).astype(jnp.bfloat16)
    looked = lax.dot_general(
        one_hot, table_ref[...], (((0,), (0,)), ((), ())), preferred_element_type=jnp.float32
    )
    start = pl.ds(first + tile, 1)
    total = looked + sine_ref[start, :] * cos_ref[...] + cosine_ref[start, :] * sin_ref[...]
    power = jnp.mean(total * total, axis=1, keepdims=True)
    normed = (total * lax.rsqrt(power + EPSILON)).astype(jnp.bfloat16)
    part = width // (2 * halves)
    for half in range(2):
        for owner in range(halves):
            source = (owner * 2 + half) * part
            target = (half * halves + owner) * part
            out_ref[:, target : target + part] = normed[:, source : source + part]


def sinusoid_tables(starts, width):
    rates = rate_row(width)
    odd = (jnp.arange(width, dtype=jnp.int32) % 2)[None, :] == 1
    places = jnp.pad(starts, (0, -starts.shape[0] % FINE)).astype(jnp.float32)
    angles = places[:, None] * rates[None, :]
    sines, cosines = jnp.sin(angles), jnp.cos(angles)
    steps = jnp.arange(FINE, dtype=jnp.float32)
    high = (steps * FINE)[:, None] * rates[None, :]
    low = steps[:, None] * rates[None, :]
    return (
        jnp.where(odd, cosines, sines),
        jnp.where(odd, -sines, cosines),
        jnp.cos(high),
        jnp.sin(high),
        jnp.cos(low),
        jnp.sin(low),
    )


def context_rows(ids, first, tables, table, owners):
    count, rows = ids.shape[0], FINE * FINE
    width = table.shape[1]
    return pl.pallas_call(
        lambda *refs: context_kernel(owners, first, *refs),
        grid=(count,),
        in_specs=[pl.BlockSpec((1, 1, rows), lambda i: (i, 0, 0))]
        + [pl.BlockSpec(array.shape, lambda i: (0, 0)) for array in (*tables, table)],
        out_specs=pl.BlockSpec((rows, width), lambda i: (i, 0)),
        out_shape=jax.ShapeDtypeStruct((count * rows, width), jnp.bfloat16),
        scratch_shapes=[pltpu.VMEM((rows, width), jnp.float32)] * 2,
        cost_estimate=pl.CostEstimate(
            flops=count * rows * width * table.shape[0] * 2,
            bytes_accessed=count * rows * width * 2,
            transcendentals=0,
        ),
        compiler_params=pltpu.CompilerParams(vmem_limit_bytes=20 * MIB),
        name="context_rows",
    )(ids[:, None, :], *tables, table)


def attention_kernel(key_tile, shifted, scalars_ref, query_ref, own_ref, other_ref, out_ref):
    tile, core = pl.program_id(0), scalars_ref[0]
    offset = scalars_ref[4] if shifted else 0
    parts, rows, size = query_ref.shape
    query = query_ref[...].reshape(parts * rows, size)
    rows = parts * rows
    query_place = (
        offset + (2 * tile + core) * rows + lax.broadcasted_iota(jnp.int32, (rows, 1), 0)
    )
    peak = jnp.full((rows, 1), MASKED, jnp.float32)
    output = jnp.zeros((rows, 2 * size), jnp.float32)
    outer, blocks, inner, columns = own_ref.shape
    keys = outer * inner
    for side, ref in enumerate((own_ref, other_ref)):
        for block in range(blocks):
            pair = ref[:, block, :, columns - 2 * size :].reshape(keys, 2 * size)
            for part in range(keys // key_tile):
                span = slice(part * key_tile, (part + 1) * key_tile)
                key, value = pair[span, :size], pair[span, size:]
                scores = lax.dot_general(
                    query, key, (((1,), (1,)), ((), ())), preferred_element_type=jnp.float32
                )
                key_place = (
                    (2 * block + (1 - core if side else core)) * keys
                    + part * key_tile
                    + lax.broadcasted_iota(jnp.int32, (1, key_tile), 1)
                )
                scores = jnp.where(key_place > query_place, MASKED, scores)
                new_peak = jnp.maximum(peak, jnp.max(scores, axis=1, keepdims=True))
                weights = jnp.exp(scores - new_peak).astype(jnp.bfloat16)
                output = output * jnp.exp(peak - new_peak) + jnp.dot(
                    weights,
                    jnp.concatenate([value, jnp.ones_like(value)], axis=1),
                    preferred_element_type=jnp.float32,
                )
                peak = new_peak
    final = (output[:, :size] / output[:, size:]).astype(jnp.bfloat16)
    out_ref[...] = final.reshape(out_ref.shape)


def head_attention(scalars, triples, own, other, shifted, key_tile):
    owners, tiles, rows = triples.shape[:3]
    keys = 2 * own.shape[0] * own.shape[1] * own.shape[2]
    return pl.pallas_call(
        lambda *refs: attention_kernel(key_tile, shifted, *refs),
        grid_spec=pltpu.PrefetchScalarGridSpec(
            num_scalar_prefetch=1,
            grid=(tiles,),
            in_specs=[
                pl.BlockSpec((owners, None, rows, HD), lambda i, s: (0, i, 0, 0)),
                pl.BlockSpec(own.shape, lambda i, s: (0, 0, 0, 0)),
                pl.BlockSpec(other.shape, lambda i, s: (0, 0, 0, 0)),
            ],
            out_specs=pl.BlockSpec((owners, None, rows, HD), lambda i, s: (0, i, 0, 0)),
        ),
        out_shape=jax.ShapeDtypeStruct((owners, tiles, rows, HD), jnp.bfloat16),
        cost_estimate=pl.CostEstimate(
            flops=8 * owners * tiles * rows * keys * HD,
            bytes_accessed=keys * HD * 4,
            transcendentals=owners * tiles * rows * keys,
        ),
        compiler_params=pltpu.CompilerParams(vmem_limit_bytes=14 * MIB),
        name="head_attention",
    )(scalars, triples, own, other)


def in_hbm(array):
    return pltpu.with_memory_space_constraint(array, pltpu.HBM)


def prepare_kernel(
    scalars_ref, query_hbm, pair_hbm, matrix_hbm, mine_ref, theirs_ref, part_ref, query_ref,
    pair_ref, loaded,
):
    core, group = scalars_ref[0], scalars_ref[3]
    heads, half, columns = mine_ref.shape
    size = columns // 3
    depth = part_ref.shape[0]
    quarter = matrix_hbm.at[pl.ds(pl.multiple_of(group * depth, depth), depth), :]
    loads = [
        pltpu.make_async_copy(query_hbm, query_ref, loaded.at[0]),
        pltpu.make_async_copy(pair_hbm, pair_ref, loaded.at[1]),
        pltpu.make_async_copy(quarter, part_ref, loaded.at[2]),
    ]
    for load in loads:
        load.start()
    loads[0].wait()
    loads[1].wait()
    for target, side in ((theirs_ref, 1 - core), (mine_ref, core)):
        rows = pl.ds(pl.multiple_of(side * half, half), half)
        for head in range(heads):
            span = slice(head * size, (head + 1) * size)
            target[head, :, 0:size] = query_ref[rows, span]
            target[head, :, size : 2 * size] = pair_ref[0, rows, span]
            target[head, :, 2 * size :] = pair_ref[1, rows, span]
    loads[2].wait()


def prepare_weights(scalars, cross_q, cross_kv, matrix, groups):
    share, columns = cross_q.shape
    shape = jax.ShapeDtypeStruct((columns // HD, share // 2, 3 * HD), jnp.bfloat16)
    part = jax.ShapeDtypeStruct((matrix.shape[0] // groups, matrix.shape[1]), jnp.bfloat16)
    return pl.pallas_call(
        prepare_kernel,
        in_specs=[IN_SMEM] + [ANYWHERE] * 3,
        out_specs=[IN_VMEM] * 3,
        out_shape=[shape, shape, part],
        scratch_shapes=[
            pltpu.VMEM(cross_q.shape, jnp.bfloat16),
            pltpu.VMEM(cross_kv.shape, jnp.bfloat16),
            pltpu.SemaphoreType.DMA((3,)),
        ],
        compiler_params=pltpu.CompilerParams(vmem_limit_bytes=8 * MIB),
        name="prepare_weights",
    )(scalars, in_hbm(cross_q), in_hbm(cross_kv), in_hbm(matrix))


def project_kernel(scalars_ref, heads_ref, mine_ref, theirs_ref, kept_ref, given_ref):
    core, duo = scalars_ref[0], scalars_ref[1]
    half = heads_ref.shape[0] // 2
    product = 0.0
    for side, matrix in ((core, mine_ref), (1 - core, theirs_ref)):
        left = jnp.concatenate([heads_ref[side * half + head] for head in range(half)], axis=1)
        product += jnp.dot(left, matrix[...], preferred_element_type=jnp.float32)
    kept_rows = kept_ref.shape[0]
    low, high = product[:kept_rows], product[kept_rows:]
    kept_ref[...] = jnp.where(duo == 0, low, high)
    given_ref[...] = jnp.where(duo == 0, high, low).astype(jnp.bfloat16)


IN_VMEM = pl.BlockSpec(memory_space=pltpu.VMEM)
IN_SMEM = pl.BlockSpec(memory_space=pltpu.SMEM)
ANYWHERE = pl.BlockSpec(memory_space=pl.ANY)


def project_rows(scalars, heads, mine, theirs):
    _, rows, _ = heads.shape
    inner, width = mine.shape
    return pl.pallas_call(
        project_kernel,
        in_specs=[IN_SMEM, IN_VMEM, IN_VMEM, IN_VMEM],
        out_specs=[IN_VMEM, IN_VMEM],
        out_shape=[
            jax.ShapeDtypeStruct((rows // 2, width), jnp.float32),
            jax.ShapeDtypeStruct((rows // 2, width), jnp.bfloat16),
        ],
        cost_estimate=pl.CostEstimate(
            flops=4 * rows * inner * width, bytes_accessed=4 * inner * width, transcendentals=0
        ),
        compiler_params=pltpu.CompilerParams(vmem_limit_bytes=8 * MIB),
        name="project_rows",
    )(scalars, heads, mine, theirs)


def triple_kernel(scale, scalars_ref, own_ref, other_ref, mine_hbm, theirs_hbm, out_ref, matrices, loaded):
    core, duo = scalars_ref[0], scalars_ref[1]
    heads = out_ref.shape[0] // 2
    kinds = mine_hbm.shape[0]
    loads = [
        pltpu.make_async_copy(source.at[kind], matrices.at[base + kind], loaded.at[base + kind])
        for base, source in ((0, mine_hbm), (kinds, theirs_hbm))
        for kind in range(kinds)
    ]
    ahead = 3
    for load in loads[:ahead]:
        load.start()
    own, other = own_ref[...], other_ref[...]
    rows = jnp.concatenate([jnp.where(duo == 0, own, other), jnp.where(duo == 0, other, own)])
    for index, load in enumerate(loads):
        load.wait()
        for later in loads[index + ahead : index + ahead + 1]:
            later.start()
        kind = index % kinds
        side = core if index < kinds else 1 - core
        product = jnp.dot(rows, matrices[index], preferred_element_type=jnp.float32)
        product = (product * (scale if kind == 0 else 1.0)).astype(jnp.bfloat16)
        for head in range(heads):
            out_ref[side * heads + head, :, kind * HD : (kind + 1) * HD] = product[
                :, head * HD : (head + 1) * HD
            ]


def triple_heads(scalars, own, other, mine, theirs):
    count, _ = own.shape
    kinds, inner, columns = mine.shape
    heads = columns // HD
    return pl.pallas_call(
        lambda *refs: triple_kernel(HD**-0.5, *refs),
        in_specs=[IN_SMEM, IN_VMEM, IN_VMEM, ANYWHERE, ANYWHERE],
        out_specs=IN_VMEM,
        out_shape=jax.ShapeDtypeStruct((2 * heads, 2 * count, kinds * HD), jnp.bfloat16),
        scratch_shapes=[
            pltpu.VMEM((2 * kinds, inner, columns), jnp.bfloat16),
            pltpu.SemaphoreType.DMA((2 * kinds,)),
        ],
        cost_estimate=pl.CostEstimate(
            flops=8 * kinds * count * inner * columns,
            bytes_accessed=4 * kinds * inner * columns,
            transcendentals=0,
        ),
        compiler_params=pltpu.CompilerParams(vmem_limit_bytes=20 * MIB),
        name="triple_heads",
    )(scalars, own, other, in_hbm(mine), in_hbm(theirs))


def add_norm_kernel(base_ref, kept_ref, came_ref, stream_ref, normed_ref):
    total = base_ref[...].astype(jnp.float32) + (
        kept_ref[...] + came_ref[...].astype(jnp.float32)
    )
    stream_ref[...] = total
    normed_ref[...] = rms_normalize(total).astype(jnp.bfloat16)


def add_norm(base, kept, came):
    return pl.pallas_call(
        add_norm_kernel,
        in_specs=[IN_VMEM] * 3,
        out_specs=[IN_VMEM] * 2,
        out_shape=[
            jax.ShapeDtypeStruct(kept.shape, jnp.float32),
            jax.ShapeDtypeStruct(kept.shape, jnp.bfloat16),
        ],
        compiler_params=pltpu.CompilerParams(vmem_limit_bytes=4 * MIB),
        name="add_norm",
    )(base, kept, came)


def context_heads_kernel(
    scale, scalars_ref, context_ref, rows_ref, mine_ref, theirs_ref, pair_ref, query_ref,
    latent_ref, weights_ref,
):
    core, duo, place = scalars_ref[0], scalars_ref[1], scalars_ref[2]
    _, part, columns = mine_ref.shape
    owners, tiles, rows, size = query_ref.shape
    inner = owners * part
    keys = pair_ref.shape[0]
    tile = owners * rows
    for side, ref in ((core, mine_ref), (1 - core, theirs_ref)):
        span = pl.ds(pl.multiple_of(side * inner, inner), inner)
        weights_ref[span, :] = ref[...].reshape(inner, columns)

    def product(left, columns):
        return jnp.dot(left, weights_ref[:, columns], preferred_element_type=jnp.float32)

    for start in range(0, keys, tile):
        span = slice(start, start + tile)
        pair_ref[span, :] = product(context_ref[span, :], slice(size, 3 * size)).astype(
            jnp.bfloat16
        )
    for index in range(tiles):
        left = rows_ref[index * tile : (index + 1) * tile, :]
        query = (product(left, slice(0, size)) * scale).astype(jnp.bfloat16)
        query_ref[:, index] = query.reshape(owners, rows, size)
    start = pl.multiple_of(duo * tile + place * rows, rows)
    latent = rows_ref[pl.ds(start, rows), :]
    for half in range(2):
        for owner in range(owners):
            source = half * inner + owner * part
            target = (owner * 2 + half) * part
            latent_ref[:, target : target + part] = latent[:, source : source + part]


def context_heads(scalars, context, latent, mine, theirs, shape):
    owners, tiles, rows = shape
    keys, width = context.shape
    size = mine.shape[2] // 3
    return pl.pallas_call(
        lambda *refs: context_heads_kernel(size**-0.5, *refs),
        in_specs=[IN_SMEM] + [IN_VMEM] * 4,
        out_specs=[IN_VMEM] * 3,
        out_shape=[
            jax.ShapeDtypeStruct((keys, 2 * size), jnp.bfloat16),
            jax.ShapeDtypeStruct((owners, tiles, rows, size), jnp.bfloat16),
            jax.ShapeDtypeStruct((rows, width), jnp.bfloat16),
        ],
        scratch_shapes=[pltpu.VMEM((width, 3 * size), jnp.bfloat16)],
        cost_estimate=pl.CostEstimate(
            flops=4 * (keys + owners * tiles * rows) * width * size,
            bytes_accessed=keys * width * 2,
            transcendentals=0,
        ),
        compiler_params=pltpu.CompilerParams(vmem_limit_bytes=12 * MIB),
        name="context_heads",
    )(scalars, context, latent, mine, theirs)


def order_kernel(scalars_ref, mine_ref, theirs_ref, *block_refs):
    core, place = scalars_ref[0], scalars_ref[2]
    heads = mine_ref.shape[0]
    for distance, block_ref in enumerate(block_refs):
        head = place ^ distance
        local = lax.rem(head, heads)
        own = lax.div(head, heads) == core

        @pl.when(own)
        def _():
            block_ref[...] = mine_ref[local]

        @pl.when(jnp.logical_not(own))
        def _():
            block_ref[...] = theirs_ref[local]


def order_blocks(scalars, mine, theirs):
    heads, rows, columns = mine.shape
    return pl.pallas_call(
        order_kernel,
        in_specs=[IN_SMEM, IN_VMEM, IN_VMEM],
        out_specs=[IN_VMEM] * (2 * heads),
        out_shape=[jax.ShapeDtypeStruct((rows, columns), jnp.bfloat16)] * (2 * heads),
        compiler_params=pltpu.CompilerParams(vmem_limit_bytes=4 * MIB),
        name="order_blocks",
    )(scalars, mine, theirs)


def gather_kernel(step, scalars_ref, *refs):
    *block_refs, out_ref = refs
    for distance, block_ref in enumerate(block_refs):
        out_ref[lax.div(scalars_ref[2], step) ^ distance] = block_ref[...]


def gather_blocks(scalars, blocks, step):
    return pl.pallas_call(
        lambda *refs: gather_kernel(step, *refs),
        in_specs=[IN_SMEM] + [IN_VMEM] * len(blocks),
        out_specs=IN_VMEM,
        out_shape=jax.ShapeDtypeStruct((len(blocks), *blocks[0].shape), blocks[0].dtype),
        compiler_params=pltpu.CompilerParams(vmem_limit_bytes=4 * MIB),
        name="gather_blocks",
    )(scalars, *blocks)


def mlp_kernel(scalars_ref, *refs):
    group = scalars_ref[3]
    *refs, hidden_ref, out_ref, loaded = refs
    count = (len(refs) - 10) // 2
    blocks, (in_ref, out_hbm), rest = refs[:count], refs[count : count + 2], refs[count + 2 :]
    load = pltpu.make_async_copy(out_hbm, out_ref, loaded)
    load.start()
    in_parts, out_parts, shares = rest[:4], rest[4:8], rest[8:]
    rows = jnp.concatenate([block[...] for block in blocks])
    depth, units = in_parts[0].shape[0], out_parts[0].shape[0]

    def hidden_of(total):
        return jax.nn.gelu(total, approximate=True).astype(jnp.bfloat16)

    hidden = hidden_of(jnp.dot(rows, in_ref[...], preferred_element_type=jnp.float32))
    quarters = [group, group ^ 2, group ^ 1, group ^ 3]
    total = 0.0
    for quarter, part in zip(quarters, in_parts):
        span = pl.ds(pl.multiple_of(quarter * depth, depth), depth)
        piece = jnp.concatenate([block[:, span] for block in blocks])
        total += jnp.dot(piece, part[...], preferred_element_type=jnp.float32)
    hidden_ref[...] = hidden_of(total)
    load.wait()
    share = jnp.dot(hidden, out_ref[...], preferred_element_type=jnp.float32)
    for quarter, part in zip(quarters, out_parts):
        span = pl.ds(pl.multiple_of(quarter * units, units), units)
        share += jnp.dot(hidden_ref[:, span], part[...], preferred_element_type=jnp.float32)
    each = blocks[0].shape[0]
    for index, target in enumerate(shares):
        target[...] = share[index * each : (index + 1) * each].astype(target.dtype)


def mlp_shares(scalars, blocks, mlp_in, mlp_out, in_parts, out_parts):
    first = jax.ShapeDtypeStruct(blocks[0].shape, jnp.float32)
    other = jax.ShapeDtypeStruct(blocks[0].shape, jnp.bfloat16)
    operands = [*blocks, mlp_in, in_hbm(mlp_out), *in_parts, *out_parts]
    return pl.pallas_call(
        mlp_kernel,
        in_specs=[IN_SMEM]
        + [IN_VMEM] * (len(blocks) + 1)
        + [ANYWHERE]
        + [IN_VMEM] * (len(operands) - len(blocks) - 2),
        out_specs=[IN_VMEM] * len(blocks),
        out_shape=[first] + [other] * (len(blocks) - 1),
        scratch_shapes=[
            pltpu.VMEM((len(blocks) * blocks[0].shape[0], mlp_in.shape[1]), jnp.bfloat16),
            pltpu.VMEM(mlp_out.shape, jnp.bfloat16),
            pltpu.SemaphoreType.DMA(()),
        ],
        cost_estimate=pl.CostEstimate(
            flops=8 * len(blocks) * blocks[0].size * mlp_in.shape[1],
            bytes_accessed=8 * mlp_in.size,
            transcendentals=0,
        ),
        compiler_params=pltpu.CompilerParams(vmem_limit_bytes=16 * MIB),
        name="mlp_shares",
    )(scalars, *operands)


def paired_device(
    token_ids,
    latent_offset,
    embed_table,
    cross_q,
    cross_kv,
    cross_out,
    self_qkv,
    self_out,
    mlp_in,
    mlp_out,
):
    owners = lax.axis_size("ctx")
    groups = lax.axis_size("lat")
    place = lax.axis_index("ctx")
    group = lax.axis_index("lat")
    core = group % 2
    duo = group // 2
    duos = groups // 2
    offset = latent_offset[0]
    block = token_ids.shape[0]
    width = embed_table.shape[1]
    share = cross_q.shape[0]
    group_rows = LATENTS // groups
    rows = group_rows // owners
    duo_rows = duos * rows
    scalars = jnp.stack([core, duo, place, group, offset]).astype(jnp.int32)

    def swap(value):
        return lax.ppermute(value, "lat", [(i, i ^ 1) for i in range(groups)])

    def cross(value):
        return lax.ppermute(value, "lat", [(i, i ^ 2) for i in range(groups)])

    def exchange(value):
        return lax.all_to_all(value, "ctx", 0, 0, tiled=True)

    distances = [2 * i for i in range(1, owners // 2)]

    def across(value, distance):
        return lax.ppermute(value, "ctx", [(i, i ^ distance) for i in range(owners)])

    def quarter(matrix):
        size = matrix.shape[0] // groups
        return lax.dynamic_slice_in_dim(matrix, group * size, size, 0)

    mine, theirs, in_part = prepare_weights(scalars, cross_q, cross_kv, mlp_in, groups)
    blocks = order_blocks(scalars, mine, swap(theirs))

    lanes = token_ids.reshape(1, block // HD, HD)
    lanes_other = across(lanes, 1)
    even = place % 2 == 0
    lanes = jnp.concatenate(
        [jnp.where(even, lanes, lanes_other), jnp.where(even, lanes_other, lanes)]
    )
    pair_lanes = [lanes]
    for distance in distances:
        pair_lanes.append(across(lanes, distance))
    every_token = gather_blocks(scalars, pair_lanes, 2).reshape(owners, block)
    arrived = [blocks[0]]
    for distance in range(1, owners):
        arrived.append(across(blocks[distance], distance))

    step = FINE * FINE
    latent_starts = (2 * jnp.arange(duos, dtype=jnp.int32) + core) * group_rows
    pieces = block // step
    half_blocks = owners // 2
    token_blocks = every_token.reshape(half_blocks, 2, block)
    own_ids = lax.dynamic_index_in_dim(token_blocks, core, 1, keepdims=False)
    flat_tokens = every_token.reshape(owners * block)
    latent_ids = jnp.stack(
        [
            lax.dynamic_slice_in_dim(
                flat_tokens, offset + (2 * i + core) * group_rows, group_rows, 0
            )
            for i in range(duos)
        ]
    )
    fetched = []
    for part in (in_part, None):
        one = across(quarter(mlp_out) if part is None else part, 1)
        two = cross(one)
        three = swap(one)
        four = swap(two)
        fetched.append((one, two, three, four))

    block_starts = (2 * jnp.arange(half_blocks, dtype=jnp.int32) + core) * block
    inner = jnp.arange(pieces, dtype=jnp.int32) * step
    latent_inner = jnp.arange(group_rows // step, dtype=jnp.int32) * step
    starts = jnp.concatenate(
        [
            (block_starts[:, None] + inner[None, :]).reshape(-1),
            (offset + latent_starts[:, None] + latent_inner[None, :]).reshape(-1),
        ]
    )
    tables = sinusoid_tables(starts, width)
    tiles = half_blocks * pieces
    context = context_rows(own_ids.reshape(-1, step), 0, tables, embed_table, owners)
    latent = context_rows(latent_ids.reshape(-1, step), tiles, tables, embed_table, owners)
    arrived = gather_blocks(scalars, arrived, 1)
    arrived_other = swap(arrived)
    pairs, queries, own_latent = context_heads(
        scalars, context, latent, arrived, arrived_other, (owners, duos, rows)
    )
    other_pairs = swap(pairs)
    by_block = (1, half_blocks, block, 2 * HD)
    attended = head_attention(
        scalars, queries, pairs.reshape(by_block), other_pairs.reshape(by_block), True, block
    )

    def project(base, attended, mine, theirs):
        heads = exchange(attended.reshape(owners, duo_rows, HD))
        kept, given = project_rows(scalars, heads, mine, theirs)
        came = cross(given)
        return add_norm(base, kept, came)

    first_stream, normed = project(own_latent, attended, cross_out, swap(cross_out))
    normed_other = cross(normed)
    self_qkv_other = swap(self_qkv)
    triples = exchange(triple_heads(scalars, normed, normed_other, self_qkv, self_qkv_other))
    triples = triples.reshape(owners, duos, rows, 3 * HD)
    self_attended = head_attention(
        scalars, triples, triples, swap(triples), False, group_rows
    )
    second_stream, mlp_normed = project(
        first_stream, self_attended, self_out, swap(self_out)
    )

    blocks = [mlp_normed]
    for distance in distances:
        blocks.append(across(mlp_normed, distance))
    kept, *given = mlp_shares(scalars, blocks, mlp_in, mlp_out, *fetched)
    result = second_stream + kept
    for share, distance in zip(given, distances):
        came = across(share, distance)
        result = result + came.astype(jnp.float32)
    return result.astype(jnp.bfloat16)[None]


def solution(mesh):
    placed = (
        P("ctx"),
        P(),
        P(),
        P("ctx", "lat"),
        P(None, "ctx", "lat"),
        P("lat", None),
        P(None, None, "lat"),
        P("lat", None),
        P(None, "ctx"),
        P("ctx", None),
    )

    def per_device(*arguments):
        owners, groups = lax.axis_size("ctx"), lax.axis_size("lat")
        local_heads = arguments[3].shape[1] // HD
        paired = groups == 4 and owners == 2 * local_heads and owners & (owners - 1) == 0
        return (paired_device if paired else general_device)(*arguments)

    return jax.shard_map(
        per_device, mesh=mesh, in_specs=placed, out_specs=P("lat", "ctx", None), check_vma=False
    )
```

```python
import math

import jax
import jax.numpy as jnp
from jax import lax
from jax.experimental import pallas as pl
from jax.experimental.pallas import tpu as pltpu
from jax.sharding import PartitionSpec as P

HD = 128
LATENTS = 1024


EPSILON = 1e-06
MASKED = -1e30


def rms_normalize(values):
    return values * lax.rsqrt(jnp.mean(values * values, axis=-1, keepdims=True) + EPSILON)


def sinusoid(places, width):
    index = jnp.arange(width // 2).astype(jnp.float32)
    rates = jnp.exp(index * (-2.0 * math.log(10000.0) / width))
    angles = places.astype(jnp.float32)[:, None] * rates[None, :]
    return jnp.stack([jnp.sin(angles), jnp.cos(angles)], axis=-1).reshape(places.shape[0], width)


def embed_rows(token_rows, table, places):
    vocab_range = jnp.arange(table.shape[0], dtype=jnp.int32)
    one_hot = (token_rows[:, None] == vocab_range[None, :]).astype(jnp.bfloat16)
    looked = jnp.dot(one_hot, table, preferred_element_type=jnp.float32)
    return rms_normalize(looked + sinusoid(places, table.shape[1])).astype(jnp.bfloat16)


def block_attention(queries, keys, values, blocked, head_size):
    scale = 1.0 / math.sqrt(head_size)
    head_count = queries.shape[1] // head_size
    query_rows = queries.shape[0]
    key_rows = keys.shape[0]
    query_heads = jnp.transpose(queries.reshape(query_rows, head_count, head_size), (1, 0, 2))
    key_heads = jnp.transpose(keys.reshape(key_rows, head_count, head_size), (1, 0, 2))
    value_heads = jnp.transpose(values.reshape(key_rows, head_count, head_size), (1, 0, 2))

    def one_head(operands):
        query, key, value = operands
        scores = (
            lax.dot_general(
                query, key, (((1,), (1,)), ((), ())), preferred_element_type=jnp.float32
            )
            * scale
        )
        scores = jnp.where(blocked, MASKED, scores)
        peak = jnp.max(scores, axis=1)
        weights = jnp.exp(scores - peak[:, None]).astype(jnp.bfloat16)
        total = jnp.sum(weights.astype(jnp.float32), axis=1)
        output = jnp.dot(weights, value, preferred_element_type=jnp.float32)
        return (peak, total, output)

    maxima, totals, outputs = lax.map(one_head, (query_heads, key_heads, value_heads))
    merged = jnp.transpose(outputs, (1, 0, 2)).reshape(query_rows, head_count * head_size)
    return (jnp.transpose(maxima), jnp.transpose(totals), merged)


def general_device(
    token_ids,
    latent_offset,
    embed_table,
    cross_q,
    cross_kv,
    cross_out,
    self_qkv,
    self_out,
    mlp_in,
    mlp_out,
):
    context_count = lax.axis_size("ctx")
    group_count = lax.axis_size("lat")
    context_index = lax.axis_index("ctx")
    group_index = lax.axis_index("lat")
    block_length = token_ids.shape[0]
    head_size = HD
    local_width = cross_q.shape[1]
    local_heads = local_width // head_size
    width = embed_table.shape[1]
    offset = latent_offset[0]
    latent_count = LATENTS
    row_count = latent_count // context_count
    group_rows = latent_count // group_count
    places = context_index * block_length + jnp.arange(block_length, dtype=jnp.int32)
    context = embed_rows(token_ids, embed_table, places)
    piece = lax.all_gather(cross_kv, "ctx", axis=1, tiled=True)
    columns = context
    key_sum = jnp.dot(columns, piece[0], preferred_element_type=jnp.float32)
    value_sum = jnp.dot(columns, piece[1], preferred_element_type=jnp.float32)
    keys = key_sum.astype(jnp.bfloat16)
    values = value_sum.astype(jnp.bfloat16)
    every_token = lax.all_gather(token_ids, "ctx", axis=0, tiled=True)
    latent_tokens = lax.dynamic_slice_in_dim(every_token, offset, latent_count, 0)
    latent_places = offset + jnp.arange(latent_count, dtype=jnp.int32)
    latent = embed_rows(latent_tokens, embed_table, latent_places)
    columns = latent
    query_sum = jnp.dot(
        columns,
        lax.all_gather(cross_q, "ctx", axis=0, tiled=True),
        preferred_element_type=jnp.float32,
    )
    queries = query_sum.astype(jnp.bfloat16)
    blocked = places[None, :] > latent_places[:, None]
    maxima, totals, outputs = block_attention(queries, keys, values, blocked, head_size)
    row_start = context_index * row_count
    came_max, came_total, came_out = (
        lax.all_to_all(maxima[:, None, :], "ctx", split_axis=0, concat_axis=1, tiled=True),
        lax.all_to_all(totals[:, None, :], "ctx", split_axis=0, concat_axis=1, tiled=True),
        lax.all_to_all(outputs[:, None, :], "ctx", split_axis=0, concat_axis=1, tiled=True),
    )
    peak = jnp.max(came_max, axis=1, keepdims=True)
    factor = jnp.exp(came_max - peak)
    own_totals = jnp.sum(came_total * factor, axis=1)
    spread = (
        came_out.reshape(row_count, context_count, local_heads, head_size) * factor[:, :, :, None]
    )
    own_outputs = jnp.sum(spread, axis=1).reshape(row_count, local_width)
    attended = (own_outputs / jnp.repeat(own_totals, head_size, axis=1)).astype(jnp.bfloat16)
    own_latent = lax.dynamic_slice_in_dim(latent, row_start, row_count, 0).astype(jnp.float32)
    first_stream = own_latent + lax.psum(
        jnp.dot(attended, cross_out, preferred_element_type=jnp.float32), "lat"
    )
    self_normed = rms_normalize(first_stream).astype(jnp.bfloat16)
    self_queries = jnp.dot(self_normed, self_qkv[0], preferred_element_type=jnp.float32).astype(
        jnp.bfloat16
    )
    self_keys = jnp.dot(self_normed, self_qkv[1], preferred_element_type=jnp.float32).astype(
        jnp.bfloat16
    )
    self_values = jnp.dot(self_normed, self_qkv[2], preferred_element_type=jnp.float32).astype(
        jnp.bfloat16
    )
    all_keys, all_values = (
        lax.all_gather(self_keys, "ctx", axis=0, tiled=True),
        lax.all_gather(self_values, "ctx", axis=0, tiled=True),
    )
    own_places = row_start + jnp.arange(row_count, dtype=jnp.int32)
    later = jnp.arange(latent_count, dtype=jnp.int32)[None, :] > own_places[:, None]
    _, self_totals, self_outputs = block_attention(
        self_queries, all_keys, all_values, later, head_size
    )
    self_attended = (self_outputs / jnp.repeat(self_totals, head_size, axis=1)).astype(jnp.bfloat16)
    second_stream = first_stream + lax.psum(
        jnp.dot(self_attended, self_out, preferred_element_type=jnp.float32).astype(jnp.bfloat16),
        "lat",
    ).astype(jnp.float32)
    mlp_normed = rms_normalize(second_stream).astype(jnp.bfloat16)
    gathered = lax.all_gather(mlp_normed, "ctx", axis=0, tiled=True)
    group_input = lax.dynamic_slice_in_dim(gathered, group_index * group_rows, group_rows, 0)
    pre_hidden = jnp.dot(group_input, mlp_in, preferred_element_type=jnp.float32)
    hidden = jax.nn.gelu(pre_hidden, approximate=True).astype(jnp.bfloat16)
    place = context_index * row_count - group_index * group_rows
    inside = jnp.logical_and(place >= 0, place < group_rows)
    residual = jnp.zeros((group_rows, width), jnp.float32)
    residual = lax.dynamic_update_slice_in_dim(
        residual, second_stream, jnp.clip(place, 0, group_rows - row_count), 0
    )
    residual = jnp.where(inside, residual, 0.0)
    result = lax.psum_scatter(
        jnp.dot(hidden, mlp_out, preferred_element_type=jnp.float32) + residual,
        "ctx",
        scatter_dimension=0,
        tiled=True,
    )
    return result.astype(jnp.bfloat16)[None]


FINE = 16
MIB = 1 << 20


def rate_row(width):
    index = (jnp.arange(width, dtype=jnp.int32) // 2).astype(jnp.float32)
    return jnp.exp(index * (-2.0 * math.log(10000.0) / width))


def context_kernel(
    halves, first, ids_ref, sine_ref, cosine_ref, high_cos_ref, high_sin_ref, low_cos_ref,
    low_sin_ref, table_ref, out_ref, cos_ref, sin_ref,
):
    tile = pl.program_id(0)

    @pl.when(tile == 0)
    def _():
        low_cos, low_sin = low_cos_ref[...], low_sin_ref[...]
        for step in range(FINE):
            high_cos, high_sin = high_cos_ref[step : step + 1], high_sin_ref[step : step + 1]
            rows = pl.ds(step * FINE, FINE)
            cos_ref[rows, :] = high_cos * low_cos - high_sin * low_sin
            sin_ref[rows, :] = high_sin * low_cos + high_cos * low_sin

    vocab, width = table_ref.shape
    rows = out_ref.shape[0]
    one_hot = (
        lax.broadcasted_iota(jnp.int32, (vocab, rows), 0) == ids_ref[0]
    ).astype(jnp.float32).astype(jnp.bfloat16)
    looked = lax.dot_general(
        one_hot, table_ref[...], (((0,), (0,)), ((), ())), preferred_element_type=jnp.float32
    )
    start = pl.ds(first + tile, 1)
    total = looked + sine_ref[start, :] * cos_ref[...] + cosine_ref[start, :] * sin_ref[...]
    power = jnp.mean(total * total, axis=1, keepdims=True)
    normed = (total * lax.rsqrt(power + EPSILON)).astype(jnp.bfloat16)
    part = width // (2 * halves)
    for half in range(2):
        for owner in range(halves):
            source = (owner * 2 + half) * part
            target = (half * halves + owner) * part
            out_ref[:, target : target + part] = normed[:, source : source + part]


def sinusoid_tables(starts, width):
    rates = rate_row(width)
    odd = (jnp.arange(width, dtype=jnp.int32) % 2)[None, :] == 1
    places = jnp.pad(starts, (0, -starts.shape[0] % FINE)).astype(jnp.float32)
    angles = places[:, None] * rates[None, :]
    sines, cosines = jnp.sin(angles), jnp.cos(angles)
    steps = jnp.arange(FINE, dtype=jnp.float32)
    high = (steps * FINE)[:, None] * rates[None, :]
    low = steps[:, None] * rates[None, :]
    return (
        jnp.where(odd, cosines, sines),
        jnp.where(odd, -sines, cosines),
        jnp.cos(high),
        jnp.sin(high),
        jnp.cos(low),
        jnp.sin(low),
    )


def context_rows(ids, first, tables, table, owners):
    count, rows = ids.shape[0], FINE * FINE
    width = table.shape[1]
    return pl.pallas_call(
        lambda *refs: context_kernel(owners, first, *refs),
        grid=(count,),
        in_specs=[pl.BlockSpec((1, 1, rows), lambda i: (i, 0, 0))]
        + [pl.BlockSpec(array.shape, lambda i: (0, 0)) for array in (*tables, table)],
        out_specs=pl.BlockSpec((rows, width), lambda i: (i, 0)),
        out_shape=jax.ShapeDtypeStruct((count * rows, width), jnp.bfloat16),
        scratch_shapes=[pltpu.VMEM((rows, width), jnp.float32)] * 2,
        cost_estimate=pl.CostEstimate(
            flops=count * rows * width * table.shape[0] * 2,
            bytes_accessed=count * rows * width * 2,
            transcendentals=0,
        ),
        compiler_params=pltpu.CompilerParams(vmem_limit_bytes=20 * MIB),
        name="context_rows",
    )(ids[:, None, :], *tables, table)


def attention_kernel(key_tile, shifted, scalars_ref, query_ref, own_ref, other_ref, out_ref):
    tile, core = pl.program_id(0), scalars_ref[0]
    offset = scalars_ref[4] if shifted else 0
    parts, rows, size = query_ref.shape
    query = query_ref[...].reshape(parts * rows, size)
    rows = parts * rows
    query_place = (
        offset + (2 * tile + core) * rows + lax.broadcasted_iota(jnp.int32, (rows, 1), 0)
    )
    peak = jnp.full((rows, 1), MASKED, jnp.float32)
    output = jnp.zeros((rows, 2 * size), jnp.float32)
    outer, blocks, inner, columns = own_ref.shape
    keys = outer * inner
    for side, ref in enumerate((own_ref, other_ref)):
        for block in range(blocks):
            pair = ref[:, block, :, columns - 2 * size :].reshape(keys, 2 * size)
            for part in range(keys // key_tile):
                span = slice(part * key_tile, (part + 1) * key_tile)
                key, value = pair[span, :size], pair[span, size:]
                scores = lax.dot_general(
                    query, key, (((1,), (1,)), ((), ())), preferred_element_type=jnp.float32
                )
                key_place = (
                    (2 * block + (1 - core if side else core)) * keys
                    + part * key_tile
                    + lax.broadcasted_iota(jnp.int32, (1, key_tile), 1)
                )
                scores = jnp.where(key_place > query_place, MASKED, scores)
                new_peak = jnp.maximum(peak, jnp.max(scores, axis=1, keepdims=True))
                weights = jnp.exp(scores - new_peak).astype(jnp.bfloat16)
                output = output * jnp.exp(peak - new_peak) + jnp.dot(
                    weights,
                    jnp.concatenate([value, jnp.ones_like(value)], axis=1),
                    preferred_element_type=jnp.float32,
                )
                peak = new_peak
    final = (output[:, :size] / output[:, size:]).astype(jnp.bfloat16)
    out_ref[...] = final.reshape(out_ref.shape)


def head_attention(scalars, triples, own, other, shifted, key_tile):
    owners, tiles, rows = triples.shape[:3]
    keys = 2 * own.shape[0] * own.shape[1] * own.shape[2]
    return pl.pallas_call(
        lambda *refs: attention_kernel(key_tile, shifted, *refs),
        grid_spec=pltpu.PrefetchScalarGridSpec(
            num_scalar_prefetch=1,
            grid=(tiles,),
            in_specs=[
                pl.BlockSpec((owners, None, rows, HD), lambda i, s: (0, i, 0, 0)),
                pl.BlockSpec(own.shape, lambda i, s: (0, 0, 0, 0)),
                pl.BlockSpec(other.shape, lambda i, s: (0, 0, 0, 0)),
            ],
            out_specs=pl.BlockSpec((owners, None, rows, HD), lambda i, s: (0, i, 0, 0)),
        ),
        out_shape=jax.ShapeDtypeStruct((owners, tiles, rows, HD), jnp.bfloat16),
        cost_estimate=pl.CostEstimate(
            flops=8 * owners * tiles * rows * keys * HD,
            bytes_accessed=keys * HD * 4,
            transcendentals=owners * tiles * rows * keys,
        ),
        compiler_params=pltpu.CompilerParams(vmem_limit_bytes=14 * MIB),
        name="head_attention",
    )(scalars, triples, own, other)


def stream_kernel(
    scalars_ref, heads_ref, came_ref, base_ref, *refs,
):
    *matrix_refs, stream_ref, normed_ref, matrices, loaded = refs
    core, duo = scalars_ref[0], scalars_ref[1]
    half = heads_ref.shape[0] // 2
    loads = [
        pltpu.make_async_copy(source, matrices.at[index], loaded.at[index])
        for index, source in enumerate(matrix_refs)
    ]
    for load in loads:
        load.start()
    total = base_ref[...].astype(jnp.float32)
    sides = [(heads_ref, core), (heads_ref, 1 - core), (came_ref, core), (came_ref, 1 - core)]
    for index, (ref, side) in enumerate(sides):
        left = jnp.concatenate([ref[side * half + head] for head in range(half)], axis=1)
        loads[index].wait()
        total += jnp.dot(left, matrices[index], preferred_element_type=jnp.float32)
    rows = stream_ref.shape[0]
    stream_ref[...] = jnp.where(duo == 0, total[:rows], total[rows:])
    normed_ref[...] = rms_normalize(total).astype(jnp.bfloat16)


def stream_rows(scalars, heads, came, base, matrices):
    rows, width = base.shape
    inner = matrices[0].shape[0]
    return pl.pallas_call(
        stream_kernel,
        in_specs=[IN_SMEM] + [IN_VMEM] * 3 + [ANYWHERE] * len(matrices),
        out_specs=[IN_VMEM] * 2,
        out_shape=[
            jax.ShapeDtypeStruct((rows // 2, width), jnp.float32),
            jax.ShapeDtypeStruct((rows, width), jnp.bfloat16),
        ],
        scratch_shapes=[
            pltpu.VMEM((len(matrices), inner, width), jnp.bfloat16),
            pltpu.SemaphoreType.DMA((len(matrices),)),
        ],
        cost_estimate=pl.CostEstimate(
            flops=8 * rows * inner * width, bytes_accessed=8 * inner * width, transcendentals=0
        ),
        compiler_params=pltpu.CompilerParams(vmem_limit_bytes=20 * MIB),
        name="stream_rows",
    )(scalars, heads, came, base, *[in_hbm(matrix) for matrix in matrices])


def in_hbm(array):
    return pltpu.with_memory_space_constraint(array, pltpu.HBM)


def prepare_kernel(
    scalars_ref, query_hbm, pair_hbm, matrix_hbm, mine_ref, theirs_ref, part_ref, query_ref,
    pair_ref, loaded,
):
    core, group = scalars_ref[0], scalars_ref[3]
    heads, half, columns = mine_ref.shape
    size = columns // 3
    depth = part_ref.shape[0]
    quarter = matrix_hbm.at[pl.ds(pl.multiple_of(group * depth, depth), depth), :]
    loads = [
        pltpu.make_async_copy(query_hbm, query_ref, loaded.at[0]),
        pltpu.make_async_copy(pair_hbm, pair_ref, loaded.at[1]),
        pltpu.make_async_copy(quarter, part_ref, loaded.at[2]),
    ]
    for load in loads:
        load.start()
    loads[0].wait()
    loads[1].wait()
    for target, side in ((theirs_ref, 1 - core), (mine_ref, core)):
        rows = pl.ds(pl.multiple_of(side * half, half), half)
        for head in range(heads):
            span = slice(head * size, (head + 1) * size)
            target[head, :, 0:size] = query_ref[rows, span]
            target[head, :, size : 2 * size] = pair_ref[0, rows, span]
            target[head, :, 2 * size :] = pair_ref[1, rows, span]
    loads[2].wait()


def prepare_weights(scalars, cross_q, cross_kv, matrix, groups):
    share, columns = cross_q.shape
    shape = jax.ShapeDtypeStruct((columns // HD, share // 2, 3 * HD), jnp.bfloat16)
    part = jax.ShapeDtypeStruct((matrix.shape[0] // groups, matrix.shape[1]), jnp.bfloat16)
    return pl.pallas_call(
        prepare_kernel,
        in_specs=[IN_SMEM] + [ANYWHERE] * 3,
        out_specs=[IN_VMEM] * 3,
        out_shape=[shape, shape, part],
        scratch_shapes=[
            pltpu.VMEM(cross_q.shape, jnp.bfloat16),
            pltpu.VMEM(cross_kv.shape, jnp.bfloat16),
            pltpu.SemaphoreType.DMA((3,)),
        ],
        compiler_params=pltpu.CompilerParams(vmem_limit_bytes=8 * MIB),
        name="prepare_weights",
    )(scalars, in_hbm(cross_q), in_hbm(cross_kv), in_hbm(matrix))


def project_kernel(scalars_ref, heads_ref, mine_ref, theirs_ref, kept_ref, given_ref):
    core, duo = scalars_ref[0], scalars_ref[1]
    half = heads_ref.shape[0] // 2
    product = 0.0
    for side, matrix in ((core, mine_ref), (1 - core, theirs_ref)):
        left = jnp.concatenate([heads_ref[side * half + head] for head in range(half)], axis=1)
        product += jnp.dot(left, matrix[...], preferred_element_type=jnp.float32)
    kept_rows = kept_ref.shape[0]
    low, high = product[:kept_rows], product[kept_rows:]
    kept_ref[...] = jnp.where(duo == 0, low, high)
    given_ref[...] = jnp.where(duo == 0, high, low).astype(jnp.bfloat16)


IN_VMEM = pl.BlockSpec(memory_space=pltpu.VMEM)
IN_SMEM = pl.BlockSpec(memory_space=pltpu.SMEM)
ANYWHERE = pl.BlockSpec(memory_space=pl.ANY)


def project_rows(scalars, heads, mine, theirs):
    _, rows, _ = heads.shape
    inner, width = mine.shape
    return pl.pallas_call(
        project_kernel,
        in_specs=[IN_SMEM, IN_VMEM, IN_VMEM, IN_VMEM],
        out_specs=[IN_VMEM, IN_VMEM],
        out_shape=[
            jax.ShapeDtypeStruct((rows // 2, width), jnp.float32),
            jax.ShapeDtypeStruct((rows // 2, width), jnp.bfloat16),
        ],
        cost_estimate=pl.CostEstimate(
            flops=4 * rows * inner * width, bytes_accessed=4 * inner * width, transcendentals=0
        ),
        compiler_params=pltpu.CompilerParams(vmem_limit_bytes=8 * MIB),
        name="project_rows",
    )(scalars, heads, mine, theirs)


def triple_kernel(scale, scalars_ref, rows_ref, mine_hbm, theirs_hbm, out_ref, matrices, loaded):
    core = scalars_ref[0]
    heads = out_ref.shape[0] // 2
    kinds = mine_hbm.shape[0]
    loads = [
        pltpu.make_async_copy(source.at[kind], matrices.at[base + kind], loaded.at[base + kind])
        for base, source in ((0, mine_hbm), (kinds, theirs_hbm))
        for kind in range(kinds)
    ]
    ahead = 3
    for load in loads[:ahead]:
        load.start()
    rows = rows_ref[...]
    for index, load in enumerate(loads):
        load.wait()
        for later in loads[index + ahead : index + ahead + 1]:
            later.start()
        kind = index % kinds
        side = core if index < kinds else 1 - core
        product = jnp.dot(rows, matrices[index], preferred_element_type=jnp.float32)
        product = (product * (scale if kind == 0 else 1.0)).astype(jnp.bfloat16)
        for head in range(heads):
            out_ref[side * heads + head, :, kind * HD : (kind + 1) * HD] = product[
                :, head * HD : (head + 1) * HD
            ]


def triple_heads(scalars, rows, mine, theirs):
    count = rows.shape[0]
    kinds, inner, columns = mine.shape
    heads = columns // HD
    return pl.pallas_call(
        lambda *refs: triple_kernel(HD**-0.5, *refs),
        in_specs=[IN_SMEM, IN_VMEM, ANYWHERE, ANYWHERE],
        out_specs=IN_VMEM,
        out_shape=jax.ShapeDtypeStruct((2 * heads, count, kinds * HD), jnp.bfloat16),
        scratch_shapes=[
            pltpu.VMEM((2 * kinds, inner, columns), jnp.bfloat16),
            pltpu.SemaphoreType.DMA((2 * kinds,)),
        ],
        cost_estimate=pl.CostEstimate(
            flops=4 * kinds * count * inner * columns,
            bytes_accessed=4 * kinds * inner * columns,
            transcendentals=0,
        ),
        compiler_params=pltpu.CompilerParams(vmem_limit_bytes=20 * MIB),
        name="triple_heads",
    )(scalars, rows, in_hbm(mine), in_hbm(theirs))


def add_norm_kernel(base_ref, kept_ref, came_ref, stream_ref, normed_ref):
    total = base_ref[...].astype(jnp.float32) + (
        kept_ref[...] + came_ref[...].astype(jnp.float32)
    )
    stream_ref[...] = total
    normed_ref[...] = rms_normalize(total).astype(jnp.bfloat16)


def add_norm(base, kept, came):
    return pl.pallas_call(
        add_norm_kernel,
        in_specs=[IN_VMEM] * 3,
        out_specs=[IN_VMEM] * 2,
        out_shape=[
            jax.ShapeDtypeStruct(kept.shape, jnp.float32),
            jax.ShapeDtypeStruct(kept.shape, jnp.bfloat16),
        ],
        compiler_params=pltpu.CompilerParams(vmem_limit_bytes=4 * MIB),
        name="add_norm",
    )(base, kept, came)


def context_heads_kernel(
    scale, scalars_ref, context_ref, rows_ref, mine_ref, theirs_ref, pair_ref, query_ref,
    latent_ref, weights_ref,
):
    core, place = scalars_ref[0], scalars_ref[2]
    _, part, columns = mine_ref.shape
    owners, tiles, rows, size = query_ref.shape
    inner = owners * part
    keys = pair_ref.shape[0]
    tile = owners * rows
    for side, ref in ((core, mine_ref), (1 - core, theirs_ref)):
        span = pl.ds(pl.multiple_of(side * inner, inner), inner)
        weights_ref[span, :] = ref[...].reshape(inner, columns)

    def product(left, columns):
        return jnp.dot(left, weights_ref[:, columns], preferred_element_type=jnp.float32)

    for start in range(0, keys, tile):
        span = slice(start, start + tile)
        pair_ref[span, :] = product(context_ref[span, :], slice(size, 3 * size)).astype(
            jnp.bfloat16
        )
    for index in range(tiles):
        left = rows_ref[index * tile : (index + 1) * tile, :]
        query = (product(left, slice(0, size)) * scale).astype(jnp.bfloat16)
        query_ref[:, index] = query.reshape(owners, rows, size)
    for index in range(tiles):
        start = pl.multiple_of(index * tile + place * rows, rows)
        latent = rows_ref[pl.ds(start, rows), :]
        for half in range(2):
            for owner in range(owners):
                source = half * inner + owner * part
                target = (owner * 2 + half) * part
                latent_ref[index * rows : (index + 1) * rows, target : target + part] = latent[
                    :, source : source + part
                ]


def context_heads(scalars, context, latent, mine, theirs, shape):
    owners, tiles, rows = shape
    keys, width = context.shape
    size = mine.shape[2] // 3
    return pl.pallas_call(
        lambda *refs: context_heads_kernel(size**-0.5, *refs),
        in_specs=[IN_SMEM] + [IN_VMEM] * 4,
        out_specs=[IN_VMEM] * 3,
        out_shape=[
            jax.ShapeDtypeStruct((keys, 2 * size), jnp.bfloat16),
            jax.ShapeDtypeStruct((owners, tiles, rows, size), jnp.bfloat16),
            jax.ShapeDtypeStruct((tiles * rows, width), jnp.bfloat16),
        ],
        scratch_shapes=[pltpu.VMEM((width, 3 * size), jnp.bfloat16)],
        cost_estimate=pl.CostEstimate(
            flops=4 * (keys + owners * tiles * rows) * width * size,
            bytes_accessed=keys * width * 2,
            transcendentals=0,
        ),
        compiler_params=pltpu.CompilerParams(vmem_limit_bytes=12 * MIB),
        name="context_heads",
    )(scalars, context, latent, mine, theirs)


def order_kernel(scalars_ref, mine_ref, theirs_ref, *block_refs):
    core, place = scalars_ref[0], scalars_ref[2]
    heads = mine_ref.shape[0]
    for distance, block_ref in enumerate(block_refs):
        head = place ^ distance
        local = lax.rem(head, heads)
        own = lax.div(head, heads) == core

        @pl.when(own)
        def _():
            block_ref[...] = mine_ref[local]

        @pl.when(jnp.logical_not(own))
        def _():
            block_ref[...] = theirs_ref[local]


def order_blocks(scalars, mine, theirs):
    heads, rows, columns = mine.shape
    return pl.pallas_call(
        order_kernel,
        in_specs=[IN_SMEM, IN_VMEM, IN_VMEM],
        out_specs=[IN_VMEM] * (2 * heads),
        out_shape=[jax.ShapeDtypeStruct((rows, columns), jnp.bfloat16)] * (2 * heads),
        compiler_params=pltpu.CompilerParams(vmem_limit_bytes=4 * MIB),
        name="order_blocks",
    )(scalars, mine, theirs)


def gather_kernel(step, scalars_ref, *refs):
    *block_refs, out_ref = refs
    for distance, block_ref in enumerate(block_refs):
        out_ref[lax.div(scalars_ref[2], step) ^ distance] = block_ref[...]


def gather_blocks(scalars, blocks, step):
    return pl.pallas_call(
        lambda *refs: gather_kernel(step, *refs),
        in_specs=[IN_SMEM] + [IN_VMEM] * len(blocks),
        out_specs=IN_VMEM,
        out_shape=jax.ShapeDtypeStruct((len(blocks), *blocks[0].shape), blocks[0].dtype),
        compiler_params=pltpu.CompilerParams(vmem_limit_bytes=4 * MIB),
        name="gather_blocks",
    )(scalars, *blocks)


def mlp_kernel(scalars_ref, *refs):
    group = scalars_ref[3]
    *refs, hidden_ref, out_ref, loaded = refs
    count = (len(refs) - 10) // 2
    blocks, (in_ref, out_hbm), rest = refs[:count], refs[count : count + 2], refs[count + 2 :]
    load = pltpu.make_async_copy(out_hbm, out_ref, loaded)
    load.start()
    in_parts, out_parts, shares = rest[:4], rest[4:8], rest[8:]
    rows = jnp.concatenate([block[...] for block in blocks])
    depth, units = in_parts[0].shape[0], out_parts[0].shape[0]

    def hidden_of(total):
        return jax.nn.gelu(total, approximate=True).astype(jnp.bfloat16)

    hidden = hidden_of(jnp.dot(rows, in_ref[...], preferred_element_type=jnp.float32))
    quarters = [group, group ^ 2, group ^ 1, group ^ 3]
    total = 0.0
    for quarter, part in zip(quarters, in_parts):
        span = pl.ds(pl.multiple_of(quarter * depth, depth), depth)
        piece = jnp.concatenate([block[:, span] for block in blocks])
        total += jnp.dot(piece, part[...], preferred_element_type=jnp.float32)
    hidden_ref[...] = hidden_of(total)
    load.wait()
    share = jnp.dot(hidden, out_ref[...], preferred_element_type=jnp.float32)
    for quarter, part in zip(quarters, out_parts):
        span = pl.ds(pl.multiple_of(quarter * units, units), units)
        share += jnp.dot(hidden_ref[:, span], part[...], preferred_element_type=jnp.float32)
    each = blocks[0].shape[0]
    for index, target in enumerate(shares):
        target[...] = share[index * each : (index + 1) * each].astype(target.dtype)


def mlp_shares(scalars, blocks, mlp_in, mlp_out, in_parts, out_parts):
    first = jax.ShapeDtypeStruct(blocks[0].shape, jnp.float32)
    other = jax.ShapeDtypeStruct(blocks[0].shape, jnp.bfloat16)
    operands = [*blocks, mlp_in, in_hbm(mlp_out), *in_parts, *out_parts]
    return pl.pallas_call(
        mlp_kernel,
        in_specs=[IN_SMEM]
        + [IN_VMEM] * (len(blocks) + 1)
        + [ANYWHERE]
        + [IN_VMEM] * (len(operands) - len(blocks) - 2),
        out_specs=[IN_VMEM] * len(blocks),
        out_shape=[first] + [other] * (len(blocks) - 1),
        scratch_shapes=[
            pltpu.VMEM((len(blocks) * blocks[0].shape[0], mlp_in.shape[1]), jnp.bfloat16),
            pltpu.VMEM(mlp_out.shape, jnp.bfloat16),
            pltpu.SemaphoreType.DMA(()),
        ],
        cost_estimate=pl.CostEstimate(
            flops=8 * len(blocks) * blocks[0].size * mlp_in.shape[1],
            bytes_accessed=8 * mlp_in.size,
            transcendentals=0,
        ),
        compiler_params=pltpu.CompilerParams(vmem_limit_bytes=16 * MIB),
        name="mlp_shares",
    )(scalars, *operands)


def paired_device(
    token_ids,
    latent_offset,
    embed_table,
    cross_q,
    cross_kv,
    cross_out,
    self_qkv,
    self_out,
    mlp_in,
    mlp_out,
):
    owners = lax.axis_size("ctx")
    groups = lax.axis_size("lat")
    place = lax.axis_index("ctx")
    group = lax.axis_index("lat")
    core = group % 2
    duo = group // 2
    duos = groups // 2
    offset = latent_offset[0]
    block = token_ids.shape[0]
    width = embed_table.shape[1]
    share = cross_q.shape[0]
    group_rows = LATENTS // groups
    rows = group_rows // owners
    duo_rows = duos * rows
    scalars = jnp.stack([core, duo, place, group, offset]).astype(jnp.int32)

    def swap(value):
        return lax.ppermute(value, "lat", [(i, i ^ 1) for i in range(groups)])

    def cross(value):
        return lax.ppermute(value, "lat", [(i, i ^ 2) for i in range(groups)])

    def exchange(value):
        return lax.all_to_all(value, "ctx", 0, 0, tiled=True)

    distances = [2 * i for i in range(1, owners // 2)]

    def across(value, distance):
        return lax.ppermute(value, "ctx", [(i, i ^ distance) for i in range(owners)])

    def quarter(matrix):
        size = matrix.shape[0] // groups
        return lax.dynamic_slice_in_dim(matrix, group * size, size, 0)

    mine, theirs, in_part = prepare_weights(scalars, cross_q, cross_kv, mlp_in, groups)
    blocks = order_blocks(scalars, mine, swap(theirs))

    lanes = token_ids.reshape(1, block // HD, HD)
    lanes_other = across(lanes, 1)
    even = place % 2 == 0
    lanes = jnp.concatenate(
        [jnp.where(even, lanes, lanes_other), jnp.where(even, lanes_other, lanes)]
    )
    pair_lanes = [lanes]
    for distance in distances:
        pair_lanes.append(across(lanes, distance))
    every_token = gather_blocks(scalars, pair_lanes, 2).reshape(owners, block)
    arrived = [blocks[0]]
    for distance in range(1, owners):
        arrived.append(across(blocks[distance], distance))

    step = FINE * FINE
    latent_starts = (2 * jnp.arange(duos, dtype=jnp.int32) + core) * group_rows
    pieces = block // step
    half_blocks = owners // 2
    token_blocks = every_token.reshape(half_blocks, 2, block)
    own_ids = lax.dynamic_index_in_dim(token_blocks, core, 1, keepdims=False)
    flat_tokens = every_token.reshape(owners * block)
    latent_ids = jnp.stack(
        [
            lax.dynamic_slice_in_dim(
                flat_tokens, offset + (2 * i + core) * group_rows, group_rows, 0
            )
            for i in range(duos)
        ]
    )
    fetched = []
    for part in (in_part, None):
        one = across(quarter(mlp_out) if part is None else part, 1)
        two = cross(one)
        three = swap(one)
        four = swap(two)
        fetched.append((one, two, three, four))

    block_starts = (2 * jnp.arange(half_blocks, dtype=jnp.int32) + core) * block
    inner = jnp.arange(pieces, dtype=jnp.int32) * step
    latent_inner = jnp.arange(group_rows // step, dtype=jnp.int32) * step
    starts = jnp.concatenate(
        [
            (block_starts[:, None] + inner[None, :]).reshape(-1),
            (offset + latent_starts[:, None] + latent_inner[None, :]).reshape(-1),
        ]
    )
    tables = sinusoid_tables(starts, width)
    tiles = half_blocks * pieces
    context = context_rows(own_ids.reshape(-1, step), 0, tables, embed_table, owners)
    latent = context_rows(latent_ids.reshape(-1, step), tiles, tables, embed_table, owners)
    arrived = gather_blocks(scalars, arrived, 1)
    arrived_other = swap(arrived)
    pairs, queries, kept_latent = context_heads(
        scalars, context, latent, arrived, arrived_other, (owners, duos, rows)
    )
    other_pairs = swap(pairs)
    by_block = (1, half_blocks, block, 2 * HD)
    attended = head_attention(
        scalars, queries, pairs.reshape(by_block), other_pairs.reshape(by_block), True, block
    )

    def project(base, attended, mine, theirs):
        heads = exchange(attended.reshape(owners, duo_rows, HD))
        kept, given = project_rows(scalars, heads, mine, theirs)
        came = cross(given)
        return add_norm(base, kept, came)

    cross_out_duo = cross(cross_out)
    cross_out_other = swap(cross_out)
    cross_out_duo_other = swap(cross_out_duo)
    cross_heads = exchange(attended.reshape(owners, duo_rows, HD))
    cross_heads_duo = cross(cross_heads)
    first_stream, normed = stream_rows(
        scalars,
        cross_heads,
        cross_heads_duo,
        kept_latent,
        (cross_out, cross_out_other, cross_out_duo, cross_out_duo_other),
    )
    self_qkv_other = swap(self_qkv)
    triples = exchange(triple_heads(scalars, normed, self_qkv, self_qkv_other))
    triples = triples.reshape(owners, duos, rows, 3 * HD)
    self_attended = head_attention(
        scalars, triples, triples, swap(triples), False, group_rows
    )
    second_stream, mlp_normed = project(
        first_stream, self_attended, self_out, swap(self_out)
    )

    blocks = [mlp_normed]
    for distance in distances:
        blocks.append(across(mlp_normed, distance))
    kept, *given = mlp_shares(scalars, blocks, mlp_in, mlp_out, *fetched)
    result = second_stream + kept
    for share, distance in zip(given, distances):
        came = across(share, distance)
        result = result + came.astype(jnp.float32)
    return result.astype(jnp.bfloat16)[None]


def solution(mesh):
    placed = (
        P("ctx"),
        P(),
        P(),
        P("ctx", "lat"),
        P(None, "ctx", "lat"),
        P("lat", None),
        P(None, None, "lat"),
        P("lat", None),
        P(None, "ctx"),
        P("ctx", None),
    )

    def per_device(*arguments):
        owners, groups = lax.axis_size("ctx"), lax.axis_size("lat")
        local_heads = arguments[3].shape[1] // HD
        paired = groups == 4 and owners == 2 * local_heads and owners & (owners - 1) == 0
        return (paired_device if paired else general_device)(*arguments)

    return jax.shard_map(
        per_device, mesh=mesh, in_specs=placed, out_specs=P("lat", "ctx", None), check_vma=False
    )
```

```python
import math

import jax
import jax.numpy as jnp
from jax import lax
from jax.experimental import pallas as pl
from jax.experimental.pallas import tpu as pltpu
from jax.sharding import PartitionSpec as P

HD = 128
LATENTS = 1024


EPSILON = 1e-06
MASKED = -1e30


def rms_normalize(values):
    return values * lax.rsqrt(jnp.mean(values * values, axis=-1, keepdims=True) + EPSILON)


def sinusoid(places, width):
    index = jnp.arange(width // 2).astype(jnp.float32)
    rates = jnp.exp(index * (-2.0 * math.log(10000.0) / width))
    angles = places.astype(jnp.float32)[:, None] * rates[None, :]
    return jnp.stack([jnp.sin(angles), jnp.cos(angles)], axis=-1).reshape(places.shape[0], width)


def embed_rows(token_rows, table, places):
    vocab_range = jnp.arange(table.shape[0], dtype=jnp.int32)
    one_hot = (token_rows[:, None] == vocab_range[None, :]).astype(jnp.bfloat16)
    looked = jnp.dot(one_hot, table, preferred_element_type=jnp.float32)
    return rms_normalize(looked + sinusoid(places, table.shape[1])).astype(jnp.bfloat16)


def block_attention(queries, keys, values, blocked, head_size):
    scale = 1.0 / math.sqrt(head_size)
    head_count = queries.shape[1] // head_size
    query_rows = queries.shape[0]
    key_rows = keys.shape[0]
    query_heads = jnp.transpose(queries.reshape(query_rows, head_count, head_size), (1, 0, 2))
    key_heads = jnp.transpose(keys.reshape(key_rows, head_count, head_size), (1, 0, 2))
    value_heads = jnp.transpose(values.reshape(key_rows, head_count, head_size), (1, 0, 2))

    def one_head(operands):
        query, key, value = operands
        scores = (
            lax.dot_general(
                query, key, (((1,), (1,)), ((), ())), preferred_element_type=jnp.float32
            )
            * scale
        )
        scores = jnp.where(blocked, MASKED, scores)
        peak = jnp.max(scores, axis=1)
        weights = jnp.exp(scores - peak[:, None]).astype(jnp.bfloat16)
        total = jnp.sum(weights.astype(jnp.float32), axis=1)
        output = jnp.dot(weights, value, preferred_element_type=jnp.float32)
        return (peak, total, output)

    maxima, totals, outputs = lax.map(one_head, (query_heads, key_heads, value_heads))
    merged = jnp.transpose(outputs, (1, 0, 2)).reshape(query_rows, head_count * head_size)
    return (jnp.transpose(maxima), jnp.transpose(totals), merged)


def general_device(
    token_ids,
    latent_offset,
    embed_table,
    cross_q,
    cross_kv,
    cross_out,
    self_qkv,
    self_out,
    mlp_in,
    mlp_out,
):
    context_count = lax.axis_size("ctx")
    group_count = lax.axis_size("lat")
    context_index = lax.axis_index("ctx")
    group_index = lax.axis_index("lat")
    block_length = token_ids.shape[0]
    head_size = HD
    local_width = cross_q.shape[1]
    local_heads = local_width // head_size
    width = embed_table.shape[1]
    offset = latent_offset[0]
    latent_count = LATENTS
    row_count = latent_count // context_count
    group_rows = latent_count // group_count
    places = context_index * block_length + jnp.arange(block_length, dtype=jnp.int32)
    context = embed_rows(token_ids, embed_table, places)
    piece = lax.all_gather(cross_kv, "ctx", axis=1, tiled=True)
    columns = context
    key_sum = jnp.dot(columns, piece[0], preferred_element_type=jnp.float32)
    value_sum = jnp.dot(columns, piece[1], preferred_element_type=jnp.float32)
    keys = key_sum.astype(jnp.bfloat16)
    values = value_sum.astype(jnp.bfloat16)
    every_token = lax.all_gather(token_ids, "ctx", axis=0, tiled=True)
    latent_tokens = lax.dynamic_slice_in_dim(every_token, offset, latent_count, 0)
    latent_places = offset + jnp.arange(latent_count, dtype=jnp.int32)
    latent = embed_rows(latent_tokens, embed_table, latent_places)
    columns = latent
    query_sum = jnp.dot(
        columns,
        lax.all_gather(cross_q, "ctx", axis=0, tiled=True),
        preferred_element_type=jnp.float32,
    )
    queries = query_sum.astype(jnp.bfloat16)
    blocked = places[None, :] > latent_places[:, None]
    maxima, totals, outputs = block_attention(queries, keys, values, blocked, head_size)
    row_start = context_index * row_count
    came_max, came_total, came_out = (
        lax.all_to_all(maxima[:, None, :], "ctx", split_axis=0, concat_axis=1, tiled=True),
        lax.all_to_all(totals[:, None, :], "ctx", split_axis=0, concat_axis=1, tiled=True),
        lax.all_to_all(outputs[:, None, :], "ctx", split_axis=0, concat_axis=1, tiled=True),
    )
    peak = jnp.max(came_max, axis=1, keepdims=True)
    factor = jnp.exp(came_max - peak)
    own_totals = jnp.sum(came_total * factor, axis=1)
    spread = (
        came_out.reshape(row_count, context_count, local_heads, head_size) * factor[:, :, :, None]
    )
    own_outputs = jnp.sum(spread, axis=1).reshape(row_count, local_width)
    attended = (own_outputs / jnp.repeat(own_totals, head_size, axis=1)).astype(jnp.bfloat16)
    own_latent = lax.dynamic_slice_in_dim(latent, row_start, row_count, 0).astype(jnp.float32)
    first_stream = own_latent + lax.psum(
        jnp.dot(attended, cross_out, preferred_element_type=jnp.float32), "lat"
    )
    self_normed = rms_normalize(first_stream).astype(jnp.bfloat16)
    self_queries = jnp.dot(self_normed, self_qkv[0], preferred_element_type=jnp.float32).astype(
        jnp.bfloat16
    )
    self_keys = jnp.dot(self_normed, self_qkv[1], preferred_element_type=jnp.float32).astype(
        jnp.bfloat16
    )
    self_values = jnp.dot(self_normed, self_qkv[2], preferred_element_type=jnp.float32).astype(
        jnp.bfloat16
    )
    all_keys, all_values = (
        lax.all_gather(self_keys, "ctx", axis=0, tiled=True),
        lax.all_gather(self_values, "ctx", axis=0, tiled=True),
    )
    own_places = row_start + jnp.arange(row_count, dtype=jnp.int32)
    later = jnp.arange(latent_count, dtype=jnp.int32)[None, :] > own_places[:, None]
    _, self_totals, self_outputs = block_attention(
        self_queries, all_keys, all_values, later, head_size
    )
    self_attended = (self_outputs / jnp.repeat(self_totals, head_size, axis=1)).astype(jnp.bfloat16)
    second_stream = first_stream + lax.psum(
        jnp.dot(self_attended, self_out, preferred_element_type=jnp.float32).astype(jnp.bfloat16),
        "lat",
    ).astype(jnp.float32)
    mlp_normed = rms_normalize(second_stream).astype(jnp.bfloat16)
    gathered = lax.all_gather(mlp_normed, "ctx", axis=0, tiled=True)
    group_input = lax.dynamic_slice_in_dim(gathered, group_index * group_rows, group_rows, 0)
    pre_hidden = jnp.dot(group_input, mlp_in, preferred_element_type=jnp.float32)
    hidden = jax.nn.gelu(pre_hidden, approximate=True).astype(jnp.bfloat16)
    place = context_index * row_count - group_index * group_rows
    inside = jnp.logical_and(place >= 0, place < group_rows)
    residual = jnp.zeros((group_rows, width), jnp.float32)
    residual = lax.dynamic_update_slice_in_dim(
        residual, second_stream, jnp.clip(place, 0, group_rows - row_count), 0
    )
    residual = jnp.where(inside, residual, 0.0)
    result = lax.psum_scatter(
        jnp.dot(hidden, mlp_out, preferred_element_type=jnp.float32) + residual,
        "ctx",
        scatter_dimension=0,
        tiled=True,
    )
    return result.astype(jnp.bfloat16)[None]


FINE = 16
MIB = 1 << 20


def rate_row(width):
    index = (jnp.arange(width, dtype=jnp.int32) // 2).astype(jnp.float32)
    return jnp.exp(index * (-2.0 * math.log(10000.0) / width))


def context_kernel(
    halves, first, ids_ref, sine_ref, cosine_ref, high_cos_ref, high_sin_ref, low_cos_ref,
    low_sin_ref, table_ref, out_ref, cos_ref, sin_ref,
):
    tile = pl.program_id(0)

    @pl.when(tile == 0)
    def _():
        low_cos, low_sin = low_cos_ref[...], low_sin_ref[...]
        for step in range(FINE):
            high_cos, high_sin = high_cos_ref[step : step + 1], high_sin_ref[step : step + 1]
            rows = pl.ds(step * FINE, FINE)
            cos_ref[rows, :] = high_cos * low_cos - high_sin * low_sin
            sin_ref[rows, :] = high_sin * low_cos + high_cos * low_sin

    vocab, width = table_ref.shape
    rows = out_ref.shape[0]
    one_hot = (
        lax.broadcasted_iota(jnp.int32, (vocab, rows), 0) == ids_ref[0]
    ).astype(jnp.float32).astype(jnp.bfloat16)
    looked = lax.dot_general(
        one_hot, table_ref[...], (((0,), (0,)), ((), ())), preferred_element_type=jnp.float32
    )
    start = pl.ds(first + tile, 1)
    total = looked + sine_ref[start, :] * cos_ref[...] + cosine_ref[start, :] * sin_ref[...]
    power = jnp.mean(total * total, axis=1, keepdims=True)
    normed = (total * lax.rsqrt(power + EPSILON)).astype(jnp.bfloat16)
    part = width // (2 * halves)
    for half in range(2):
        for owner in range(halves):
            source = (owner * 2 + half) * part
            target = (half * halves + owner) * part
            out_ref[:, target : target + part] = normed[:, source : source + part]


def sinusoid_tables(starts, width):
    rates = rate_row(width)
    odd = (jnp.arange(width, dtype=jnp.int32) % 2)[None, :] == 1
    places = jnp.pad(starts, (0, -starts.shape[0] % FINE)).astype(jnp.float32)
    angles = places[:, None] * rates[None, :]
    sines, cosines = jnp.sin(angles), jnp.cos(angles)
    steps = jnp.arange(FINE, dtype=jnp.float32)
    high = (steps * FINE)[:, None] * rates[None, :]
    low = steps[:, None] * rates[None, :]
    return (
        jnp.where(odd, cosines, sines),
        jnp.where(odd, -sines, cosines),
        jnp.cos(high),
        jnp.sin(high),
        jnp.cos(low),
        jnp.sin(low),
    )


def context_rows(ids, first, tables, table, owners):
    count, rows = ids.shape[0], FINE * FINE
    width = table.shape[1]
    return pl.pallas_call(
        lambda *refs: context_kernel(owners, first, *refs),
        grid=(count,),
        in_specs=[pl.BlockSpec((1, 1, rows), lambda i: (i, 0, 0))]
        + [pl.BlockSpec(array.shape, lambda i: (0, 0)) for array in (*tables, table)],
        out_specs=pl.BlockSpec((rows, width), lambda i: (i, 0)),
        out_shape=jax.ShapeDtypeStruct((count * rows, width), jnp.bfloat16),
        scratch_shapes=[pltpu.VMEM((rows, width), jnp.float32)] * 2,
        cost_estimate=pl.CostEstimate(
            flops=count * rows * width * table.shape[0] * 2,
            bytes_accessed=count * rows * width * 2,
            transcendentals=0,
        ),
        compiler_params=pltpu.CompilerParams(vmem_limit_bytes=12 * MIB),
        name="context_rows",
    )(ids[:, None, :], *tables, table)


def attention_kernel(key_tile, shifted, scalars_ref, query_ref, own_ref, other_ref, out_ref):
    tile, core = pl.program_id(0), scalars_ref[0]
    offset = scalars_ref[4] if shifted else 0
    parts, rows, size = query_ref.shape
    query = query_ref[...].reshape(parts * rows, size)
    rows = parts * rows
    query_place = (
        offset + (2 * tile + core) * rows + lax.broadcasted_iota(jnp.int32, (rows, 1), 0)
    )
    peak = jnp.full((rows, 1), MASKED, jnp.float32)
    output = jnp.zeros((rows, 2 * size), jnp.float32)
    outer, blocks, inner, columns = own_ref.shape
    keys = outer * inner
    for side, ref in enumerate((own_ref, other_ref)):
        for block in range(blocks):
            pair = ref[:, block, :, columns - 2 * size :].reshape(keys, 2 * size)
            for part in range(keys // key_tile):
                span = slice(part * key_tile, (part + 1) * key_tile)
                key, value = pair[span, :size], pair[span, size:]
                scores = lax.dot_general(
                    query, key, (((1,), (1,)), ((), ())), preferred_element_type=jnp.float32
                )
                key_place = (
                    (2 * block + (1 - core if side else core)) * keys
                    + part * key_tile
                    + lax.broadcasted_iota(jnp.int32, (1, key_tile), 1)
                )
                scores = jnp.where(key_place > query_place, MASKED, scores)
                new_peak = jnp.maximum(peak, jnp.max(scores, axis=1, keepdims=True))
                weights = jnp.exp(scores - new_peak).astype(jnp.bfloat16)
                output = output * jnp.exp(peak - new_peak) + jnp.dot(
                    weights,
                    jnp.concatenate([value, jnp.ones_like(value)], axis=1),
                    preferred_element_type=jnp.float32,
                )
                peak = new_peak
    final = (output[:, :size] / output[:, size:]).astype(jnp.bfloat16)
    out_ref[...] = final.reshape(out_ref.shape)


def head_attention(scalars, triples, own, other, shifted, key_tile):
    owners, tiles, rows = triples.shape[:3]
    keys = 2 * own.shape[0] * own.shape[1] * own.shape[2]
    return pl.pallas_call(
        lambda *refs: attention_kernel(key_tile, shifted, *refs),
        grid_spec=pltpu.PrefetchScalarGridSpec(
            num_scalar_prefetch=1,
            grid=(tiles,),
            in_specs=[
                pl.BlockSpec((owners, None, rows, HD), lambda i, s: (0, i, 0, 0)),
                pl.BlockSpec(own.shape, lambda i, s: (0, 0, 0, 0)),
                pl.BlockSpec(other.shape, lambda i, s: (0, 0, 0, 0)),
            ],
            out_specs=pl.BlockSpec((owners, None, rows, HD), lambda i, s: (0, i, 0, 0)),
        ),
        out_shape=jax.ShapeDtypeStruct((owners, tiles, rows, HD), jnp.bfloat16),
        cost_estimate=pl.CostEstimate(
            flops=8 * owners * tiles * rows * keys * HD,
            bytes_accessed=keys * HD * 4,
            transcendentals=owners * tiles * rows * keys,
        ),
        compiler_params=pltpu.CompilerParams(vmem_limit_bytes=14 * MIB),
        name="head_attention",
    )(scalars, triples, own, other)


def stream_kernel(
    scalars_ref, heads_ref, came_ref, base_ref, *refs,
):
    *matrix_refs, stream_ref, normed_ref, matrices, loaded = refs
    core, duo = scalars_ref[0], scalars_ref[1]
    half = heads_ref.shape[0] // 2
    loads = [
        pltpu.make_async_copy(source, matrices.at[index], loaded.at[index])
        for index, source in enumerate(matrix_refs)
    ]
    for load in loads:
        load.start()
    total = base_ref[...].astype(jnp.float32)
    sides = [(heads_ref, core), (heads_ref, 1 - core), (came_ref, core), (came_ref, 1 - core)]
    for index, (ref, side) in enumerate(sides):
        left = jnp.concatenate([ref[side * half + head] for head in range(half)], axis=1)
        loads[index].wait()
        total += jnp.dot(left, matrices[index], preferred_element_type=jnp.float32)
    rows = stream_ref.shape[0]
    stream_ref[...] = jnp.where(duo == 0, total[:rows], total[rows:])
    normed_ref[...] = rms_normalize(total).astype(jnp.bfloat16)


def stream_rows(scalars, heads, came, base, matrices):
    rows, width = base.shape
    inner = matrices[0].shape[0]
    return pl.pallas_call(
        stream_kernel,
        in_specs=[IN_SMEM] + [IN_VMEM] * 3 + [ANYWHERE] * len(matrices),
        out_specs=[IN_VMEM] * 2,
        out_shape=[
            jax.ShapeDtypeStruct((rows // 2, width), jnp.float32),
            jax.ShapeDtypeStruct((rows, width), jnp.bfloat16),
        ],
        scratch_shapes=[
            pltpu.VMEM((len(matrices), inner, width), jnp.bfloat16),
            pltpu.SemaphoreType.DMA((len(matrices),)),
        ],
        cost_estimate=pl.CostEstimate(
            flops=8 * rows * inner * width, bytes_accessed=8 * inner * width, transcendentals=0
        ),
        compiler_params=pltpu.CompilerParams(vmem_limit_bytes=20 * MIB),
        name="stream_rows",
    )(scalars, heads, came, base, *[in_hbm(matrix) for matrix in matrices])


def in_hbm(array):
    return pltpu.with_memory_space_constraint(array, pltpu.HBM)


def prepare_kernel(
    scalars_ref, query_hbm, pair_hbm, matrix_hbm, mine_ref, theirs_ref, part_ref, query_ref,
    pair_ref, loaded,
):
    core, group = scalars_ref[0], scalars_ref[3]
    heads, half, columns = mine_ref.shape
    size = columns // 3
    depth = part_ref.shape[0]
    quarter = matrix_hbm.at[pl.ds(pl.multiple_of(group * depth, depth), depth), :]
    loads = [
        pltpu.make_async_copy(query_hbm, query_ref, loaded.at[0]),
        pltpu.make_async_copy(pair_hbm, pair_ref, loaded.at[1]),
        pltpu.make_async_copy(quarter, part_ref, loaded.at[2]),
    ]
    for load in loads:
        load.start()
    loads[0].wait()
    loads[1].wait()
    for target, side in ((theirs_ref, 1 - core), (mine_ref, core)):
        rows = pl.ds(pl.multiple_of(side * half, half), half)
        for head in range(heads):
            span = slice(head * size, (head + 1) * size)
            target[head, :, 0:size] = query_ref[rows, span]
            target[head, :, size : 2 * size] = pair_ref[0, rows, span]
            target[head, :, 2 * size :] = pair_ref[1, rows, span]
    loads[2].wait()


def prepare_weights(scalars, cross_q, cross_kv, matrix, groups):
    share, columns = cross_q.shape
    shape = jax.ShapeDtypeStruct((columns // HD, share // 2, 3 * HD), jnp.bfloat16)
    part = jax.ShapeDtypeStruct((matrix.shape[0] // groups, matrix.shape[1]), jnp.bfloat16)
    return pl.pallas_call(
        prepare_kernel,
        in_specs=[IN_SMEM] + [ANYWHERE] * 3,
        out_specs=[IN_VMEM] * 3,
        out_shape=[shape, shape, part],
        scratch_shapes=[
            pltpu.VMEM(cross_q.shape, jnp.bfloat16),
            pltpu.VMEM(cross_kv.shape, jnp.bfloat16),
            pltpu.SemaphoreType.DMA((3,)),
        ],
        compiler_params=pltpu.CompilerParams(vmem_limit_bytes=8 * MIB),
        name="prepare_weights",
    )(scalars, in_hbm(cross_q), in_hbm(cross_kv), in_hbm(matrix))


def project_kernel(scalars_ref, heads_ref, mine_ref, theirs_ref, kept_ref, given_ref):
    core, duo = scalars_ref[0], scalars_ref[1]
    half = heads_ref.shape[0] // 2
    product = 0.0
    for side, matrix in ((core, mine_ref), (1 - core, theirs_ref)):
        left = jnp.concatenate([heads_ref[side * half + head] for head in range(half)], axis=1)
        product += jnp.dot(left, matrix[...], preferred_element_type=jnp.float32)
    kept_rows = kept_ref.shape[0]
    low, high = product[:kept_rows], product[kept_rows:]
    kept_ref[...] = jnp.where(duo == 0, low, high)
    given_ref[...] = jnp.where(duo == 0, high, low).astype(jnp.bfloat16)


IN_VMEM = pl.BlockSpec(memory_space=pltpu.VMEM)
IN_SMEM = pl.BlockSpec(memory_space=pltpu.SMEM)
ANYWHERE = pl.BlockSpec(memory_space=pl.ANY)


def project_rows(scalars, heads, mine, theirs):
    _, rows, _ = heads.shape
    inner, width = mine.shape
    return pl.pallas_call(
        project_kernel,
        in_specs=[IN_SMEM, IN_VMEM, IN_VMEM, IN_VMEM],
        out_specs=[IN_VMEM, IN_VMEM],
        out_shape=[
            jax.ShapeDtypeStruct((rows // 2, width), jnp.float32),
            jax.ShapeDtypeStruct((rows // 2, width), jnp.bfloat16),
        ],
        cost_estimate=pl.CostEstimate(
            flops=4 * rows * inner * width, bytes_accessed=4 * inner * width, transcendentals=0
        ),
        compiler_params=pltpu.CompilerParams(vmem_limit_bytes=8 * MIB),
        name="project_rows",
    )(scalars, heads, mine, theirs)


def triple_kernel(scale, scalars_ref, rows_ref, mine_hbm, theirs_hbm, out_ref, matrices, loaded):
    core = scalars_ref[0]
    heads = out_ref.shape[0] // 2
    kinds = mine_hbm.shape[0]
    loads = [
        pltpu.make_async_copy(source.at[kind], matrices.at[base + kind], loaded.at[base + kind])
        for base, source in ((0, mine_hbm), (kinds, theirs_hbm))
        for kind in range(kinds)
    ]
    ahead = 3
    for load in loads[:ahead]:
        load.start()
    rows = rows_ref[...]
    for index, load in enumerate(loads):
        load.wait()
        for later in loads[index + ahead : index + ahead + 1]:
            later.start()
        kind = index % kinds
        side = core if index < kinds else 1 - core
        product = jnp.dot(rows, matrices[index], preferred_element_type=jnp.float32)
        product = (product * (scale if kind == 0 else 1.0)).astype(jnp.bfloat16)
        for head in range(heads):
            out_ref[side * heads + head, :, kind * HD : (kind + 1) * HD] = product[
                :, head * HD : (head + 1) * HD
            ]


def triple_heads(scalars, rows, mine, theirs):
    count = rows.shape[0]
    kinds, inner, columns = mine.shape
    heads = columns // HD
    return pl.pallas_call(
        lambda *refs: triple_kernel(HD**-0.5, *refs),
        in_specs=[IN_SMEM, IN_VMEM, ANYWHERE, ANYWHERE],
        out_specs=IN_VMEM,
        out_shape=jax.ShapeDtypeStruct((2 * heads, count, kinds * HD), jnp.bfloat16),
        scratch_shapes=[
            pltpu.VMEM((2 * kinds, inner, columns), jnp.bfloat16),
            pltpu.SemaphoreType.DMA((2 * kinds,)),
        ],
        cost_estimate=pl.CostEstimate(
            flops=4 * kinds * count * inner * columns,
            bytes_accessed=4 * kinds * inner * columns,
            transcendentals=0,
        ),
        compiler_params=pltpu.CompilerParams(vmem_limit_bytes=20 * MIB),
        name="triple_heads",
    )(scalars, rows, in_hbm(mine), in_hbm(theirs))


def add_norm_kernel(base_ref, kept_ref, came_ref, stream_ref, normed_ref):
    total = base_ref[...].astype(jnp.float32) + (
        kept_ref[...] + came_ref[...].astype(jnp.float32)
    )
    stream_ref[...] = total
    normed_ref[...] = rms_normalize(total).astype(jnp.bfloat16)


def add_norm(base, kept, came):
    return pl.pallas_call(
        add_norm_kernel,
        in_specs=[IN_VMEM] * 3,
        out_specs=[IN_VMEM] * 2,
        out_shape=[
            jax.ShapeDtypeStruct(kept.shape, jnp.float32),
            jax.ShapeDtypeStruct(kept.shape, jnp.bfloat16),
        ],
        compiler_params=pltpu.CompilerParams(vmem_limit_bytes=4 * MIB),
        name="add_norm",
    )(base, kept, came)


def context_heads_kernel(
    scale, scalars_ref, context_ref, rows_ref, mine_ref, theirs_ref, pair_ref, query_ref,
    latent_ref, weights_ref,
):
    core, place = scalars_ref[0], scalars_ref[2]
    _, part, columns = mine_ref.shape
    owners, tiles, rows, size = query_ref.shape
    inner = owners * part
    keys = pair_ref.shape[0]
    tile = owners * rows
    for side, ref in ((core, mine_ref), (1 - core, theirs_ref)):
        span = pl.ds(pl.multiple_of(side * inner, inner), inner)
        weights_ref[span, :] = ref[...].reshape(inner, columns)

    def product(left, columns):
        return jnp.dot(left, weights_ref[:, columns], preferred_element_type=jnp.float32)

    for start in range(0, keys, tile):
        span = slice(start, start + tile)
        pair_ref[span, :] = product(context_ref[span, :], slice(size, 3 * size)).astype(
            jnp.bfloat16
        )
    for index in range(tiles):
        left = rows_ref[index * tile : (index + 1) * tile, :]
        query = (product(left, slice(0, size)) * scale).astype(jnp.bfloat16)
        query_ref[:, index] = query.reshape(owners, rows, size)
    for index in range(tiles):
        start = pl.multiple_of(index * tile + place * rows, rows)
        latent = rows_ref[pl.ds(start, rows), :]
        for half in range(2):
            for owner in range(owners):
                source = half * inner + owner * part
                target = (owner * 2 + half) * part
                latent_ref[index * rows : (index + 1) * rows, target : target + part] = latent[
                    :, source : source + part
                ]


def context_heads(scalars, context, latent, mine, theirs, shape):
    owners, tiles, rows = shape
    keys, width = context.shape
    size = mine.shape[2] // 3
    return pl.pallas_call(
        lambda *refs: context_heads_kernel(size**-0.5, *refs),
        in_specs=[IN_SMEM] + [IN_VMEM] * 4,
        out_specs=[IN_VMEM] * 3,
        out_shape=[
            jax.ShapeDtypeStruct((keys, 2 * size), jnp.bfloat16),
            jax.ShapeDtypeStruct((owners, tiles, rows, size), jnp.bfloat16),
            jax.ShapeDtypeStruct((tiles * rows, width), jnp.bfloat16),
        ],
        scratch_shapes=[pltpu.VMEM((width, 3 * size), jnp.bfloat16)],
        cost_estimate=pl.CostEstimate(
            flops=4 * (keys + owners * tiles * rows) * width * size,
            bytes_accessed=keys * width * 2,
            transcendentals=0,
        ),
        compiler_params=pltpu.CompilerParams(vmem_limit_bytes=12 * MIB),
        name="context_heads",
    )(scalars, context, latent, mine, theirs)


def order_kernel(scalars_ref, mine_ref, theirs_ref, *block_refs):
    core, place = scalars_ref[0], scalars_ref[2]
    heads = mine_ref.shape[0]
    for distance, block_ref in enumerate(block_refs):
        head = place ^ distance
        local = lax.rem(head, heads)
        own = lax.div(head, heads) == core

        @pl.when(own)
        def _():
            block_ref[...] = mine_ref[local]

        @pl.when(jnp.logical_not(own))
        def _():
            block_ref[...] = theirs_ref[local]


def order_blocks(scalars, mine, theirs):
    heads, rows, columns = mine.shape
    return pl.pallas_call(
        order_kernel,
        in_specs=[IN_SMEM, IN_VMEM, IN_VMEM],
        out_specs=[IN_VMEM] * (2 * heads),
        out_shape=[jax.ShapeDtypeStruct((rows, columns), jnp.bfloat16)] * (2 * heads),
        compiler_params=pltpu.CompilerParams(vmem_limit_bytes=4 * MIB),
        name="order_blocks",
    )(scalars, mine, theirs)


def gather_kernel(step, scalars_ref, *refs):
    *block_refs, out_ref, loaded = refs
    loads = [
        pltpu.make_async_copy(
            block_ref, out_ref.at[lax.div(scalars_ref[2], step) ^ distance], loaded.at[distance]
        )
        for distance, block_ref in enumerate(block_refs)
    ]
    for load in loads:
        load.start()
    for load in loads:
        load.wait()


def gather_blocks(scalars, blocks, step):
    return pl.pallas_call(
        lambda *refs: gather_kernel(step, *refs),
        in_specs=[IN_SMEM] + [ANYWHERE] * len(blocks),
        out_specs=IN_VMEM,
        out_shape=jax.ShapeDtypeStruct((len(blocks), *blocks[0].shape), blocks[0].dtype),
        scratch_shapes=[pltpu.SemaphoreType.DMA((len(blocks),))],
        compiler_params=pltpu.CompilerParams(vmem_limit_bytes=4 * MIB),
        name="gather_blocks",
    )(scalars, *blocks)


def mlp_kernel(scalars_ref, *refs):
    group = scalars_ref[3]
    *refs, hidden_ref, out_ref, loaded = refs
    count = (len(refs) - 10) // 2
    blocks, (in_ref, out_hbm), rest = refs[:count], refs[count : count + 2], refs[count + 2 :]
    load = pltpu.make_async_copy(out_hbm, out_ref, loaded)
    load.start()
    in_parts, out_parts, shares = rest[:4], rest[4:8], rest[8:]
    rows = jnp.concatenate([block[...] for block in blocks])
    depth, units = in_parts[0].shape[0], out_parts[0].shape[0]

    def hidden_of(total):
        return jax.nn.gelu(total, approximate=True).astype(jnp.bfloat16)

    hidden = hidden_of(jnp.dot(rows, in_ref[...], preferred_element_type=jnp.float32))
    quarters = [group, group ^ 2, group ^ 1, group ^ 3]
    total = 0.0
    for quarter, part in zip(quarters, in_parts):
        span = pl.ds(pl.multiple_of(quarter * depth, depth), depth)
        piece = jnp.concatenate([block[:, span] for block in blocks])
        total += jnp.dot(piece, part[...], preferred_element_type=jnp.float32)
    hidden_ref[...] = hidden_of(total)
    load.wait()
    share = jnp.dot(hidden, out_ref[...], preferred_element_type=jnp.float32)
    for quarter, part in zip(quarters, out_parts):
        span = pl.ds(pl.multiple_of(quarter * units, units), units)
        share += jnp.dot(hidden_ref[:, span], part[...], preferred_element_type=jnp.float32)
    each = blocks[0].shape[0]
    for index, target in enumerate(shares):
        target[...] = share[index * each : (index + 1) * each].astype(target.dtype)


def mlp_shares(scalars, blocks, mlp_in, mlp_out, in_parts, out_parts):
    first = jax.ShapeDtypeStruct(blocks[0].shape, jnp.float32)
    other = jax.ShapeDtypeStruct(blocks[0].shape, jnp.bfloat16)
    operands = [*blocks, mlp_in, in_hbm(mlp_out), *in_parts, *out_parts]
    return pl.pallas_call(
        mlp_kernel,
        in_specs=[IN_SMEM]
        + [IN_VMEM] * (len(blocks) + 1)
        + [ANYWHERE]
        + [IN_VMEM] * (len(operands) - len(blocks) - 2),
        out_specs=[IN_VMEM] * len(blocks),
        out_shape=[first] + [other] * (len(blocks) - 1),
        scratch_shapes=[
            pltpu.VMEM((len(blocks) * blocks[0].shape[0], mlp_in.shape[1]), jnp.bfloat16),
            pltpu.VMEM(mlp_out.shape, jnp.bfloat16),
            pltpu.SemaphoreType.DMA(()),
        ],
        cost_estimate=pl.CostEstimate(
            flops=8 * len(blocks) * blocks[0].size * mlp_in.shape[1],
            bytes_accessed=8 * mlp_in.size,
            transcendentals=0,
        ),
        compiler_params=pltpu.CompilerParams(vmem_limit_bytes=16 * MIB),
        name="mlp_shares",
    )(scalars, *operands)


def paired_device(
    token_ids,
    latent_offset,
    embed_table,
    cross_q,
    cross_kv,
    cross_out,
    self_qkv,
    self_out,
    mlp_in,
    mlp_out,
):
    owners = lax.axis_size("ctx")
    groups = lax.axis_size("lat")
    place = lax.axis_index("ctx")
    group = lax.axis_index("lat")
    core = group % 2
    duo = group // 2
    duos = groups // 2
    offset = latent_offset[0]
    block = token_ids.shape[0]
    width = embed_table.shape[1]
    share = cross_q.shape[0]
    group_rows = LATENTS // groups
    rows = group_rows // owners
    duo_rows = duos * rows
    scalars = jnp.stack([core, duo, place, group, offset]).astype(jnp.int32)

    def swap(value):
        return lax.ppermute(value, "lat", [(i, i ^ 1) for i in range(groups)])

    def cross(value):
        return lax.ppermute(value, "lat", [(i, i ^ 2) for i in range(groups)])

    def exchange(value):
        return lax.all_to_all(value, "ctx", 0, 0, tiled=True)

    distances = [2 * i for i in range(1, owners // 2)]

    def across(value, distance):
        return lax.ppermute(value, "ctx", [(i, i ^ distance) for i in range(owners)])

    def quarter(matrix):
        size = matrix.shape[0] // groups
        return lax.dynamic_slice_in_dim(matrix, group * size, size, 0)

    mine, theirs, in_part = prepare_weights(scalars, cross_q, cross_kv, mlp_in, groups)
    blocks = order_blocks(scalars, mine, swap(theirs))

    lanes = token_ids.reshape(1, block // HD, HD)
    lanes_other = across(lanes, 1)
    even = place % 2 == 0
    lanes = jnp.concatenate(
        [jnp.where(even, lanes, lanes_other), jnp.where(even, lanes_other, lanes)]
    )
    pair_lanes = [lanes]
    for distance in distances:
        pair_lanes.append(across(lanes, distance))
    every_token = gather_blocks(scalars, pair_lanes, 2).reshape(owners, block)
    arrived = [blocks[0]]
    for distance in range(1, owners):
        arrived.append(across(blocks[distance], distance))

    step = FINE * FINE
    latent_starts = (2 * jnp.arange(duos, dtype=jnp.int32) + core) * group_rows
    pieces = block // step
    half_blocks = owners // 2
    token_blocks = every_token.reshape(half_blocks, 2, block)
    own_ids = lax.dynamic_index_in_dim(token_blocks, core, 1, keepdims=False)
    flat_tokens = every_token.reshape(owners * block)
    latent_ids = jnp.stack(
        [
            lax.dynamic_slice_in_dim(
                flat_tokens, offset + (2 * i + core) * group_rows, group_rows, 0
            )
            for i in range(duos)
        ]
    )
    fetched = []
    for part in (in_part, None):
        one = across(quarter(mlp_out) if part is None else part, 1)
        two = cross(one)
        three = swap(one)
        four = swap(two)
        fetched.append((one, two, three, four))

    block_starts = (2 * jnp.arange(half_blocks, dtype=jnp.int32) + core) * block
    inner = jnp.arange(pieces, dtype=jnp.int32) * step
    latent_inner = jnp.arange(group_rows // step, dtype=jnp.int32) * step
    starts = jnp.concatenate(
        [
            (block_starts[:, None] + inner[None, :]).reshape(-1),
            (offset + latent_starts[:, None] + latent_inner[None, :]).reshape(-1),
        ]
    )
    tables = sinusoid_tables(starts, width)
    tiles = half_blocks * pieces
    context = context_rows(own_ids.reshape(-1, step), 0, tables, embed_table, owners)
    latent = context_rows(latent_ids.reshape(-1, step), tiles, tables, embed_table, owners)
    arrived = [arrived[0], *map(in_hbm, arrived[1:])]
    arrived = gather_blocks(scalars, arrived, 1)
    arrived_other = swap(arrived)
    pairs, queries, kept_latent = context_heads(
        scalars, context, latent, arrived, arrived_other, (owners, duos, rows)
    )
    other_pairs = swap(pairs)
    by_block = (1, half_blocks, block, 2 * HD)
    attended = head_attention(
        scalars, queries, pairs.reshape(by_block), other_pairs.reshape(by_block), True, block
    )

    def project(base, attended, mine, theirs):
        heads = exchange(attended.reshape(owners, duo_rows, HD))
        kept, given = project_rows(scalars, heads, mine, theirs)
        came = cross(given)
        return add_norm(base, kept, came)

    cross_out_duo = cross(cross_out)
    cross_out_other = swap(cross_out)
    cross_out_duo_other = swap(cross_out_duo)
    cross_heads = exchange(attended.reshape(owners, duo_rows, HD))
    cross_heads_duo = cross(cross_heads)
    first_stream, normed = stream_rows(
        scalars,
        cross_heads,
        cross_heads_duo,
        kept_latent,
        (cross_out, cross_out_other, cross_out_duo, cross_out_duo_other),
    )
    self_qkv_other = swap(self_qkv)
    triples = exchange(triple_heads(scalars, normed, self_qkv, self_qkv_other))
    triples = triples.reshape(owners, duos, rows, 3 * HD)
    self_attended = head_attention(
        scalars, triples, triples, swap(triples), False, group_rows
    )
    second_stream, mlp_normed = project(
        first_stream, self_attended, self_out, swap(self_out)
    )

    blocks = [mlp_normed]
    for distance in distances:
        blocks.append(across(mlp_normed, distance))
    kept, *given = mlp_shares(scalars, blocks, mlp_in, mlp_out, *fetched)
    result = second_stream + kept
    for share, distance in zip(given, distances):
        came = across(share, distance)
        result = result + came.astype(jnp.float32)
    return result.astype(jnp.bfloat16)[None]


def solution(mesh):
    placed = (
        P("ctx"),
        P(),
        P(),
        P("ctx", "lat"),
        P(None, "ctx", "lat"),
        P("lat", None),
        P(None, None, "lat"),
        P("lat", None),
        P(None, "ctx"),
        P("ctx", None),
    )

    def per_device(*arguments):
        owners, groups = lax.axis_size("ctx"), lax.axis_size("lat")
        local_heads = arguments[3].shape[1] // HD
        paired = groups == 4 and owners == 2 * local_heads and owners & (owners - 1) == 0
        return (paired_device if paired else general_device)(*arguments)

    return jax.shard_map(
        per_device, mesh=mesh, in_specs=placed, out_specs=P("lat", "ctx", None), check_vma=False
    )
```
